256 devices in a mesh: gx: 16 (over x, z_hi), gy: 8 (over z_lo, y), gz: 2 (over core).
Axes of the slice: x: 4, y: 4, z: 8 (z_hi: 4, z_lo: 2; z = z_hi * 2 + z_lo), core: 2. Of those that a mesh axis runs over, the one named last changes fastest.
Arguments:
- state: float32 [5, 128, 128, 256], P(None, 'gx', 'gy', 'gz'), may hold values from -2 to 10, as said below
- adjoint: float32 [5, 128, 128, 256], P(None, 'gx', 'gy', 'gz'), may hold values from -6 to 6
- metric: float32 [9, 128, 128, 256], P(None, 'gx', 'gy', 'gz'), may hold values from -0.6 to 2.5, as said below
- jacobian: float32 [128, 128, 256], P('gx', 'gy', 'gz'), may hold values from 0.5 to 2
- boundary_kind_code: int32 [32, 32, 64], P('gx', 'gy', 'gz'), may hold values from 0 to 1
- orient: int32 [3, 32, 32, 64], P(None, 'gx', 'gy', 'gz'), may hold values from 0 to 1
Outputs:
- adjoint_residual: float32 [5, 128, 128, 256], P(None, 'gx', 'gy', 'gz')
The draws below stay inside these ranges and needn't reach their ends.
Inputs may be any that keep to these rules, and one draw needn't show every extreme that they name: `state`: conserved variables of a gas with positive density and positive pressure. `metric`: in each direction's vector, the component along that direction is positive. `boundary_kind_code`: 0 marks a wall, 1 a farfield; read only on faces of the domain's boundary. `orient`: 1 reverses the facing of the first tangential index across the element's upper face; ignored on the domain's upper boundary.
All inputs are finite; a program needn't handle non-finite values.
Results may differ from the reference program's by a relative error of at most 0.0003.
Values sent between devices are 32-bit elements; how exact they have to be, the bound alone decides.
A program may use at most 192 MiB of HBM per device.

```python
import math
import jax
import jax.numpy as jnp
import numpy as np
from jax import lax

VARS = 5
STREAM_ELEMENTS = 32
SPAN_ELEMENTS = 32
WALLNORMAL_COUNT = 64
NX = 128
NY = 128
NZ = 256


def draw_state(key, part):
    shape = (NX, NY, NZ)
    keys = jax.random.split(key, 3)
    density = jnp.exp(jax.random.uniform(keys[0], shape, jnp.float32, -0.69, 0.69))
    velocity = jnp.clip(0.25 * jax.random.normal(keys[1], (3,) + shape, jnp.float32), -0.6, 0.6)
    pressure = jnp.exp(jax.random.uniform(keys[2], shape, jnp.float32, -0.69, 0.69))
    momentum = density[None] * velocity
    energy = pressure / 0.4 + 0.5 * density * jnp.sum(velocity * velocity, axis=0)
    return jnp.concatenate([density[None], momentum, energy[None]], axis=0).astype(jnp.float32)


def draw_metric(key, part):
    shape = (9, NX, NY, NZ)
    keys = jax.random.split(key, 2)
    component = lax.broadcasted_iota(jnp.int32, (9, 1, 1, 1), 0)
    own = component % 4 == 0
    diagonal = jnp.exp(jax.random.uniform(keys[0], shape, jnp.float32, -0.69, 0.69))
    cross = jnp.clip(0.25 * jax.random.normal(keys[1], shape, jnp.float32), -0.6, 0.6)
    return jnp.where(own, diagonal, cross).astype(jnp.float32)


def place_ends(values, key, least, top_value):
    shape = values.shape
    index_at = [jax.random.randint(jax.random.fold_in(key, axis), (), 0, shape[axis]) for axis in range(len(shape))]
    values = values.at[tuple(index_at)].set(least)
    longest = shape.index(max(shape))
    index_at[longest] = (index_at[longest] + 1) % shape[longest]
    return values.at[tuple(index_at)].set(top_value)


def levels(stream_key, dims, cuts, smallest, high):
    gain = 1.0
    for axis_at, shards_of in cuts:
        heights = jax.random.uniform(jax.random.fold_in(jax.random.fold_in(stream_key, 6), axis_at), (shards_of,), jnp.float32, smallest / len(cuts), high / len(cuts))
        gain = gain * jnp.repeat(jnp.exp(heights), dims[axis_at] // shards_of).reshape((-1,) + (1,) * (len(dims) - 1 - axis_at))
    return gain


def centred(own_key, dims, deviation, limit, cuts=(), dtype=jnp.bfloat16):
    drawn = deviation * jax.random.normal(own_key, dims, jnp.float32)
    if cuts:
        drawn = drawn * levels(own_key, dims, cuts, -0.22, 0.18)
    return jnp.clip(drawn, -limit, limit).astype(dtype)


def setup_inputs(seed: int = 0) -> dict:
    splits = jax.random.split(jax.random.key(seed), 7)
    state = draw_state(jax.random.fold_in(splits[6], 71), 0)
    adjoint = centred(splits[1], (VARS, NX, NY, NZ), 1.0, 6.0, ((1, 16), (2, 8), (3, 2)), jnp.float32)
    metric = draw_metric(jax.random.fold_in(splits[6], 71), 0)
    jacobian = jnp.clip(jnp.exp(math.log(2.0) - 1.3862944 * jax.random.uniform(splits[3], (NX, NY, NZ), jnp.float32) ** levels(splits[3], (NX, NY, NZ), ((0, 16), (1, 8), (2, 2)), -0.2, 0.2)), 0.5, 2.0)
    boundary_kind_code = place_ends(jax.random.randint(splits[4], (STREAM_ELEMENTS, SPAN_ELEMENTS, WALLNORMAL_COUNT), 0, 2), jax.random.fold_in(splits[4], 1), 0, 1).astype(jnp.int32)
    orient = place_ends(jax.random.randint(splits[5], (3, STREAM_ELEMENTS, SPAN_ELEMENTS, WALLNORMAL_COUNT), 0, 2), jax.random.fold_in(splits[5], 1), 0, 1).astype(jnp.int32)
    return dict(state=state, adjoint=adjoint, metric=metric, jacobian=jacobian, boundary_kind_code=boundary_kind_code, orient=orient)


GAMMA = 1.4
INFLOW_STATE = (1.0, 0.4, 0.0, 0.1, 2.085)

def lobatto_matrix():
    points = np.array([-1.0, -1.0 / np.sqrt(5.0), 1.0 / np.sqrt(5.0), 1.0])
    weights = np.array([1.0 / np.prod([points[place] - points[other] for other in range(4) if other != place]) for place in range(4)])
    table = np.zeros((4, 4))
    for place in range(4):
        for other in range(4):
            if other != place:
                table[place, other] = weights[other] / weights[place] / (points[place] - points[other])
        table[place, place] = -np.sum(table[place])
    return table

def line_factors(offset):
    table = lobatto_matrix()
    lower = [float(2.0 * table[place, place + offset]) if place + offset < 4 else 0.0 for place in range(4)]
    upper = [float(2.0 * table[place + offset, place]) if place + offset < 4 else 0.0 for place in range(4)]
    if offset == 1:
        lower[3] = 6.0
        upper[3] = -6.0
    return (lower, upper)

def primitives(values):
    density = values[0]
    momentum = values[1:4]
    velocity = momentum / density[None]
    pressure = (GAMMA - 1.0) * (values[4] - 0.5 * lax.optimization_barrier(jnp.sum(momentum * velocity, axis=0)))
    return (density, velocity, pressure)

def log_mean(first, second):
    ratio = first / second
    frac = (ratio - 1.0) / (ratio + 1.0)
    square = frac * frac
    small = square < 0.01
    series = 1.0 + square / 3.0 + square * square / 5.0 + square * square * square / 7.0
    safe = jnp.where(small, 1.0, frac)
    logged = jnp.log(ratio) / (2.0 * safe)
    factor = jnp.where(small, series, logged)
    return (first + second) / (2.0 * factor)

def two_point(left, right):
    left_density, left_velocity, left_pressure = primitives(left[0:5])
    right_density, right_velocity, right_pressure = primitives(right[0:5])
    normal_avg = 0.5 * (left[5:8] + right[5:8])
    left_beta = left_density / (2.0 * left_pressure)
    right_beta = right_density / (2.0 * right_pressure)
    density_log = log_mean(left_density, right_density)
    beta_log = log_mean(left_beta, right_beta)
    velocity_avg = 0.5 * (left_velocity + right_velocity)
    pressure_hat = 0.5 * (left_density + right_density) / (left_beta + right_beta)
    speed_square = 0.5 * (lax.optimization_barrier(jnp.sum(left_velocity * left_velocity, axis=0)) + lax.optimization_barrier(jnp.sum(right_velocity * right_velocity, axis=0)))
    mass = density_log * lax.optimization_barrier(jnp.sum(velocity_avg * normal_avg, axis=0))
    momentum_flux = mass[None] * velocity_avg + pressure_hat[None] * normal_avg
    energy_flux = mass * (0.5 / ((GAMMA - 1.0) * beta_log) - 0.5 * speed_square) + lax.optimization_barrier(jnp.sum(momentum_flux * velocity_avg, axis=0))
    return jnp.concatenate([mass[None], momentum_flux, energy_flux[None]], axis=0)

def dissipation(left, right):
    left_density, left_velocity, left_pressure = primitives(left[0:5])
    right_density, right_velocity, right_pressure = primitives(right[0:5])
    normal_avg = 0.5 * (left[5:8] + right[5:8])
    vector_length = jnp.sqrt(lax.optimization_barrier(jnp.sum(normal_avg * normal_avg, axis=0)))
    unit = normal_avg / vector_length[None]
    left_normal = lax.optimization_barrier(jnp.sum(left_velocity * unit, axis=0))
    right_normal = lax.optimization_barrier(jnp.sum(right_velocity * unit, axis=0))
    left_sound = jnp.sqrt(GAMMA * left_pressure / left_density)
    right_sound = jnp.sqrt(GAMMA * right_pressure / right_density)
    speed = jnp.sqrt(0.5 * (left_normal * left_normal + right_normal * right_normal)) + 0.5 * (left_sound + right_sound)
    return 0.5 * (speed * vector_length)[None] * (right[0:5] - left[0:5])

def face_flux(left, right):
    return two_point(left, right) - dissipation(left, right)

def ghost(inner, code):
    normal = inner[5:8]
    unit = normal / jnp.sqrt(lax.optimization_barrier(jnp.sum(normal * normal, axis=0)))[None]
    momentum = inner[1:4]
    along = lax.optimization_barrier(jnp.sum(momentum * unit, axis=0))
    reflected = momentum - 2.0 * along[None] * unit
    wall = jnp.concatenate([inner[0:1], reflected, inner[4:5]], axis=0)
    farfield = jnp.stack([jnp.full_like(inner[0], value) for value in INFLOW_STATE], axis=0)
    outer = jnp.where((code == 1)[None], farfield, wall)
    return jnp.concatenate([outer, normal], axis=0)

def flip_blocks(values, dim):
    shape = values.shape
    split = shape[:dim] + (shape[dim] // 4, 4) + shape[dim + 1:]
    return jnp.flip(values.reshape(split), dim + 1).reshape(shape)

def expand(elements):
    return jnp.repeat(jnp.repeat(jnp.repeat(elements, 4, axis=0), 4, axis=1), 4, axis=2)

def pick(local, values):
    result = jnp.zeros(local.shape, jnp.float32)
    for index, value in enumerate(values):
        result = result + value * (local == index).astype(jnp.float32)
    return result

def interior_terms(state, normal, flags, axis):
    bundle = jnp.concatenate([state, normal], axis=0)
    length = state.shape[axis]
    tangent = 2 if axis == 1 else 1
    total = jnp.zeros_like(state)
    for offset in (1, 2, 3):
        left = lax.slice_in_dim(bundle, 0, length - offset, axis=axis)
        right = lax.slice_in_dim(bundle, offset, length, axis=axis)
        shape = [1, 1, 1, 1]
        shape[axis] = length - offset
        local = lax.broadcasted_iota(jnp.int32, tuple(shape), axis) % 4
        lower, upper = line_factors(offset)
        left_factor = pick(local, lower)
        right_factor = pick(local, upper)
        if offset == 1:
            face = local == 3
            turned = face & (lax.slice_in_dim(flags, 0, length - 1, axis=axis - 1)[None] == 1)
            left = jnp.where(turned, flip_blocks(left, tangent), left)
            flux = jax.checkpoint(two_point)(left, right) - jnp.where(face, jax.checkpoint(dissipation)(left, right), 0.0)
            to_left = left_factor * flux
            to_left = jnp.where(turned, flip_blocks(to_left, tangent), to_left)
        else:
            flux = jax.checkpoint(two_point)(left, right)
            to_left = left_factor * flux
        to_right = right_factor * flux
        after = [(0, 0)] * 4
        after[axis] = (0, offset)
        before = [(0, 0)] * 4
        before[axis] = (offset, 0)
        total = total + jnp.pad(to_left, after) + jnp.pad(to_right, before)
    return total

def interior_pullback(state, normal, weight, flags, axis):
    terms, pull = jax.vjp(lambda values: interior_terms(values, normal, flags, axis), state)
    return pull(weight)[0]

def domain_faces(state, normal, weight, codes, axis):
    length = state.shape[axis]
    first_state = lax.slice_in_dim(state, 0, 1, axis=axis)
    first_normal = lax.slice_in_dim(normal, 0, 1, axis=axis)
    first_weight = lax.slice_in_dim(weight, 0, 1, axis=axis)
    first_code = lax.slice_in_dim(codes, 0, 1, axis=axis - 1)
    last_state = lax.slice_in_dim(state, length - 1, length, axis=axis)
    last_normal = lax.slice_in_dim(normal, length - 1, length, axis=axis)
    last_weight = lax.slice_in_dim(weight, length - 1, length, axis=axis)
    last_code = lax.slice_in_dim(codes, length - 1, length, axis=axis - 1)

    def lower(values):
        right = jnp.concatenate([values, first_normal], axis=0)
        return -6.0 * face_flux(ghost(right, first_code), right)

    def upper(values):
        left = jnp.concatenate([values, last_normal], axis=0)
        return 6.0 * face_flux(left, ghost(left, last_code))
    unused, pull_lower = jax.vjp(lower, first_state)
    grad_first = pull_lower(first_weight)[0]
    unused, pull_upper = jax.vjp(upper, last_state)
    grad_last = pull_upper(last_weight)[0]
    after = [(0, 0)] * 4
    after[axis] = (0, length - 1)
    before = [(0, 0)] * 4
    before[axis] = (length - 1, 0)
    return jnp.pad(grad_first, after) + jnp.pad(grad_last, before)

def reference(state, adjoint, metric, jacobian, boundary_kind_code, orient):
    weight = -adjoint / jacobian[None]
    codes = expand(boundary_kind_code)
    result = jnp.zeros_like(state)
    for direction in range(3):
        axis = direction + 1
        normal = metric[3 * direction:3 * direction + 3]
        flags = expand(orient[direction])
        block_extent = 3 if axis == 2 else 2
        count = state.shape[block_extent] // 4

        def one_block(index, accum):
            start = (index * 4).astype(jnp.int32)
            part_state = lax.dynamic_slice_in_dim(state, start, 4, axis=block_extent)
            part_normal = lax.dynamic_slice_in_dim(normal, start, 4, axis=block_extent)
            part_weight = lax.dynamic_slice_in_dim(weight, start, 4, axis=block_extent)
            part_flags = lax.dynamic_slice_in_dim(flags, start, 4, axis=block_extent - 1)
            piece = interior_pullback(part_state, part_normal, part_weight, part_flags, axis)
            return lax.dynamic_update_slice_in_dim(accum, piece, start, axis=block_extent)
        result = result + lax.fori_loop(0, count, one_block, jnp.zeros_like(state))
        result = result + domain_faces(state, normal, weight, codes, axis)
    return result
```

```python
import jax
import jax.numpy as jnp
import numpy as np
from jax import lax
from jax.experimental import pallas as pl
from jax.experimental.pallas import tpu as pltpu
from jax.sharding import PartitionSpec as P

INFLOW_STATE = (1.0, 0.4, 0.0, 0.1, 2.085)
MESH = pl.DeviceIdType.MESH
SLOTS = 7


def lobatto_matrix():
    points = np.array([-1.0, -1.0 / np.sqrt(5.0), 1.0 / np.sqrt(5.0), 1.0])
    weights = np.array(
        [
            1.0 / np.prod([points[place] - points[other] for other in range(4) if other != place])
            for place in range(4)
        ]
    )
    table = np.zeros((4, 4))
    for place in range(4):
        for other in range(4):
            if other != place:
                table[place, other] = (
                    weights[other] / weights[place] / (points[place] - points[other])
                )
        table[place, place] = -np.sum(table[place])
    return table


QUAD = (1.0, 5.0, 5.0, 1.0)
TABLE = lobatto_matrix()


def rcp(value):
    guess = pl.reciprocal(value, approx=True)
    return guess * (2.0 - value * guess)


def dot3(first, second):
    return first[0] * second[0] + first[1] * second[1] + first[2] * second[2]


def log_terms(a, b, log_a, log_b, inv_a, inv_b):
    s = a + b
    rs = rcp(s)
    f = (a - b) * rs
    q = f * f
    small = q < 0.01
    series = 1.0 + q * (1.0 / 3.0 + q * (1.0 / 5.0 + q * (1.0 / 7.0)))
    slope = f * (2.0 / 3.0 + q * (4.0 / 5.0 + q * (6.0 / 7.0)))
    rf = rcp(f)
    logged = (log_a - log_b) * rf
    log_slope = ((s * inv_a) * (s * inv_b) - logged) * rf
    return s, rs, f, jnp.where(small, series, logged), jnp.where(small, slope, log_slope)


def pair(left, right, scale, left_weight=1.0, right_weight=1.0, face=False):
    rho_l, vl, beta_l = left[0], left[1:4], left[4]
    rho_r, vr, beta_r = right[0], right[1:4], right[4]
    wl, wr = left[9:14], right[9:14]
    if left_weight != 1.0:
        wl = [left_weight * w for w in wl]
    if right_weight != 1.0:
        wr = [right_weight * w for w in wr]
    om = [x - y for x, y in zip(wl, wr)]
    o0, ov, oh = om[0], om[1:4], om[4]
    g = [(x + y) * scale for x, y in zip(left[14:17], right[14:17])]
    vs = [x + y for x, y in zip(vl, vr)]
    rho_s, _, rho_f, rho_factor, rho_slope = log_terms(
        rho_l, rho_r, left[5], right[5], left[7], right[7]
    )
    _, beta_i, beta_f, beta_factor, beta_slope = log_terms(
        beta_l, beta_r, left[6], right[6], left[8], right[8]
    )
    p = rcp(rho_factor)
    half_p = 0.5 * p
    mean = rho_s * half_p
    through = dot3(vs, g)
    a = o0 + 0.5 * dot3(ov, vs) + oh * (dot3(vl, vr) + 5.0 * (beta_factor * beta_i))
    b = dot3(ov, g) + oh * through
    ph = rho_s * beta_i
    bi = beta_i * b
    ua = through * a
    k = half_p * (p * rho_slope)
    x = ua * (half_p + k * rho_f) + bi
    y = ua * k
    d_rho_l, d_rho_r = x - y, x + y
    t = mean * through
    e = t * oh
    c = mean * a + ph * oh
    half_t = 0.5 * t
    z = [c * gg + half_t * oo for gg, oo in zip(g, ov)]
    d_v_l = [zz + e * v for zz, v in zip(z, vr)]
    d_v_r = [zz + e * v for zz, v in zip(z, vl)]
    e5 = (-5.0 * e) * (beta_i * beta_i)
    x = e5 * (beta_factor + beta_slope * beta_f) - ph * bi
    y = e5 * beta_slope
    d_beta_l, d_beta_r = x - y, x + y
    if face:
        xl = o0 + dot3(ov, vl) + oh * (10.0 * left[8] * 0.5 + dot3(vl, vl))
        xr = o0 + dot3(ov, vr) + oh * (10.0 * right[8] * 0.5 + dot3(vr, vr))
        kappa = rho_l * xl - rho_r * xr
        n2 = dot3(g, g)
        half_len = 0.5 * jnp.sqrt(n2)
        cl = jnp.sqrt(1.4 * left[8])
        cr = jnp.sqrt(1.4 * right[8])
        sl = dot3(vl, g)
        sr = dot3(vr, g)
        mean_square = 0.5 * (sl * sl + sr * sr)
        rt = lax.rsqrt(mean_square)
        sigma = mean_square * rt + half_len * (cl + cr)
        kr = (0.5 * kappa) * rt
        krl, krr = kr * sl, kr * sr
        ml, mr = sigma * rho_l, sigma * rho_r
        oh2 = 2.0 * oh
        el, er = ml * oh2, mr * oh2
        d_v_l = [d + krl * gg + ml * oo + el * v for d, gg, oo, v in zip(d_v_l, g, ov, vl)]
        d_v_r = [d + krr * gg - mr * oo - er * v for d, gg, oo, v in zip(d_v_r, g, ov, vr)]
        d_rho_l = d_rho_l + sigma * xl
        d_rho_r = d_rho_r - sigma * xr
        kl = kappa * half_len
        d_beta_l = d_beta_l - left[8] * (kl * cl + 5.0 * (el * left[8]))
        d_beta_r = d_beta_r - right[8] * (kl * cr - 5.0 * (er * right[8]))
    return [d_rho_l, *d_v_l, d_beta_l], [d_rho_r, *d_v_r, d_beta_r]


def node_extras(rho, beta, inv_rho, inv_beta):
    return [0.5 * jnp.log(rho), 0.5 * jnp.log(beta), inv_rho, inv_beta]


def line(load, store):
    total = [None] * 4
    for a in range(4):
        for b in range(a + 1, 4):
            factor = 2.0 * QUAD[a] * TABLE[a, b] / 4.0
            wa, wb = 1.0 / QUAD[a], 1.0 / QUAD[b]
            if wa == wb:
                factor, wa, wb = factor * wa, 1.0, 1.0
            first, second = pair(load(a), load(b), float(factor), wa, wb)
            for node, part in ((a, first), (b, second)):
                total[node] = part if total[node] is None else [x + y for x, y in zip(total[node], part)]
    for a in range(4):
        store(a, total[a])


def kernel(
    nx, ny,
    state_ref, adj_ref, met_ref, jac_ref, code_ref, orient_ref, out_ref,
    st, ad, mt, jc, cd, ori, nb, tb, acc, acct, send, recv, gout, mb, el,
    load_sem, send_sem, recv_sem,
):
    f32 = jnp.float32
    ix, iy, iz = lax.axis_index("gx"), lax.axis_index("gy"), lax.axis_index("gz")
    low_x, high_x, low_y, high_y = ix == 0, ix == nx - 1, iy == 0, iy == ny - 1
    ids = [
        {"gx": lax.max(ix - 1, 0)}, {"gx": lax.min(ix + 1, nx - 1)},
        {"gy": lax.max(iy - 1, 0)}, {"gy": lax.min(iy + 1, ny - 1)},
        {"gz": 1 - iz},
    ]
    edge = [low_x, high_x, low_y, high_y, None]
    spans = [(0, 2), (2, 2), (4, 1), (5, 1), (6, 1)]

    loads = [
        pltpu.make_async_copy(src, dst, load_sem.at[n])
        for n, (src, dst) in enumerate(
            ((code_ref, cd), (orient_ref, ori), (state_ref, st), (adj_ref, ad), (jac_ref, jc), (met_ref, mt))
        )
    ]
    for copy in loads:
        copy.start()

    barrier = pltpu.get_barrier_semaphore()
    for side in range(5):
        def greet(side=side):
            pl.semaphore_signal(barrier, inc=1, device_id=ids[side], device_id_type=MESH)

        if edge[side] is None:
            greet()
        else:
            pl.when(jnp.logical_not(edge[side]))(greet)

            @pl.when(edge[side])
            def _(side=side):
                first, count = spans[side]
                for slot in range(first, first + count):
                    for n in range(13):
                        recv[slot, n] = jnp.zeros((8, 128), f32)

    sub = lax.broadcasted_iota(jnp.int32, (8, 128), 0)
    lane = lax.broadcasted_iota(jnp.int32, (8, 128), 1)
    sub_flip = sub ^ 3
    lane_flip = lane ^ 48

    def flip_sub(value):
        return jnp.take_along_axis(value, sub_flip, axis=0, mode="promise_in_bounds")

    def flip_lane(value):
        return jnp.take_along_axis(value, lane_flip, axis=1, mode="promise_in_bounds")

    loads[0].wait()
    loads[1].wait()
    el[0:8, :] = cd[...].astype(f32)
    el[8:32, :] = ori[...].astype(f32)
    spread = (
        lax.broadcasted_iota(jnp.int32, (32, 128), 1) // 4 == lax.broadcasted_iota(jnp.int32, (32, 128), 0)
    ).astype(f32)
    wide = jnp.dot(el[...], spread, preferred_element_type=f32)
    xy = lax.broadcasted_iota(jnp.int32, (8, 128), 1)
    spread_xy = ((xy // 64) * 4 + (xy % 16) // 4 == sub).astype(f32)
    contract = (((0,), (0,)), ((), ()))
    code_z = lax.dot_general(el[0:8, :], spread_xy, contract, preferred_element_type=f32)
    flag_z = lax.dot_general(el[24:32, :], spread_xy, contract, preferred_element_type=f32)

    def two_rows(first, second):
        return jnp.where(
            sub < 4,
            jnp.broadcast_to(wide[first : first + 1], (8, 128)),
            jnp.broadcast_to(wide[second : second + 1], (8, 128)),
        )

    def x_rows(base, ex, half):
        return two_rows(base + ex * 4 + 2 * half, base + ex * 4 + 2 * half + 1)

    def y_rows(base, ey):
        return two_rows(base + ey, base + 4 + ey)

    codes = [x_rows(0, 0, 0), x_rows(0, 0, 1), x_rows(0, 1, 0), x_rows(0, 1, 1), y_rows(0, 0), y_rows(0, 3)]
    low_row = sub % 2 == 0
    codes.append(
        jnp.where(
            low_row,
            jnp.broadcast_to(code_z[0:1], (8, 128)),
            jnp.broadcast_to(code_z[31:32], (8, 128)),
        )
    )
    one, zero = jnp.ones((8, 128), f32), jnp.zeros((8, 128), f32)
    at_edge = [jnp.where(e, one, zero) for e in (low_x, low_x, high_x, high_x, low_y, high_y)]
    at_edge.append(jnp.where(low_row, jnp.where(iz == 0, one, zero), jnp.where(iz == 1, one, zero)))
    signs = [-1.5 * one, -1.5 * one, 1.5 * one, 1.5 * one, -1.5 * one, 1.5 * one, jnp.where(low_row, -1.5 * one, 1.5 * one)]
    for slot in range(SLOTS):
        mb[slot, 0] = signs[slot]
        far = at_edge[slot] * codes[slot]
        mb[slot, 1] = far
        mb[slot, 2] = at_edge[slot] - far
    flag_x_mid = [x_rows(8, 0, half) > 0.5 for half in range(2)]
    flag_x_top = [(x_rows(8, 1, half) > 0.5) & jnp.logical_not(high_x) for half in range(2)]
    flag_y_mid = [y_rows(16, ey) > 0.5 for ey in range(3)]
    flag_y_top = (y_rows(16, 3) > 0.5) & jnp.logical_not(high_y)
    flag_z_top = (jnp.broadcast_to(flag_z[31:32], (8, 128)) > 0.5) & jnp.logical_not(low_row) & (iz == 0)

    def convert(rows):
        rho, m, energy = st[0, rows], [st[n, rows] for n in (1, 2, 3)], st[4, rows]
        r = rcp(rho)
        v = [x * r for x in m]
        pressure = 0.4 * (energy - 0.5 * dot3(m, v))
        beta = (0.5 * rho) * rcp(pressure)
        rj = -rcp(jc[rows])
        w = [ad[n, rows] * rj for n in range(5)]
        w[4] = 0.5 * w[4]
        values = [rho, *v, beta, *node_extras(rho, beta, 0.5 * r, pressure * r), *w]
        for n, value in enumerate(values):
            nb[n, rows] = value
        return values

    for load in loads[2:]:
        load.wait()

    def pack(slot, values, flag=None, flip=None):
        for n, value in enumerate(values):
            if flag is not None:
                value = jnp.where(flag, flip(value), value)
            send[slot, n] = value

    for slot, block in ((0, 0), (1, 1), (2, 14), (3, 15)):
        rows = pl.ds(block * 8, 8)
        values = convert(rows)
        raw = values[0:5] + values[9:14] + [mt[n, rows] for n in range(3)]
        if slot < 2:
            pack(slot, raw)
        else:
            pack(slot, raw, flag_x_top[slot - 2], flip_sub)

    waits = lax.convert_element_type(
        5 - jnp.where(low_x, 1, 0) - jnp.where(high_x, 1, 0) - jnp.where(low_y, 1, 0) - jnp.where(high_y, 1, 0), jnp.int32
    )
    pl.semaphore_wait(barrier, waits)

    landing = [1, 0, 3, 2, 4]
    copies = []
    for side in range(5):
        first, count = spans[side]
        target, _ = spans[landing[side]]
        copies.append(
            pltpu.make_async_remote_copy(
                src_ref=send.at[pl.ds(first, count)],
                dst_ref=recv.at[pl.ds(target, count)],
                send_sem=send_sem.at[side],
                recv_sem=recv_sem.at[landing[side]],
                device_id=ids[side],
                device_id_type=MESH,
            )
        )

    def on_side(side, act):
        if edge[side] is None:
            act()
        else:
            pl.when(jnp.logical_not(edge[side]))(act)

    on_side(0, lambda: copies[0].start())
    on_side(1, lambda: copies[1].start())

    @pl.loop(2, 14)
    def _(block):
        convert(pl.ds(pl.multiple_of(block * 8, 8), 8))

    def load_y(y):
        rows = pl.ds(y, 8, stride=16)
        return [nb[n, rows] for n in range(14)] + [mt[3 + n, rows] for n in range(3)]

    for slot, y in ((4, 0), (5, 15)):
        values = load_y(y)
        raw = values[0:5] + values[9:17]
        if slot == 4:
            pack(slot, raw)
        else:
            pack(slot, raw, flag_y_top, flip_sub)
    on_side(2, lambda: copies[2].start())
    on_side(3, lambda: copies[3].start())

    for n in range(5):
        tb[n, 0:128] = jnp.transpose(nb[n])
        tb[9 + n, 0:128] = jnp.transpose(nb[9 + n])
    for n in range(3):
        tb[14 + n, 0:128] = jnp.transpose(mt[6 + n])
    raw_t = [0, 1, 2, 3, 4, 9, 10, 11, 12, 13, 14, 15, 16]
    low_z = [jnp.broadcast_to(tb[n, 0:1], (8, 128)) for n in raw_t]
    high_z = [jnp.broadcast_to(tb[n, 127:128], (8, 128)) for n in raw_t]
    pack(6, [jnp.where(low_row, x, y) for x, y in zip(low_z, high_z)], flag_z_top, flip_lane)
    copies[4].start()

    @pl.loop(0, 16)
    def _(block):
        rows = pl.ds(pl.multiple_of(block * 8, 8), 8)
        rho, beta = tb[0, rows], tb[4, rows]
        for n, value in enumerate(node_extras(rho, beta, 0.5 * rcp(rho), 0.5 * rcp(beta))):
            tb[5 + n, rows] = value

    def load_x(rows):
        return [nb[n, rows] for n in range(14)] + [mt[n, rows] for n in range(3)]

    @pl.loop(0, 4)
    def _(chunk):
        base = (chunk // 2) * 64 + (chunk % 2) * 8

        def at(a):
            return pl.ds(pl.multiple_of(base + a * 16, 8), 8)

        def store(a, total):
            for n in range(5):
                acc[n, at(a)] = total[n]

        line(lambda a: load_x(at(a)), store)

    def add(ref, rows, parts):
        for n in range(5):
            ref[n, rows] = ref[n, rows] + parts[n]

    def flipped(values, flag, flip):
        return [jnp.where(flag, flip(value), value) for value in values]

    for half in range(2):
        lower, upper = pl.ds(48 + 8 * half, 8), pl.ds(64 + 8 * half, 8)
        left = flipped(load_x(lower), flag_x_mid[half], flip_sub)
        to_l, to_u = pair(left, load_x(upper), 1.5, face=True)
        add(acc, lower, flipped(to_l, flag_x_mid[half], flip_sub))
        add(acc, upper, to_u)

    @pl.loop(0, 4)
    def _(chunk):
        def store(a, total):
            add(acc, pl.ds(chunk * 4 + a, 8, stride=16), total)

        line(lambda a: load_y(chunk * 4 + a), store)

    for ey in range(3):
        left = flipped(load_y(4 * ey + 3), flag_y_mid[ey], flip_sub)
        to_l, to_u = pair(left, load_y(4 * ey + 4), 1.5, face=True)
        add(acc, pl.ds(4 * ey + 3, 8, stride=16), flipped(to_l, flag_y_mid[ey], flip_sub))
        add(acc, pl.ds(4 * ey + 4, 8, stride=16), to_u)

    def rows_z(chunk, a):
        return pl.ds(chunk * 32 + a, 8, stride=4)

    def load_z(rows):
        return [tb[n, rows] for n in range(17)]

    @pl.loop(0, 4)
    def _(chunk):
        def store(a, total):
            for n in range(5):
                acct[n, rows_z(chunk, a)] = total[n]

        line(lambda a: load_z(rows_z(chunk, a)), store)

    for chunk in range(4):
        flag = flag_z[8 * chunk : 8 * chunk + 8] > 0.5
        lower = rows_z(chunk, 3)
        left = flipped(load_z(lower), flag, flip_lane)
        upper = rows_z(chunk, 4)
        right = load_z(upper)
        to_l, to_u = pair(left, right, 1.5, face=True)
        to_l = flipped(to_l, flag, flip_lane)
        if chunk == 3:
            inside = sub < 7
            to_l = [jnp.where(inside, x, 0.0) for x in to_l]
            to_u = [jnp.where(inside, x, 0.0) for x in to_u]
        add(acct, lower, to_l)
        add(acct, upper, to_u)

    for side in (4, 2, 3, 0, 1):
        on_side(side, lambda side=side: copies[landing[side]].wait_recv())
    for n in range(13):
        recv[6, n] = pltpu.roll(recv[6, n], 1, 0)

    inflow = np.array(INFLOW_STATE)
    inflow_v = inflow[1:4] / inflow[0]
    inflow_p = 0.4 * (inflow[4] - 0.5 * np.sum(inflow[1:4] * inflow_v))
    far_values = [float(inflow[0]), *[float(x) for x in inflow_v], float(inflow[0] / (2.0 * inflow_p))]

    @pl.loop(0, SLOTS)
    def _(slot):
        own = [send[slot, n] for n in range(13)]
        other = [recv[slot, n] for n in range(13)]
        scale, far, wall = mb[slot, 0], mb[slot, 1], mb[slot, 2]
        is_far, is_wall = far > 0.5, wall > 0.5
        outside = is_far | is_wall
        g = own[10:13]
        turn = 2.0 * rcp(dot3(g, g))

        def mirror(v):
            along = turn * dot3(v, g)
            return [x - along * y for x, y in zip(v, g)]

        image = [own[0], *mirror(own[1:4]), own[4]]
        oth = [
            jnp.where(is_far, f, jnp.where(is_wall, i, o)) for f, i, o in zip(far_values, image, other[0:5])
        ]
        oth_w = [jnp.where(outside, 0.0, o) for o in other[5:10]]
        oth_g = [jnp.where(outside, i, o) for i, o in zip(g, other[10:13])]

        def full(prim, w, normal):
            return [*prim, *node_extras(prim[0], prim[4], 0.5 * rcp(prim[0]), 0.5 * rcp(prim[4])), *w, *normal]

        mine, theirs = pair(full(own[0:5], own[5:10], g), full(oth, oth_w, oth_g), scale, face=True)
        back = [theirs[0], *mirror(theirs[1:4]), theirs[4]]
        for n in range(5):
            gout[slot, n] = mine[n] + jnp.where(is_wall, back[n], 0.0)

    for slot, block in ((0, 0), (1, 1), (2, 14), (3, 15)):
        parts = [gout[slot, n] for n in range(5)]
        if slot >= 2:
            parts = flipped(parts, flag_x_top[slot - 2], flip_sub)
        add(acc, pl.ds(block * 8, 8), parts)
    add(acc, pl.ds(0, 8, stride=16), [gout[4, n] for n in range(5)])
    add(acc, pl.ds(15, 8, stride=16), flipped([gout[5, n] for n in range(5)], flag_y_top, flip_sub))
    for n in range(5):
        part = gout[6, n]
        part = jnp.where(flag_z_top, flip_lane(part), part)
        acct[n, 0:1] = acct[n, 0:1] + part[0:1]
        acct[n, 127:128] = acct[n, 127:128] + part[1:2]

    for n in range(5):
        acc[n] = acc[n] + jnp.transpose(acct[n, 0:128])

    @pl.loop(0, 16)
    def _(block):
        rows = pl.ds(pl.multiple_of(block * 8, 8), 8)
        v, beta, r = [nb[n, rows] for n in (1, 2, 3)], nb[4, rows], 2.0 * nb[7, rows]
        d_rho, d_v, d_beta = acc[0, rows], [acc[n, rows] for n in (1, 2, 3)], acc[4, rows]
        db = d_beta * (beta * r)
        d_p = (-0.8 * beta) * db
        out_ref[4, rows] = d_p
        for n in range(3):
            out_ref[1 + n, rows] = d_v[n] * r - d_p * v[n]
        out_ref[0, rows] = d_rho + db - r * dot3(d_v, v) + 0.5 * d_p * dot3(v, v)

    for side in (4, 2, 3, 0, 1):
        on_side(side, lambda side=side: copies[side].wait_send())


def solution(mesh):
    nx, ny, nz = mesh.shape["gx"], mesh.shape["gy"], mesh.shape["gz"]
    assert nz == 2

    def body(state, adjoint, metric, jacobian, boundary_kind_code, orient):
        assert state.shape == (5, 8, 16, 128)
        f32 = jnp.float32
        hbm = pl.BlockSpec(memory_space=pl.ANY)
        vmem = pltpu.VMEM
        out = pl.pallas_call(
            lambda *refs: kernel(nx, ny, *refs),
            out_shape=jax.ShapeDtypeStruct((5, 128, 128), f32),
            in_specs=[hbm] * 6,
            out_specs=pl.BlockSpec(memory_space=vmem),
            scratch_shapes=[
                vmem((5, 128, 128), f32),
                vmem((5, 128, 128), f32),
                vmem((9, 128, 128), f32),
                vmem((128, 128), f32),
                vmem((8, 32), jnp.int32),
                vmem((24, 32), jnp.int32),
                vmem((14, 128, 128), f32),
                vmem((17, 136, 128), f32),
                vmem((5, 128, 128), f32),
                vmem((5, 136, 128), f32),
                vmem((SLOTS, 13, 8, 128), f32),
                vmem((SLOTS, 13, 8, 128), f32),
                vmem((SLOTS, 5, 8, 128), f32),
                vmem((SLOTS, 3, 8, 128), f32),
                vmem((32, 32), f32),
                pltpu.SemaphoreType.DMA((6,)),
                pltpu.SemaphoreType.DMA((5,)),
                pltpu.SemaphoreType.DMA((5,)),
            ],
            compiler_params=pltpu.CompilerParams(
                collective_id=0, has_side_effects=True, vmem_limit_bytes=32 * 1024 * 1024
            ),
            name="adjoint_residual",
        )(
            state.reshape(5, 128, 128),
            adjoint.reshape(5, 128, 128),
            metric.reshape(9, 128, 128),
            jacobian.reshape(128, 128),
            boundary_kind_code.reshape(8, 32),
            orient.reshape(24, 32),
        )
        return out.reshape(5, 8, 16, 128)

    return jax.shard_map(
        body,
        mesh=mesh,
        in_specs=(
            P(None, "gx", "gy", "gz"),
            P(None, "gx", "gy", "gz"),
            P(None, "gx", "gy", "gz"),
            P("gx", "gy", "gz"),
            P("gx", "gy", "gz"),
            P(None, "gx", "gy", "gz"),
        ),
        out_specs=P(None, "gx", "gy", "gz"),
        check_vma=False,
    )
```

```python
import jax
import jax.numpy as jnp
import numpy as np
from jax import lax
from jax.experimental import pallas as pl
from jax.experimental.pallas import tpu as pltpu
from jax.sharding import PartitionSpec as P

INFLOW_STATE = (1.0, 0.4, 0.0, 0.1, 2.085)
MESH = pl.DeviceIdType.MESH
SLOTS = 7


def lobatto_matrix():
    points = np.array([-1.0, -1.0 / np.sqrt(5.0), 1.0 / np.sqrt(5.0), 1.0])
    weights = np.array(
        [
            1.0 / np.prod([points[place] - points[other] for other in range(4) if other != place])
            for place in range(4)
        ]
    )
    table = np.zeros((4, 4))
    for place in range(4):
        for other in range(4):
            if other != place:
                table[place, other] = (
                    weights[other] / weights[place] / (points[place] - points[other])
                )
        table[place, place] = -np.sum(table[place])
    return table


QUAD = (1.0, 5.0, 5.0, 1.0)
TABLE = lobatto_matrix()


def rcp(value):
    guess = pl.reciprocal(value, approx=True)
    return guess * (2.0 - value * guess)


def dot3(first, second):
    return first[0] * second[0] + first[1] * second[1] + first[2] * second[2]


def log_terms(a, b, log_a, log_b, inv_a, inv_b):
    s = a + b
    rs = rcp(s)
    f = (a - b) * rs
    q = f * f
    small = q < 0.01
    series = 1.0 + q * (1.0 / 3.0 + q * (1.0 / 5.0 + q * (1.0 / 7.0)))
    slope = f * (2.0 / 3.0 + q * (4.0 / 5.0 + q * (6.0 / 7.0)))
    rf = rcp(f)
    logged = (log_a - log_b) * rf
    log_slope = ((s * inv_a) * (s * inv_b) - logged) * rf
    return s, rs, f, jnp.where(small, series, logged), jnp.where(small, slope, log_slope)


def pair(left, right, scale, left_weight=1.0, right_weight=1.0, face=False):
    rho_l, vl, beta_l = left[0], left[1:4], left[4]
    rho_r, vr, beta_r = right[0], right[1:4], right[4]
    wl, wr = left[9:14], right[9:14]
    if left_weight != 1.0:
        wl = [left_weight * w for w in wl]
    if right_weight != 1.0:
        wr = [right_weight * w for w in wr]
    om = [x - y for x, y in zip(wl, wr)]
    o0, ov, oh = om[0], om[1:4], om[4]
    g = [(x + y) * scale for x, y in zip(left[14:17], right[14:17])]
    vs = [x + y for x, y in zip(vl, vr)]
    rho_s, _, rho_f, rho_factor, rho_slope = log_terms(
        rho_l, rho_r, left[5], right[5], left[7], right[7]
    )
    _, beta_i, beta_f, beta_factor, beta_slope = log_terms(
        beta_l, beta_r, left[6], right[6], left[8], right[8]
    )
    p = rcp(rho_factor)
    half_p = 0.5 * p
    mean = rho_s * half_p
    through = dot3(vs, g)
    a = o0 + 0.5 * dot3(ov, vs) + oh * (dot3(vl, vr) + 5.0 * (beta_factor * beta_i))
    b = dot3(ov, g) + oh * through
    ph = rho_s * beta_i
    bi = beta_i * b
    ua = through * a
    k = half_p * (p * rho_slope)
    x = ua * (half_p + k * rho_f) + bi
    y = ua * k
    d_rho_l, d_rho_r = x - y, x + y
    t = mean * through
    e = t * oh
    c = mean * a + ph * oh
    half_t = 0.5 * t
    z = [c * gg + half_t * oo for gg, oo in zip(g, ov)]
    d_v_l = [zz + e * v for zz, v in zip(z, vr)]
    d_v_r = [zz + e * v for zz, v in zip(z, vl)]
    e5 = (-5.0 * e) * (beta_i * beta_i)
    x = e5 * (beta_factor + beta_slope * beta_f) - ph * bi
    y = e5 * beta_slope
    d_beta_l, d_beta_r = x - y, x + y
    if face:
        xl = o0 + dot3(ov, vl) + oh * (10.0 * left[8] * 0.5 + dot3(vl, vl))
        xr = o0 + dot3(ov, vr) + oh * (10.0 * right[8] * 0.5 + dot3(vr, vr))
        kappa = rho_l * xl - rho_r * xr
        n2 = dot3(g, g)
        half_len = 0.5 * jnp.sqrt(n2)
        cl = jnp.sqrt(1.4 * left[8])
        cr = jnp.sqrt(1.4 * right[8])
        sl = dot3(vl, g)
        sr = dot3(vr, g)
        mean_square = 0.5 * (sl * sl + sr * sr)
        rt = lax.rsqrt(mean_square)
        sigma = mean_square * rt + half_len * (cl + cr)
        kr = (0.5 * kappa) * rt
        krl, krr = kr * sl, kr * sr
        ml, mr = sigma * rho_l, sigma * rho_r
        oh2 = 2.0 * oh
        el, er = ml * oh2, mr * oh2
        d_v_l = [d + krl * gg + ml * oo + el * v for d, gg, oo, v in zip(d_v_l, g, ov, vl)]
        d_v_r = [d + krr * gg - mr * oo - er * v for d, gg, oo, v in zip(d_v_r, g, ov, vr)]
        d_rho_l = d_rho_l + sigma * xl
        d_rho_r = d_rho_r - sigma * xr
        kl = kappa * half_len
        d_beta_l = d_beta_l - left[8] * (kl * cl + 5.0 * (el * left[8]))
        d_beta_r = d_beta_r - right[8] * (kl * cr - 5.0 * (er * right[8]))
    return [d_rho_l, *d_v_l, d_beta_l], [d_rho_r, *d_v_r, d_beta_r]


def node_extras(rho, beta, inv_rho, inv_beta):
    return [0.5 * jnp.log(rho), 0.5 * jnp.log(beta), inv_rho, inv_beta]


def line(load, store):
    total = [None] * 4
    for a in range(4):
        for b in range(a + 1, 4):
            factor = 2.0 * QUAD[a] * TABLE[a, b] / 4.0
            wa, wb = 1.0 / QUAD[a], 1.0 / QUAD[b]
            if wa == wb:
                factor, wa, wb = factor * wa, 1.0, 1.0
            first, second = pair(load(a), load(b), float(factor), wa, wb)
            for node, part in ((a, first), (b, second)):
                total[node] = part if total[node] is None else [x + y for x, y in zip(total[node], part)]
    for a in range(4):
        store(a, total[a])


def kernel(
    nx, ny,
    state_ref, adj_ref, met_ref, jac_ref, code_ref, orient_ref, out_ref,
    st, ad, mt, jc, cd, ori, nb, tb, acc, acct, send, recv, gout, mb, el,
    load_sem, send_sem, recv_sem,
):
    f32 = jnp.float32
    ix, iy, iz = lax.axis_index("gx"), lax.axis_index("gy"), lax.axis_index("gz")
    low_x, high_x, low_y, high_y = ix == 0, ix == nx - 1, iy == 0, iy == ny - 1
    ids = [
        {"gx": lax.max(ix - 1, 0)}, {"gx": lax.min(ix + 1, nx - 1)},
        {"gy": lax.max(iy - 1, 0)}, {"gy": lax.min(iy + 1, ny - 1)},
        {"gz": 1 - iz},
    ]
    edge = [low_x, high_x, low_y, high_y, None]
    spans = [(0, 2), (2, 2), (4, 1), (5, 1), (6, 1)]

    outer = [pl.ds(0, 16), pl.ds(112, 16)]
    inner = pl.ds(16, 96)
    moves = [(code_ref, cd), (orient_ref, ori)]
    for rows in outer:
        moves += [(src.at[:, rows], dst.at[:, rows]) for src, dst in ((state_ref, st), (adj_ref, ad))]
        moves += [(jac_ref.at[rows], jc.at[rows]), (met_ref.at[0:3, rows], mt.at[0:3, rows])]
    moves += [(src.at[:, inner], dst.at[:, inner]) for src, dst in ((state_ref, st), (adj_ref, ad))]
    moves += [(jac_ref.at[inner], jc.at[inner]), (met_ref.at[3:9], mt.at[3:9])]
    moves.append((met_ref.at[0:3, inner], mt.at[0:3, inner]))
    loads = [pltpu.make_async_copy(src, dst, load_sem.at[n]) for n, (src, dst) in enumerate(moves)]
    barrier = pltpu.get_barrier_semaphore()
    for side in range(5):
        def greet(side=side):
            pl.semaphore_signal(barrier, inc=1, device_id=ids[side], device_id_type=MESH)

        if edge[side] is None:
            greet()
        else:
            pl.when(jnp.logical_not(edge[side]))(greet)
    for copy in loads:
        copy.start()
    for side in range(4):
        if edge[side] is not None:
            @pl.when(edge[side])
            def _(side=side):
                first, count = spans[side]
                for slot in range(first, first + count):
                    for n in range(13):
                        recv[slot, n] = jnp.zeros((8, 128), f32)

    sub = lax.broadcasted_iota(jnp.int32, (8, 128), 0)
    lane = lax.broadcasted_iota(jnp.int32, (8, 128), 1)
    sub_flip = sub ^ 3
    lane_flip = lane ^ 48

    def flip_sub(value):
        return jnp.take_along_axis(value, sub_flip, axis=0, mode="promise_in_bounds")

    def flip_lane(value):
        return jnp.take_along_axis(value, lane_flip, axis=1, mode="promise_in_bounds")

    loads[0].wait()
    loads[1].wait()
    el[0:8, :] = cd[...].astype(f32)
    el[8:32, :] = ori[...].astype(f32)
    spread = (
        lax.broadcasted_iota(jnp.int32, (32, 128), 1) // 4 == lax.broadcasted_iota(jnp.int32, (32, 128), 0)
    ).astype(f32)
    wide = jnp.dot(el[...], spread, preferred_element_type=f32)
    xy = lax.broadcasted_iota(jnp.int32, (8, 128), 1)
    spread_xy = ((xy // 64) * 4 + (xy % 16) // 4 == sub).astype(f32)
    contract = (((0,), (0,)), ((), ()))
    code_z = lax.dot_general(el[0:8, :], spread_xy, contract, preferred_element_type=f32)
    flag_z = lax.dot_general(el[24:32, :], spread_xy, contract, preferred_element_type=f32)

    def two_rows(first, second):
        return jnp.where(
            sub < 4,
            jnp.broadcast_to(wide[first : first + 1], (8, 128)),
            jnp.broadcast_to(wide[second : second + 1], (8, 128)),
        )

    def x_rows(base, ex, half):
        return two_rows(base + ex * 4 + 2 * half, base + ex * 4 + 2 * half + 1)

    def y_rows(base, ey):
        return two_rows(base + ey, base + 4 + ey)

    codes = [x_rows(0, 0, 0), x_rows(0, 0, 1), x_rows(0, 1, 0), x_rows(0, 1, 1), y_rows(0, 0), y_rows(0, 3)]
    low_row = sub % 2 == 0
    codes.append(
        jnp.where(
            low_row,
            jnp.broadcast_to(code_z[0:1], (8, 128)),
            jnp.broadcast_to(code_z[31:32], (8, 128)),
        )
    )
    one, zero = jnp.ones((8, 128), f32), jnp.zeros((8, 128), f32)
    at_edge = [jnp.where(e, one, zero) for e in (low_x, low_x, high_x, high_x, low_y, high_y)]
    at_edge.append(jnp.where(low_row, jnp.where(iz == 0, one, zero), jnp.where(iz == 1, one, zero)))
    signs = [-1.5 * one, -1.5 * one, 1.5 * one, 1.5 * one, -1.5 * one, 1.5 * one, jnp.where(low_row, -1.5 * one, 1.5 * one)]
    for slot in range(SLOTS):
        mb[slot, 0] = signs[slot]
        far = at_edge[slot] * codes[slot]
        mb[slot, 1] = far
        mb[slot, 2] = at_edge[slot] - far
    flag_x_mid = [x_rows(8, 0, half) > 0.5 for half in range(2)]
    flag_x_top = [(x_rows(8, 1, half) > 0.5) & jnp.logical_not(high_x) for half in range(2)]
    flag_y_mid = [y_rows(16, ey) > 0.5 for ey in range(3)]
    flag_y_top = (y_rows(16, 3) > 0.5) & jnp.logical_not(high_y)
    flag_z_top = (jnp.broadcast_to(flag_z[31:32], (8, 128)) > 0.5) & jnp.logical_not(low_row) & (iz == 0)

    def convert(rows):
        rho, m, energy = st[0, rows], [st[n, rows] for n in (1, 2, 3)], st[4, rows]
        r = rcp(rho)
        v = [x * r for x in m]
        pressure = 0.4 * (energy - 0.5 * dot3(m, v))
        beta = (0.5 * rho) * rcp(pressure)
        rj = -rcp(jc[rows])
        w = [ad[n, rows] * rj for n in range(5)]
        w[4] = 0.5 * w[4]
        values = [rho, *v, beta, *node_extras(rho, beta, 0.5 * r, pressure * r), *w]
        for n, value in enumerate(values):
            nb[n, rows] = value
        return values

    for load in loads[2:10]:
        load.wait()

    def pack(slot, values, flag=None, flip=None):
        for n, value in enumerate(values):
            if flag is not None:
                value = jnp.where(flag, flip(value), value)
            send[slot, n] = value

    for slot, block in ((0, 0), (1, 1), (2, 14), (3, 15)):
        rows = pl.ds(block * 8, 8)
        values = convert(rows)
        raw = values[0:5] + values[9:14] + [mt[n, rows] for n in range(3)]
        if slot < 2:
            pack(slot, raw)
        else:
            pack(slot, raw, flag_x_top[slot - 2], flip_sub)

    waits = lax.convert_element_type(
        5 - jnp.where(low_x, 1, 0) - jnp.where(high_x, 1, 0) - jnp.where(low_y, 1, 0) - jnp.where(high_y, 1, 0), jnp.int32
    )
    pl.semaphore_wait(barrier, waits)

    landing = [1, 0, 3, 2, 4]
    def copy_of(side, place):
        source, target = spans[side][0] + place, spans[landing[side]][0] + place
        return pltpu.make_async_remote_copy(
            src_ref=send.at[source],
            dst_ref=recv.at[target],
            send_sem=send_sem.at[source],
            recv_sem=recv_sem.at[target],
            device_id=ids[side],
            device_id_type=MESH,
        )

    copies = [[copy_of(side, place) for place in range(spans[side][1])] for side in range(5)]

    def on_side(side, act):
        if edge[side] is None:
            act()
        else:
            pl.when(jnp.logical_not(edge[side]))(act)

    for place in range(2):
        for side in (0, 1):
            on_side(side, copies[side][place].start)

    for load in loads[10:13]:
        load.wait()

    @pl.loop(2, 14)
    def _(block):
        convert(pl.ds(pl.multiple_of(block * 8, 8), 8))

    loads[13].wait()

    def load_y(y):
        rows = pl.ds(y, 8, stride=16)
        return [nb[n, rows] for n in range(14)] + [mt[3 + n, rows] for n in range(3)]

    for slot, y in ((4, 0), (5, 15)):
        values = load_y(y)
        raw = values[0:5] + values[9:17]
        if slot == 4:
            pack(slot, raw)
        else:
            pack(slot, raw, flag_y_top, flip_sub)
    on_side(2, copies[2][0].start)
    on_side(3, copies[3][0].start)

    for n in range(5):
        tb[n, 0:128] = jnp.transpose(nb[n])
        tb[9 + n, 0:128] = jnp.transpose(nb[9 + n])
    for n in range(3):
        tb[14 + n, 0:128] = jnp.transpose(mt[6 + n])
    raw_t = [0, 1, 2, 3, 4, 9, 10, 11, 12, 13, 14, 15, 16]
    low_z = [jnp.broadcast_to(tb[n, 0:1], (8, 128)) for n in raw_t]
    high_z = [jnp.broadcast_to(tb[n, 127:128], (8, 128)) for n in raw_t]
    pack(6, [jnp.where(low_row, x, y) for x, y in zip(low_z, high_z)], flag_z_top, flip_lane)
    copies[4][0].start()

    @pl.loop(0, 16)
    def _(block):
        rows = pl.ds(pl.multiple_of(block * 8, 8), 8)
        rho, beta = tb[0, rows], tb[4, rows]
        for n, value in enumerate(node_extras(rho, beta, 0.5 * rcp(rho), 0.5 * rcp(beta))):
            tb[5 + n, rows] = value

    loads[14].wait()

    def load_x(rows):
        return [nb[n, rows] for n in range(14)] + [mt[n, rows] for n in range(3)]

    @pl.loop(0, 4)
    def _(chunk):
        base = (chunk // 2) * 64 + (chunk % 2) * 8

        def at(a):
            return pl.ds(pl.multiple_of(base + a * 16, 8), 8)

        def store(a, total):
            for n in range(5):
                acc[n, at(a)] = total[n]

        line(lambda a: load_x(at(a)), store)

    def add(ref, rows, parts):
        for n in range(5):
            ref[n, rows] = ref[n, rows] + parts[n]

    def flipped(values, flag, flip):
        return [jnp.where(flag, flip(value), value) for value in values]

    for half in range(2):
        lower, upper = pl.ds(48 + 8 * half, 8), pl.ds(64 + 8 * half, 8)
        left = flipped(load_x(lower), flag_x_mid[half], flip_sub)
        to_l, to_u = pair(left, load_x(upper), 1.5, face=True)
        add(acc, lower, flipped(to_l, flag_x_mid[half], flip_sub))
        add(acc, upper, to_u)

    @pl.loop(0, 4)
    def _(chunk):
        def store(a, total):
            add(acc, pl.ds(chunk * 4 + a, 8, stride=16), total)

        line(lambda a: load_y(chunk * 4 + a), store)

    for ey in range(3):
        left = flipped(load_y(4 * ey + 3), flag_y_mid[ey], flip_sub)
        to_l, to_u = pair(left, load_y(4 * ey + 4), 1.5, face=True)
        add(acc, pl.ds(4 * ey + 3, 8, stride=16), flipped(to_l, flag_y_mid[ey], flip_sub))
        add(acc, pl.ds(4 * ey + 4, 8, stride=16), to_u)

    def rows_z(chunk, a):
        return pl.ds(chunk * 32 + a, 8, stride=4)

    def load_z(rows):
        return [tb[n, rows] for n in range(17)]

    @pl.loop(0, 4)
    def _(chunk):
        def store(a, total):
            for n in range(5):
                acct[n, rows_z(chunk, a)] = total[n]

        line(lambda a: load_z(rows_z(chunk, a)), store)

    for chunk in range(4):
        flag = flag_z[8 * chunk : 8 * chunk + 8] > 0.5
        lower = rows_z(chunk, 3)
        left = flipped(load_z(lower), flag, flip_lane)
        upper = rows_z(chunk, 4)
        right = load_z(upper)
        to_l, to_u = pair(left, right, 1.5, face=True)
        to_l = flipped(to_l, flag, flip_lane)
        if chunk == 3:
            inside = sub < 7
            to_l = [jnp.where(inside, x, 0.0) for x in to_l]
            to_u = [jnp.where(inside, x, 0.0) for x in to_u]
        add(acct, lower, to_l)
        add(acct, upper, to_u)

    for side in (4, 2, 3):
        on_side(side, copies[landing[side]][0].wait_recv)
    for n in range(13):
        recv[6, n] = pltpu.roll(recv[6, n], 1, 0)

    inflow = np.array(INFLOW_STATE)
    inflow_v = inflow[1:4] / inflow[0]
    inflow_p = 0.4 * (inflow[4] - 0.5 * np.sum(inflow[1:4] * inflow_v))
    far_values = [float(inflow[0]), *[float(x) for x in inflow_v], float(inflow[0] / (2.0 * inflow_p))]

    def side_faces(slot):
        own = [send[slot, n] for n in range(13)]
        other = [recv[slot, n] for n in range(13)]
        scale, far, wall = mb[slot, 0], mb[slot, 1], mb[slot, 2]
        is_far, is_wall = far > 0.5, wall > 0.5
        outside = is_far | is_wall
        g = own[10:13]
        turn = 2.0 * rcp(dot3(g, g))

        def mirror(v):
            along = turn * dot3(v, g)
            return [x - along * y for x, y in zip(v, g)]

        image = [own[0], *mirror(own[1:4]), own[4]]
        oth = [
            jnp.where(is_far, f, jnp.where(is_wall, i, o)) for f, i, o in zip(far_values, image, other[0:5])
        ]
        oth_w = [jnp.where(outside, 0.0, o) for o in other[5:10]]
        oth_g = [jnp.where(outside, i, o) for i, o in zip(g, other[10:13])]

        def full(prim, w, normal):
            return [*prim, *node_extras(prim[0], prim[4], 0.5 * rcp(prim[0]), 0.5 * rcp(prim[4])), *w, *normal]

        mine, theirs = pair(full(own[0:5], own[5:10], g), full(oth, oth_w, oth_g), scale, face=True)
        back = [theirs[0], *mirror(theirs[1:4]), theirs[4]]
        return [x + jnp.where(is_wall, y, 0.0) for x, y in zip(mine, back)]

    @pl.loop(4, SLOTS)
    def _(slot):
        for n, part in enumerate(side_faces(slot)):
            gout[slot - 4, n] = part

    add(acc, pl.ds(0, 8, stride=16), [gout[0, n] for n in range(5)])
    add(acc, pl.ds(15, 8, stride=16), flipped([gout[1, n] for n in range(5)], flag_y_top, flip_sub))
    for n in range(5):
        part = gout[2, n]
        part = jnp.where(flag_z_top, flip_lane(part), part)
        acct[n, 0:1] = acct[n, 0:1] + part[0:1]
        acct[n, 127:128] = acct[n, 127:128] + part[1:2]

    for n in range(5):
        acc[n] = acc[n] + jnp.transpose(acct[n, 0:128])

    def finish(rows, parts):
        v, beta, r = [nb[n, rows] for n in (1, 2, 3)], nb[4, rows], 2.0 * nb[7, rows]
        d_rho, d_v, d_beta = parts[0], parts[1:4], parts[4]
        db = d_beta * (beta * r)
        d_p = (-0.8 * beta) * db
        out_ref[4, rows] = d_p
        for n in range(3):
            out_ref[1 + n, rows] = d_v[n] * r - d_p * v[n]
        out_ref[0, rows] = d_rho + db - r * dot3(d_v, v) + 0.5 * d_p * dot3(v, v)

    @pl.loop(2, 14)
    def _(block):
        rows = pl.ds(pl.multiple_of(block * 8, 8), 8)
        finish(rows, [acc[n, rows] for n in range(5)])

    for slot in (0, 2, 1, 3):
        on_side(slot // 2, copies[landing[slot // 2]][slot % 2].wait_recv)

        rows = pl.ds((slot // 2) * 112 + (slot % 2) * 8, 8)
        parts = side_faces(slot)
        if slot >= 2:
            parts = flipped(parts, flag_x_top[slot - 2], flip_sub)
        finish(rows, [acc[n, rows] + part for n, part in enumerate(parts)])

    for side in (4, 2, 3, 0, 1):
        for copy in copies[side]:
            on_side(side, copy.wait_send)


def solution(mesh):
    nx, ny, nz = mesh.shape["gx"], mesh.shape["gy"], mesh.shape["gz"]
    assert nz == 2

    def body(state, adjoint, metric, jacobian, boundary_kind_code, orient):
        assert state.shape == (5, 8, 16, 128)
        f32 = jnp.float32
        hbm = pl.BlockSpec(memory_space=pltpu.HBM)
        vmem = pltpu.VMEM
        out = pl.pallas_call(
            lambda *refs: kernel(nx, ny, *refs),
            out_shape=jax.ShapeDtypeStruct((5, 128, 128), f32),
            in_specs=[hbm] * 6,
            out_specs=pl.BlockSpec(memory_space=vmem),
            scratch_shapes=[
                vmem((5, 128, 128), f32),
                vmem((5, 128, 128), f32),
                vmem((9, 128, 128), f32),
                vmem((128, 128), f32),
                vmem((8, 32), jnp.int32),
                vmem((24, 32), jnp.int32),
                vmem((14, 128, 128), f32),
                vmem((17, 136, 128), f32),
                vmem((5, 128, 128), f32),
                vmem((5, 136, 128), f32),
                vmem((SLOTS, 13, 8, 128), f32),
                vmem((SLOTS, 13, 8, 128), f32),
                vmem((3, 5, 8, 128), f32),
                vmem((SLOTS, 3, 8, 128), f32),
                vmem((32, 32), f32),
                pltpu.SemaphoreType.DMA((15,)),
                pltpu.SemaphoreType.DMA((SLOTS,)),
                pltpu.SemaphoreType.DMA((SLOTS,)),
            ],
            compiler_params=pltpu.CompilerParams(
                collective_id=0, has_side_effects=True, vmem_limit_bytes=32 * 1024 * 1024
            ),
            name="adjoint_residual",
        )(
            *(
                pltpu.with_memory_space_constraint(value, pltpu.HBM)
                for value in (
                    state.reshape(5, 128, 128),
                    adjoint.reshape(5, 128, 128),
                    metric.reshape(9, 128, 128),
                    jacobian.reshape(128, 128),
                    boundary_kind_code.reshape(8, 32),
                    orient.reshape(24, 32),
                )
            )
        )
        return out.reshape(5, 8, 16, 128)

    return jax.shard_map(
        body,
        mesh=mesh,
        in_specs=(
            P(None, "gx", "gy", "gz"),
            P(None, "gx", "gy", "gz"),
            P(None, "gx", "gy", "gz"),
            P("gx", "gy", "gz"),
            P("gx", "gy", "gz"),
            P(None, "gx", "gy", "gz"),
        ),
        out_specs=P(None, "gx", "gy", "gz"),
        check_vma=False,
    )
```

```python
import jax
import jax.numpy as jnp
import numpy as np
from jax import lax
from jax.experimental import pallas as pl
from jax.experimental.pallas import tpu as pltpu
from jax.sharding import PartitionSpec as P

INFLOW_STATE = (1.0, 0.4, 0.0, 0.1, 2.085)
MESH = pl.DeviceIdType.MESH
SLOTS = 7


def lobatto_matrix():
    points = np.array([-1.0, -1.0 / np.sqrt(5.0), 1.0 / np.sqrt(5.0), 1.0])
    weights = np.array(
        [
            1.0 / np.prod([points[place] - points[other] for other in range(4) if other != place])
            for place in range(4)
        ]
    )
    table = np.zeros((4, 4))
    for place in range(4):
        for other in range(4):
            if other != place:
                table[place, other] = (
                    weights[other] / weights[place] / (points[place] - points[other])
                )
        table[place, place] = -np.sum(table[place])
    return table


QUAD = (1.0, 5.0, 5.0, 1.0)
TABLE = lobatto_matrix()


def rcp(value):
    guess = pl.reciprocal(value, approx=True)
    return guess * (2.0 - value * guess)


def dot3(first, second):
    return first[0] * second[0] + first[1] * second[1] + first[2] * second[2]


def log_terms(a, b, log_a, log_b, inv_a, inv_b):
    s = a + b
    rs = rcp(s)
    f = (a - b) * rs
    q = f * f
    small = q < 0.01
    series = 1.0 + q * (1.0 / 3.0 + q * (1.0 / 5.0 + q * (1.0 / 7.0)))
    slope = f * (2.0 / 3.0 + q * (4.0 / 5.0 + q * (6.0 / 7.0)))
    rf = rcp(f)
    logged = (log_a - log_b) * rf
    log_slope = ((s * inv_a) * (s * inv_b) - logged) * rf
    return s, rs, f, jnp.where(small, series, logged), jnp.where(small, slope, log_slope)


def pair(left, right, scale, left_weight=1.0, right_weight=1.0, face=False):
    rho_l, vl, beta_l = left[0], left[1:4], left[4]
    rho_r, vr, beta_r = right[0], right[1:4], right[4]
    wl, wr = left[9:14], right[9:14]
    if left_weight != 1.0:
        wl = [left_weight * w for w in wl]
    if right_weight != 1.0:
        wr = [right_weight * w for w in wr]
    om = [x - y for x, y in zip(wl, wr)]
    o0, ov, oh = om[0], om[1:4], om[4]
    g = [(x + y) * scale for x, y in zip(left[14:17], right[14:17])]
    vs = [x + y for x, y in zip(vl, vr)]
    rho_s, _, rho_f, rho_factor, rho_slope = log_terms(
        rho_l, rho_r, left[5], right[5], left[7], right[7]
    )
    _, beta_i, beta_f, beta_factor, beta_slope = log_terms(
        beta_l, beta_r, left[6], right[6], left[8], right[8]
    )
    p = rcp(rho_factor)
    half_p = 0.5 * p
    mean = rho_s * half_p
    through = dot3(vs, g)
    a = o0 + 0.5 * dot3(ov, vs) + oh * (dot3(vl, vr) + 5.0 * (beta_factor * beta_i))
    b = dot3(ov, g) + oh * through
    ph = rho_s * beta_i
    bi = beta_i * b
    ua = through * a
    k = half_p * (p * rho_slope)
    x = ua * (half_p + k * rho_f) + bi
    y = ua * k
    d_rho_l, d_rho_r = x - y, x + y
    t = mean * through
    e = t * oh
    c = mean * a + ph * oh
    half_t = 0.5 * t
    z = [c * gg + half_t * oo for gg, oo in zip(g, ov)]
    d_v_l = [zz + e * v for zz, v in zip(z, vr)]
    d_v_r = [zz + e * v for zz, v in zip(z, vl)]
    e5 = (-5.0 * e) * (beta_i * beta_i)
    x = e5 * (beta_factor + beta_slope * beta_f) - ph * bi
    y = e5 * beta_slope
    d_beta_l, d_beta_r = x - y, x + y
    if face:
        xl = o0 + dot3(ov, vl) + oh * (10.0 * left[8] * 0.5 + dot3(vl, vl))
        xr = o0 + dot3(ov, vr) + oh * (10.0 * right[8] * 0.5 + dot3(vr, vr))
        kappa = rho_l * xl - rho_r * xr
        n2 = dot3(g, g)
        half_len = 0.5 * jnp.sqrt(n2)
        cl = jnp.sqrt(1.4 * left[8])
        cr = jnp.sqrt(1.4 * right[8])
        sl = dot3(vl, g)
        sr = dot3(vr, g)
        mean_square = 0.5 * (sl * sl + sr * sr)
        rt = lax.rsqrt(mean_square)
        sigma = mean_square * rt + half_len * (cl + cr)
        kr = (0.5 * kappa) * rt
        krl, krr = kr * sl, kr * sr
        ml, mr = sigma * rho_l, sigma * rho_r
        oh2 = 2.0 * oh
        el, er = ml * oh2, mr * oh2
        d_v_l = [d + krl * gg + ml * oo + el * v for d, gg, oo, v in zip(d_v_l, g, ov, vl)]
        d_v_r = [d + krr * gg - mr * oo - er * v for d, gg, oo, v in zip(d_v_r, g, ov, vr)]
        d_rho_l = d_rho_l + sigma * xl
        d_rho_r = d_rho_r - sigma * xr
        kl = kappa * half_len
        d_beta_l = d_beta_l - left[8] * (kl * cl + 5.0 * (el * left[8]))
        d_beta_r = d_beta_r - right[8] * (kl * cr - 5.0 * (er * right[8]))
    return [d_rho_l, *d_v_l, d_beta_l], [d_rho_r, *d_v_r, d_beta_r]


def node_extras(rho, beta, inv_rho, inv_beta):
    return [0.5 * jnp.log(rho), 0.5 * jnp.log(beta), inv_rho, inv_beta]


def line(load, store):
    total = [None] * 4
    for a in range(4):
        for b in range(a + 1, 4):
            factor = 2.0 * QUAD[a] * TABLE[a, b] / 4.0
            wa, wb = 1.0 / QUAD[a], 1.0 / QUAD[b]
            if wa == wb:
                factor, wa, wb = factor * wa, 1.0, 1.0
            first, second = pair(load(a), load(b), float(factor), wa, wb)
            for node, part in ((a, first), (b, second)):
                total[node] = part if total[node] is None else [x + y for x, y in zip(total[node], part)]
    for a in range(4):
        store(a, total[a])


def kernel(
    nx, ny,
    state_ref, adj_ref, met_ref, jac_ref, code_ref, orient_ref, out_ref,
    st, ad, mt, jc, cd, ori, nb, tb, acc, acct, send, recv, gout, mb, el,
    load_sem, send_sem, recv_sem, ready_sem,
):
    f32 = jnp.float32
    ix, iy, iz = lax.axis_index("gx"), lax.axis_index("gy"), lax.axis_index("gz")
    low_x, high_x, low_y, high_y = ix == 0, ix == nx - 1, iy == 0, iy == ny - 1
    ids = [
        {"gx": lax.max(ix - 1, 0)}, {"gx": lax.min(ix + 1, nx - 1)},
        {"gy": lax.max(iy - 1, 0)}, {"gy": lax.min(iy + 1, ny - 1)},
        {"gz": 1 - iz},
    ]
    inner_side = [jnp.logical_not(e) for e in (low_x, high_x, low_y, high_y)] + [None]
    opens = [(ix + 3) % 4 < 2, ix % 4 >= 2, (iy + 3) % 4 != 3, iy % 4 == 3, iz == 0]

    def both(first, second):
        return second if first is None else first & second

    greets = [both(there, jnp.logical_not(theirs)) for there, theirs in zip(inner_side, opens)]
    greeted = [both(there, theirs) for there, theirs in zip(inner_side, opens)]
    spans = [(0, 2), (2, 2), (4, 1), (5, 1), (6, 1)]

    outer = [pl.ds(0, 16), pl.ds(112, 16)]
    inner = pl.ds(16, 96)
    moves = [(code_ref, cd), (orient_ref, ori)]
    for rows in outer:
        moves += [(src.at[:, rows], dst.at[:, rows]) for src, dst in ((state_ref, st), (adj_ref, ad))]
        moves += [(jac_ref.at[rows], jc.at[rows]), (met_ref.at[0:3, rows], mt.at[0:3, rows])]
    moves += [(src.at[:, inner], dst.at[:, inner]) for src, dst in ((state_ref, st), (adj_ref, ad))]
    moves += [(jac_ref.at[inner], jc.at[inner]), (met_ref.at[3:6], mt.at[3:6])]
    moves += [(met_ref.at[0:3, inner], mt.at[0:3, inner]), (met_ref.at[6:9], mt.at[6:9])]
    loads = [pltpu.make_async_copy(src, dst, load_sem.at[n]) for n, (src, dst) in enumerate(moves)]
    barrier = pltpu.get_barrier_semaphore()
    for side in range(5):
        @pl.when(greets[side])
        def _(side=side):
            pl.semaphore_signal(barrier, inc=1, device_id=ids[side], device_id_type=MESH)

    for copy in loads:
        copy.start()
    for side in range(4):
        @pl.when(jnp.logical_not(inner_side[side]))
        def _(side=side):
            first, count = spans[side]
            for slot in range(first, first + count):
                for n in range(13):
                    recv[slot, n] = jnp.zeros((8, 128), f32)

    sub = lax.broadcasted_iota(jnp.int32, (8, 128), 0)
    lane = lax.broadcasted_iota(jnp.int32, (8, 128), 1)
    sub_flip = sub ^ 3
    lane_flip = lane ^ 48

    def flip_sub(value):
        return jnp.take_along_axis(value, sub_flip, axis=0, mode="promise_in_bounds")

    def flip_lane(value):
        return jnp.take_along_axis(value, lane_flip, axis=1, mode="promise_in_bounds")

    loads[0].wait()
    loads[1].wait()
    el[0:8, :] = cd[...].astype(f32)
    el[8:32, :] = ori[...].astype(f32)
    spread = (
        lax.broadcasted_iota(jnp.int32, (32, 128), 1) // 4 == lax.broadcasted_iota(jnp.int32, (32, 128), 0)
    ).astype(f32)
    wide = jnp.dot(el[...], spread, preferred_element_type=f32)
    xy = lax.broadcasted_iota(jnp.int32, (8, 128), 1)
    spread_xy = ((xy // 64) * 4 + (xy % 16) // 4 == sub).astype(f32)
    contract = (((0,), (0,)), ((), ()))
    code_z = lax.dot_general(el[0:8, :], spread_xy, contract, preferred_element_type=f32)
    flag_z = lax.dot_general(el[24:32, :], spread_xy, contract, preferred_element_type=f32)

    def two_rows(first, second):
        return jnp.where(
            sub < 4,
            jnp.broadcast_to(wide[first : first + 1], (8, 128)),
            jnp.broadcast_to(wide[second : second + 1], (8, 128)),
        )

    def x_rows(base, ex, half):
        return two_rows(base + ex * 4 + 2 * half, base + ex * 4 + 2 * half + 1)

    def y_rows(base, ey):
        return two_rows(base + ey, base + 4 + ey)

    codes = [x_rows(0, 0, 0), x_rows(0, 0, 1), x_rows(0, 1, 0), x_rows(0, 1, 1), y_rows(0, 0), y_rows(0, 3)]
    low_row = sub % 2 == 0
    codes.append(
        jnp.where(
            low_row,
            jnp.broadcast_to(code_z[0:1], (8, 128)),
            jnp.broadcast_to(code_z[31:32], (8, 128)),
        )
    )
    one, zero = jnp.ones((8, 128), f32), jnp.zeros((8, 128), f32)
    at_edge = [jnp.where(e, one, zero) for e in (low_x, low_x, high_x, high_x, low_y, high_y)]
    at_edge.append(jnp.where(low_row, jnp.where(iz == 0, one, zero), jnp.where(iz == 1, one, zero)))
    signs = [-1.5 * one, -1.5 * one, 1.5 * one, 1.5 * one, -1.5 * one, 1.5 * one, jnp.where(low_row, -1.5 * one, 1.5 * one)]
    for slot in range(SLOTS):
        mb[slot, 0] = signs[slot]
        far = at_edge[slot] * codes[slot]
        mb[slot, 1] = far
        mb[slot, 2] = at_edge[slot] - far
    flag_x_mid = [x_rows(8, 0, half) > 0.5 for half in range(2)]
    flag_x_top = [(x_rows(8, 1, half) > 0.5) & jnp.logical_not(high_x) for half in range(2)]
    flag_y_mid = [y_rows(16, ey) > 0.5 for ey in range(3)]
    flag_y_top = (y_rows(16, 3) > 0.5) & jnp.logical_not(high_y)
    flag_z_top = (jnp.broadcast_to(flag_z[31:32], (8, 128)) > 0.5) & jnp.logical_not(low_row) & (iz == 0)

    def convert(rows, keep=True):
        rho, m, energy = st[0, rows], [st[n, rows] for n in (1, 2, 3)], st[4, rows]
        r = rcp(rho)
        v = [x * r for x in m]
        pressure = 0.4 * (energy - 0.5 * dot3(m, v))
        beta = (0.5 * rho) * rcp(pressure)
        rj = -rcp(jc[rows])
        w = [ad[n, rows] * rj for n in range(5)]
        w[4] = 0.5 * w[4]
        values = [rho, *v, beta, *node_extras(rho, beta, 0.5 * r, pressure * r), *w]
        if keep:
            for n, value in enumerate(values):
                nb[n, rows] = value
        return values

    for load in loads[2:10]:
        load.wait()

    def pack(slot, values, flag=None, flip=None):
        for n, value in enumerate(values):
            if flag is not None:
                value = jnp.where(flag, flip(value), value)
            send[slot, n] = value

    for slot, block in ((0, 0), (1, 1), (2, 14), (3, 15)):
        rows = pl.ds(block * 8, 8)
        values = convert(rows)
        raw = values[0:5] + values[9:14] + [mt[n, rows] for n in range(3)]
        if slot < 2:
            pack(slot, raw)
        else:
            pack(slot, raw, flag_x_top[slot - 2], flip_sub)

    landing = [1, 0, 3, 2, 4]
    def copy_of(side, place):
        source, target = spans[side][0] + place, spans[landing[side]][0] + place
        return pltpu.make_async_remote_copy(
            src_ref=send.at[source],
            dst_ref=recv.at[target],
            send_sem=send_sem.at[source],
            recv_sem=recv_sem.at[target],
            device_id=ids[side],
            device_id_type=MESH,
        )

    copies = [[copy_of(side, place) for place in range(spans[side][1])] for side in range(5)]

    def on_side(side, act):
        if inner_side[side] is None:
            act()
        else:
            pl.when(inner_side[side])(act)

    def start(side):
        for copy in copies[side]:
            copy.start()

    arrivals = sum(jnp.where(here, 1, 0) for here in greeted)

    @pl.when(arrivals > 0)
    def _():
        pl.semaphore_wait(barrier, arrivals)

    for side in range(5):
        @pl.when(greeted[side])
        def _(side=side):
            pl.semaphore_signal(ready_sem.at[landing[side]], inc=1, device_id=ids[side], device_id_type=MESH)

    for side in (1, 0):
        pl.when(greeted[side])(lambda side=side: start(side))

    for load in loads[10:14]:
        load.wait()
    for slot, y, flag in ((4, 0, None), (5, 15, flag_y_top)):
        rows = pl.ds(y, 8, stride=16)
        values = convert(rows, keep=False)
        pack(slot, values[0:5] + values[9:14] + [mt[3 + n, rows] for n in range(3)], flag, flip_sub)
    for side in (2, 3):
        pl.when(greeted[side])(lambda side=side: start(side))

    @pl.loop(2, 14)
    def _(block):
        convert(pl.ds(pl.multiple_of(block * 8, 8), 8))

    def load_y(y):
        rows = pl.ds(y, 8, stride=16)
        return [nb[n, rows] for n in range(14)] + [mt[3 + n, rows] for n in range(3)]

    loads[14].wait()

    def load_x(rows):
        return [nb[n, rows] for n in range(14)] + [mt[n, rows] for n in range(3)]

    @pl.loop(0, 4)
    def _(chunk):
        base = (chunk // 2) * 64 + (chunk % 2) * 8

        def at(a):
            return pl.ds(pl.multiple_of(base + a * 16, 8), 8)

        def store(a, total):
            for n in range(5):
                acc[n, at(a)] = total[n]

        line(lambda a: load_x(at(a)), store)

    for side in (1, 0, 2, 3):
        @pl.when(greets[side])
        def _(side=side):
            pl.semaphore_wait(ready_sem.at[side], 1)
            start(side)

    loads[15].wait()
    for n in range(5):
        tb[n, 0:128] = jnp.transpose(nb[n])
        tb[9 + n, 0:128] = jnp.transpose(nb[9 + n])
    for n in range(3):
        tb[14 + n, 0:128] = jnp.transpose(mt[6 + n])
    raw_t = [0, 1, 2, 3, 4, 9, 10, 11, 12, 13, 14, 15, 16]
    low_z = [jnp.broadcast_to(tb[n, 0:1], (8, 128)) for n in raw_t]
    high_z = [jnp.broadcast_to(tb[n, 127:128], (8, 128)) for n in raw_t]
    pack(6, [jnp.where(low_row, x, y) for x, y in zip(low_z, high_z)], flag_z_top, flip_lane)

    @pl.when(greets[4])
    def _():
        pl.semaphore_wait(ready_sem.at[4], 1)

    copies[4][0].start()

    @pl.loop(0, 16)
    def _(block):
        rows = pl.ds(pl.multiple_of(block * 8, 8), 8)
        rho, beta = tb[0, rows], tb[4, rows]
        for n, value in enumerate(node_extras(rho, beta, 0.5 * rcp(rho), 0.5 * rcp(beta))):
            tb[5 + n, rows] = value

    def add(ref, rows, parts):
        for n in range(5):
            ref[n, rows] = ref[n, rows] + parts[n]

    def flipped(values, flag, flip):
        return [jnp.where(flag, flip(value), value) for value in values]

    for half in range(2):
        lower, upper = pl.ds(48 + 8 * half, 8), pl.ds(64 + 8 * half, 8)
        left = flipped(load_x(lower), flag_x_mid[half], flip_sub)
        to_l, to_u = pair(left, load_x(upper), 1.5, face=True)
        add(acc, lower, flipped(to_l, flag_x_mid[half], flip_sub))
        add(acc, upper, to_u)

    @pl.loop(0, 4)
    def _(chunk):
        def store(a, total):
            add(acc, pl.ds(chunk * 4 + a, 8, stride=16), total)

        line(lambda a: load_y(chunk * 4 + a), store)

    for ey in range(3):
        left = flipped(load_y(4 * ey + 3), flag_y_mid[ey], flip_sub)
        to_l, to_u = pair(left, load_y(4 * ey + 4), 1.5, face=True)
        add(acc, pl.ds(4 * ey + 3, 8, stride=16), flipped(to_l, flag_y_mid[ey], flip_sub))
        add(acc, pl.ds(4 * ey + 4, 8, stride=16), to_u)

    def rows_z(chunk, a):
        return pl.ds(chunk * 32 + a, 8, stride=4)

    def load_z(rows):
        return [tb[n, rows] for n in range(17)]

    @pl.loop(0, 4)
    def _(chunk):
        def store(a, total):
            for n in range(5):
                acct[n, rows_z(chunk, a)] = total[n]

        line(lambda a: load_z(rows_z(chunk, a)), store)

    for chunk in range(4):
        flag = flag_z[8 * chunk : 8 * chunk + 8] > 0.5
        lower = rows_z(chunk, 3)
        left = flipped(load_z(lower), flag, flip_lane)
        upper = rows_z(chunk, 4)
        right = load_z(upper)
        to_l, to_u = pair(left, right, 1.5, face=True)
        to_l = flipped(to_l, flag, flip_lane)
        if chunk == 3:
            inside = sub < 7
            to_l = [jnp.where(inside, x, 0.0) for x in to_l]
            to_u = [jnp.where(inside, x, 0.0) for x in to_u]
        add(acct, lower, to_l)
        add(acct, upper, to_u)

    for side in (4, 2, 3):
        on_side(side, copies[landing[side]][0].wait_recv)
    for n in range(13):
        recv[6, n] = pltpu.roll(recv[6, n], 1, 0)

    inflow = np.array(INFLOW_STATE)
    inflow_v = inflow[1:4] / inflow[0]
    inflow_p = 0.4 * (inflow[4] - 0.5 * np.sum(inflow[1:4] * inflow_v))
    far_values = [float(inflow[0]), *[float(x) for x in inflow_v], float(inflow[0] / (2.0 * inflow_p))]

    def side_faces(slot):
        own = [send[slot, n] for n in range(13)]
        other = [recv[slot, n] for n in range(13)]
        scale, far, wall = mb[slot, 0], mb[slot, 1], mb[slot, 2]
        is_far, is_wall = far > 0.5, wall > 0.5
        outside = is_far | is_wall
        g = own[10:13]
        turn = 2.0 * rcp(dot3(g, g))

        def mirror(v):
            along = turn * dot3(v, g)
            return [x - along * y for x, y in zip(v, g)]

        image = [own[0], *mirror(own[1:4]), own[4]]
        oth = [
            jnp.where(is_far, f, jnp.where(is_wall, i, o)) for f, i, o in zip(far_values, image, other[0:5])
        ]
        oth_w = [jnp.where(outside, 0.0, o) for o in other[5:10]]
        oth_g = [jnp.where(outside, i, o) for i, o in zip(g, other[10:13])]

        def full(prim, w, normal):
            return [*prim, *node_extras(prim[0], prim[4], 0.5 * rcp(prim[0]), 0.5 * rcp(prim[4])), *w, *normal]

        mine, theirs = pair(full(own[0:5], own[5:10], g), full(oth, oth_w, oth_g), scale, face=True)
        back = [theirs[0], *mirror(theirs[1:4]), theirs[4]]
        return [x + jnp.where(is_wall, y, 0.0) for x, y in zip(mine, back)]

    @pl.loop(4, SLOTS)
    def _(slot):
        for n, part in enumerate(side_faces(slot)):
            gout[slot - 4, n] = part

    add(acc, pl.ds(0, 8, stride=16), [gout[0, n] for n in range(5)])
    add(acc, pl.ds(15, 8, stride=16), flipped([gout[1, n] for n in range(5)], flag_y_top, flip_sub))
    for n in range(5):
        part = gout[2, n]
        part = jnp.where(flag_z_top, flip_lane(part), part)
        acct[n, 0:1] = acct[n, 0:1] + part[0:1]
        acct[n, 127:128] = acct[n, 127:128] + part[1:2]

    for n in range(5):
        acc[n] = acc[n] + jnp.transpose(acct[n, 0:128])

    def finish(rows, parts):
        v, beta, r = [nb[n, rows] for n in (1, 2, 3)], nb[4, rows], 2.0 * nb[7, rows]
        d_rho, d_v, d_beta = parts[0], parts[1:4], parts[4]
        db = d_beta * (beta * r)
        d_p = (-0.8 * beta) * db
        out_ref[4, rows] = d_p
        for n in range(3):
            out_ref[1 + n, rows] = d_v[n] * r - d_p * v[n]
        out_ref[0, rows] = d_rho + db - r * dot3(d_v, v) + 0.5 * d_p * dot3(v, v)

    @pl.loop(2, 14)
    def _(block):
        rows = pl.ds(pl.multiple_of(block * 8, 8), 8)
        finish(rows, [acc[n, rows] for n in range(5)])

    for slot in (2, 3, 0, 1):
        on_side(slot // 2, copies[landing[slot // 2]][slot % 2].wait_recv)

        rows = pl.ds((slot // 2) * 112 + (slot % 2) * 8, 8)
        parts = side_faces(slot)
        if slot >= 2:
            parts = flipped(parts, flag_x_top[slot - 2], flip_sub)
        finish(rows, [acc[n, rows] + part for n, part in enumerate(parts)])

    for side in (4, 2, 3, 0, 1):
        for copy in copies[side]:
            on_side(side, copy.wait_send)


def solution(mesh):
    nx, ny, nz = mesh.shape["gx"], mesh.shape["gy"], mesh.shape["gz"]
    assert nz == 2

    def body(state, adjoint, metric, jacobian, boundary_kind_code, orient):
        assert state.shape == (5, 8, 16, 128)
        f32 = jnp.float32
        hbm = pl.BlockSpec(memory_space=pltpu.HBM)
        vmem = pltpu.VMEM
        out = pl.pallas_call(
            lambda *refs: kernel(nx, ny, *refs),
            out_shape=jax.ShapeDtypeStruct((5, 128, 128), f32),
            in_specs=[hbm] * 6,
            out_specs=pl.BlockSpec(memory_space=vmem),
            scratch_shapes=[
                vmem((5, 128, 128), f32),
                vmem((5, 128, 128), f32),
                vmem((9, 128, 128), f32),
                vmem((128, 128), f32),
                vmem((8, 32), jnp.int32),
                vmem((24, 32), jnp.int32),
                vmem((14, 128, 128), f32),
                vmem((17, 136, 128), f32),
                vmem((5, 128, 128), f32),
                vmem((5, 136, 128), f32),
                vmem((SLOTS, 13, 8, 128), f32),
                vmem((SLOTS, 13, 8, 128), f32),
                vmem((3, 5, 8, 128), f32),
                vmem((SLOTS, 3, 8, 128), f32),
                vmem((32, 32), f32),
                pltpu.SemaphoreType.DMA((16,)),
                pltpu.SemaphoreType.DMA((SLOTS,)),
                pltpu.SemaphoreType.DMA((SLOTS,)),
                pltpu.SemaphoreType.REGULAR((5,)),
            ],
            compiler_params=pltpu.CompilerParams(
                collective_id=0, has_side_effects=True, vmem_limit_bytes=32 * 1024 * 1024
            ),
            name="adjoint_residual",
        )(
            *(
                pltpu.with_memory_space_constraint(value, pltpu.HBM)
                for value in (
                    state.reshape(5, 128, 128),
                    adjoint.reshape(5, 128, 128),
                    metric.reshape(9, 128, 128),
                    jacobian.reshape(128, 128),
                    boundary_kind_code.reshape(8, 32),
                    orient.reshape(24, 32),
                )
            )
        )
        return out.reshape(5, 8, 16, 128)

    return jax.shard_map(
        body,
        mesh=mesh,
        in_specs=(
            P(None, "gx", "gy", "gz"),
            P(None, "gx", "gy", "gz"),
            P(None, "gx", "gy", "gz"),
            P("gx", "gy", "gz"),
            P("gx", "gy", "gz"),
            P(None, "gx", "gy", "gz"),
        ),
        out_specs=P(None, "gx", "gy", "gz"),
        check_vma=False,
    )
```

```python
import jax
import jax.numpy as jnp
import numpy as np
from jax import lax
from jax.experimental import pallas as pl
from jax.experimental.pallas import tpu as pltpu
from jax.sharding import PartitionSpec as P

INFLOW_STATE = (1.0, 0.4, 0.0, 0.1, 2.085)
MESH = pl.DeviceIdType.MESH
SLOTS = 7


def lobatto_matrix():
    points = np.array([-1.0, -1.0 / np.sqrt(5.0), 1.0 / np.sqrt(5.0), 1.0])
    weights = np.array(
        [
            1.0 / np.prod([points[place] - points[other] for other in range(4) if other != place])
            for place in range(4)
        ]
    )
    table = np.zeros((4, 4))
    for place in range(4):
        for other in range(4):
            if other != place:
                table[place, other] = (
                    weights[other] / weights[place] / (points[place] - points[other])
                )
        table[place, place] = -np.sum(table[place])
    return table


QUAD = (1.0, 5.0, 5.0, 1.0)
TABLE = lobatto_matrix()


def rcp(value):
    guess = pl.reciprocal(value, approx=True)
    return guess * (2.0 - value * guess)


def dot3(first, second):
    return first[0] * second[0] + first[1] * second[1] + first[2] * second[2]


def log_terms(a, b, log_a, log_b, inv_a, inv_b):
    s = a + b
    rs = rcp(s)
    f = (a - b) * rs
    q = f * f
    small = q < 0.01
    series = 1.0 + q * (1.0 / 3.0 + q * (1.0 / 5.0 + q * (1.0 / 7.0)))
    slope = f * (2.0 / 3.0 + q * (4.0 / 5.0 + q * (6.0 / 7.0)))
    rf = rcp(f)
    logged = (log_a - log_b) * rf
    log_slope = ((s * inv_a) * (s * inv_b) - logged) * rf
    return s, rs, f, jnp.where(small, series, logged), jnp.where(small, slope, log_slope)


def pair(left, right, scale, left_weight=1.0, right_weight=1.0, face=False):
    rho_l, vl, beta_l = left[0], left[1:4], left[4]
    rho_r, vr, beta_r = right[0], right[1:4], right[4]
    wl, wr = left[9:14], right[9:14]
    if left_weight != 1.0:
        wl = [left_weight * w for w in wl]
    if right_weight != 1.0:
        wr = [right_weight * w for w in wr]
    om = [x - y for x, y in zip(wl, wr)]
    o0, ov, oh = om[0], om[1:4], om[4]
    g = [(x + y) * scale for x, y in zip(left[14:17], right[14:17])]
    vs = [x + y for x, y in zip(vl, vr)]
    rho_s, _, rho_f, rho_factor, rho_slope = log_terms(
        rho_l, rho_r, left[5], right[5], left[7], right[7]
    )
    _, beta_i, beta_f, beta_factor, beta_slope = log_terms(
        beta_l, beta_r, left[6], right[6], left[8], right[8]
    )
    p = rcp(rho_factor)
    half_p = 0.5 * p
    mean = rho_s * half_p
    through = dot3(vs, g)
    a = o0 + 0.5 * dot3(ov, vs) + oh * (dot3(vl, vr) + 5.0 * (beta_factor * beta_i))
    b = dot3(ov, g) + oh * through
    ph = rho_s * beta_i
    bi = beta_i * b
    ua = through * a
    k = half_p * (p * rho_slope)
    x = ua * (half_p + k * rho_f) + bi
    y = ua * k
    d_rho_l, d_rho_r = x - y, x + y
    t = mean * through
    e = t * oh
    c = mean * a + ph * oh
    half_t = 0.5 * t
    z = [c * gg + half_t * oo for gg, oo in zip(g, ov)]
    d_v_l = [zz + e * v for zz, v in zip(z, vr)]
    d_v_r = [zz + e * v for zz, v in zip(z, vl)]
    e5 = (-5.0 * e) * (beta_i * beta_i)
    x = e5 * (beta_factor + beta_slope * beta_f) - ph * bi
    y = e5 * beta_slope
    d_beta_l, d_beta_r = x - y, x + y
    if face:
        xl = o0 + dot3(ov, vl) + oh * (10.0 * left[8] * 0.5 + dot3(vl, vl))
        xr = o0 + dot3(ov, vr) + oh * (10.0 * right[8] * 0.5 + dot3(vr, vr))
        kappa = rho_l * xl - rho_r * xr
        n2 = dot3(g, g)
        half_len = 0.5 * jnp.sqrt(n2)
        cl = jnp.sqrt(1.4 * left[8])
        cr = jnp.sqrt(1.4 * right[8])
        sl = dot3(vl, g)
        sr = dot3(vr, g)
        mean_square = 0.5 * (sl * sl + sr * sr)
        rt = lax.rsqrt(mean_square)
        sigma = mean_square * rt + half_len * (cl + cr)
        kr = (0.5 * kappa) * rt
        krl, krr = kr * sl, kr * sr
        ml, mr = sigma * rho_l, sigma * rho_r
        oh2 = 2.0 * oh
        el, er = ml * oh2, mr * oh2
        d_v_l = [d + krl * gg + ml * oo + el * v for d, gg, oo, v in zip(d_v_l, g, ov, vl)]
        d_v_r = [d + krr * gg - mr * oo - er * v for d, gg, oo, v in zip(d_v_r, g, ov, vr)]
        d_rho_l = d_rho_l + sigma * xl
        d_rho_r = d_rho_r - sigma * xr
        kl = kappa * half_len
        d_beta_l = d_beta_l - left[8] * (kl * cl + 5.0 * (el * left[8]))
        d_beta_r = d_beta_r - right[8] * (kl * cr - 5.0 * (er * right[8]))
    return [d_rho_l, *d_v_l, d_beta_l], [d_rho_r, *d_v_r, d_beta_r]


def node_extras(rho, beta, inv_rho, inv_beta):
    return [0.5 * jnp.log(rho), 0.5 * jnp.log(beta), inv_rho, inv_beta]


def primitives(u):
    v = [x * rcp(u[0]) for x in u[1:4]]
    pressure = 0.4 * (u[4] - 0.5 * dot3(u[1:4], v))
    return [u[0], *v, (0.5 * u[0]) * rcp(pressure)]


def line(load, store):
    total = [None] * 4
    for a in range(4):
        for b in range(a + 1, 4):
            factor = 2.0 * QUAD[a] * TABLE[a, b] / 4.0
            wa, wb = 1.0 / QUAD[a], 1.0 / QUAD[b]
            if wa == wb:
                factor, wa, wb = factor * wa, 1.0, 1.0
            first, second = pair(load(a), load(b), float(factor), wa, wb)
            for node, part in ((a, first), (b, second)):
                total[node] = part if total[node] is None else [x + y for x, y in zip(total[node], part)]
    for a in range(4):
        store(a, total[a])


def kernel(
    nx, ny,
    state_ref, adj_ref, met_ref, jac_ref, code_ref, orient_ref, out_ref,
    st, ad, mt, jc, cd, ori, nb, tb, acc, acct, send, recv, gout, mb, el,
    send_w, recv_u, recv_g, recv_w, recv_f, xo,
    load_sem, send_sem, recv_sem, x_send_sem, x_recv_sem, ready_sem,
):
    f32 = jnp.float32
    ix, iy, iz = lax.axis_index("gx"), lax.axis_index("gy"), lax.axis_index("gz")
    low_x, high_x, low_y, high_y = ix == 0, ix == nx - 1, iy == 0, iy == ny - 1
    ids = [
        {"gx": lax.max(ix - 1, 0)}, {"gx": lax.min(ix + 1, nx - 1)},
        {"gy": lax.max(iy - 1, 0)}, {"gy": lax.min(iy + 1, ny - 1)},
        {"gz": 1 - iz},
    ]
    inner_side = [jnp.logical_not(e) for e in (low_x, high_x, low_y, high_y)] + [None]
    opens = [(ix + 3) % 4 < 2, ix % 4 >= 2, (iy + 3) % 4 != 3, iy % 4 == 3, iz == 0]

    def both(first, second):
        return second if first is None else first & second

    greets = [both(there, jnp.logical_not(theirs)) for there, theirs in zip(inner_side, opens)]
    greeted = [both(there, theirs) for there, theirs in zip(inner_side, opens)]
    place = [None, None, 0, 1, 2]

    outer = [pl.ds(0, 16), pl.ds(112, 16)]
    inner = pl.ds(16, 96)
    moves = [(code_ref, cd), (orient_ref, ori)]
    for rows in outer:
        moves += [(src.at[:, rows], dst.at[:, rows]) for src, dst in ((state_ref, st), (adj_ref, ad))]
        moves += [(jac_ref.at[rows], jc.at[rows]), (met_ref.at[0:3, rows], mt.at[0:3, rows])]
    moves += [(src.at[:, inner], dst.at[:, inner]) for src, dst in ((state_ref, st), (adj_ref, ad))]
    moves += [(jac_ref.at[inner], jc.at[inner]), (met_ref.at[3:6], mt.at[3:6])]
    moves += [(met_ref.at[0:3, inner], mt.at[0:3, inner]), (met_ref.at[6:9], mt.at[6:9])]
    loads = [pltpu.make_async_copy(src, dst, load_sem.at[n]) for n, (src, dst) in enumerate(moves)]
    barrier = pltpu.get_barrier_semaphore()
    for side in range(5):
        @pl.when(greets[side])
        def _(side=side):
            pl.semaphore_signal(barrier, inc=1, device_id=ids[side], device_id_type=MESH)

    for copy in loads:
        copy.start()
    for side in range(4):
        @pl.when(jnp.logical_not(inner_side[side]))
        def _(side=side):
            blank = jnp.zeros((8, 128), f32)
            if side < 2:
                for ref, count in ((recv_u, 5), (recv_g, 3), (recv_w, 5)):
                    for n in range(count):
                        for half in range(2):
                            ref[side, n, pl.ds(8 * half, 8)] = blank
                if side == 0:
                    recv_f[...] = jnp.zeros((8, 32), jnp.int32)
            else:
                for n in range(13):
                    recv[place[side], n] = blank

    landing = [1, 0, 3, 2, 4]
    ends = [pl.ds(0, 16), pl.ds(112, 16)]

    def remote(source, target, sent, received, side):
        return pltpu.make_async_remote_copy(
            src_ref=source, dst_ref=target, send_sem=sent, recv_sem=received,
            device_id=ids[side], device_id_type=MESH,
        )

    def x_copy(side, n, source, target):
        return remote(source, target, x_send_sem.at[4 * side + n], x_recv_sem.at[4 * landing[side] + n], side)

    raw_copies, weight_copies = [], []
    for side in range(2):
        to = landing[side]
        raw_copies.append(
            [
                x_copy(side, 0, state_ref.at[:, ends[side]], recv_u.at[to]),
                x_copy(side, 1, met_ref.at[0:3, ends[side]], recv_g.at[to]),
            ]
        )
        weight_copies.append(x_copy(side, 2, send_w.at[side], recv_w.at[to]))
    flag_copy = x_copy(1, 3, orient_ref.at[0:8], recv_f)
    raw_copies[1].insert(0, flag_copy)
    copies = {
        side: remote(
            send.at[place[side]], recv.at[place[landing[side]]],
            send_sem.at[place[side]], recv_sem.at[place[landing[side]]], side,
        )
        for side in (2, 3, 4)
    }

    def on_side(side, act):
        if inner_side[side] is None:
            act()
        else:
            pl.when(inner_side[side])(act)

    def start_raw(side):
        for copy in raw_copies[side]:
            copy.start()

    arrivals = sum(jnp.where(here, 1, 0) for here in greeted)

    @pl.when(arrivals > 0)
    def _():
        pl.semaphore_wait(barrier, arrivals)

    for side in (1, 0):
        pl.when(greeted[side])(lambda side=side: start_raw(side))
    for side in range(5):
        @pl.when(greeted[side])
        def _(side=side):
            pl.semaphore_signal(ready_sem.at[landing[side]], inc=1, device_id=ids[side], device_id_type=MESH)

    sub = lax.broadcasted_iota(jnp.int32, (8, 128), 0)
    lane = lax.broadcasted_iota(jnp.int32, (8, 128), 1)
    sub_flip = sub ^ 3
    lane_flip = lane ^ 48

    def flip_sub(value):
        return jnp.take_along_axis(value, sub_flip, axis=0, mode="promise_in_bounds")

    def flip_lane(value):
        return jnp.take_along_axis(value, lane_flip, axis=1, mode="promise_in_bounds")

    loads[0].wait()
    loads[1].wait()
    el[0:8, :] = cd[...].astype(f32)
    el[8:32, :] = ori[...].astype(f32)
    spread = (
        lax.broadcasted_iota(jnp.int32, (32, 128), 1) // 4 == lax.broadcasted_iota(jnp.int32, (32, 128), 0)
    ).astype(f32)
    wide = jnp.dot(el[...], spread, preferred_element_type=f32)
    xy = lax.broadcasted_iota(jnp.int32, (8, 128), 1)
    spread_xy = ((xy // 64) * 4 + (xy % 16) // 4 == sub).astype(f32)
    contract = (((0,), (0,)), ((), ()))
    code_z = lax.dot_general(el[0:8, :], spread_xy, contract, preferred_element_type=f32)
    flag_z = lax.dot_general(el[24:32, :], spread_xy, contract, preferred_element_type=f32)

    def two_rows(first, second):
        return jnp.where(
            sub < 4,
            jnp.broadcast_to(wide[first : first + 1], (8, 128)),
            jnp.broadcast_to(wide[second : second + 1], (8, 128)),
        )

    def x_rows(base, ex, half):
        return two_rows(base + ex * 4 + 2 * half, base + ex * 4 + 2 * half + 1)

    def y_rows(base, ey):
        return two_rows(base + ey, base + 4 + ey)

    codes = [x_rows(0, 0, 0), x_rows(0, 0, 1), x_rows(0, 1, 0), x_rows(0, 1, 1), y_rows(0, 0), y_rows(0, 3)]
    low_row = sub % 2 == 0
    codes.append(
        jnp.where(
            low_row,
            jnp.broadcast_to(code_z[0:1], (8, 128)),
            jnp.broadcast_to(code_z[31:32], (8, 128)),
        )
    )
    one, zero = jnp.ones((8, 128), f32), jnp.zeros((8, 128), f32)
    at_edge = [jnp.where(e, one, zero) for e in (low_x, low_x, high_x, high_x, low_y, high_y)]
    at_edge.append(jnp.where(low_row, jnp.where(iz == 0, one, zero), jnp.where(iz == 1, one, zero)))
    signs = [-1.5 * one, -1.5 * one, 1.5 * one, 1.5 * one, -1.5 * one, 1.5 * one, jnp.where(low_row, -1.5 * one, 1.5 * one)]
    for slot in range(SLOTS):
        mb[slot, 0] = signs[slot]
        far = at_edge[slot] * codes[slot]
        mb[slot, 1] = far
        mb[slot, 2] = at_edge[slot] - far
    flag_x_mid = [x_rows(8, 0, half) > 0.5 for half in range(2)]
    for half in range(2):
        mb[2 + half, 3] = x_rows(8, 1, half)
    flag_y_mid = [y_rows(16, ey) > 0.5 for ey in range(3)]
    flag_y_top = (y_rows(16, 3) > 0.5) & jnp.logical_not(high_y)
    flag_z_top = (jnp.broadcast_to(flag_z[31:32], (8, 128)) > 0.5) & jnp.logical_not(low_row) & (iz == 0)

    def convert(rows, keep=True):
        rho, m, energy = st[0, rows], [st[n, rows] for n in (1, 2, 3)], st[4, rows]
        r = rcp(rho)
        v = [x * r for x in m]
        pressure = 0.4 * (energy - 0.5 * dot3(m, v))
        beta = (0.5 * rho) * rcp(pressure)
        rj = -rcp(jc[rows])
        w = [ad[n, rows] * rj for n in range(5)]
        w[4] = 0.5 * w[4]
        values = [rho, *v, beta, *node_extras(rho, beta, 0.5 * r, pressure * r), *w]
        if keep:
            for n, value in enumerate(values):
                nb[n, rows] = value
        return values

    for load in loads[2:10]:
        load.wait()

    def pack(slot, values, flag=None, flip=None):
        for n, value in enumerate(values):
            if flag is not None:
                value = jnp.where(flag, flip(value), value)
            send[slot, n] = value

    for slot, block in ((2, 14), (3, 15), (0, 0), (1, 1)):
        values = convert(pl.ds(block * 8, 8))
        for n in range(5):
            send_w[slot // 2, n, pl.ds(8 * (slot % 2), 8)] = values[9 + n]
    for side in (1, 0):
        pl.when(greeted[side])(weight_copies[side].start)

    for load in loads[10:14]:
        load.wait()
    for slot, y, flag in ((0, 0, None), (1, 15, flag_y_top)):
        rows = pl.ds(y, 8, stride=16)
        values = convert(rows, keep=False)
        pack(slot, values[0:5] + values[9:14] + [mt[3 + n, rows] for n in range(3)], flag, flip_sub)
    for side in (2, 3):
        pl.when(greeted[side])(copies[side].start)

    @pl.loop(2, 14)
    def _(block):
        convert(pl.ds(pl.multiple_of(block * 8, 8), 8))

    def load_y(y):
        rows = pl.ds(y, 8, stride=16)
        return [nb[n, rows] for n in range(14)] + [mt[3 + n, rows] for n in range(3)]

    loads[14].wait()

    def load_x(rows):
        return [nb[n, rows] for n in range(14)] + [mt[n, rows] for n in range(3)]

    @pl.loop(0, 4)
    def _(chunk):
        base = (chunk // 2) * 64 + (chunk % 2) * 8

        def at(a):
            return pl.ds(pl.multiple_of(base + a * 16, 8), 8)

        def store(a, total):
            for n in range(5):
                acc[n, at(a)] = total[n]

        line(lambda a: load_x(at(a)), store)

    for side in (2, 3, 1, 0):
        @pl.when(greets[side])
        def _(side=side):
            pl.semaphore_wait(ready_sem.at[side], 1)
            if side < 2:
                start_raw(side)
                weight_copies[side].start()
            else:
                copies[side].start()

    loads[15].wait()
    for n in range(5):
        tb[n, 0:128] = jnp.transpose(nb[n])
        tb[9 + n, 0:128] = jnp.transpose(nb[9 + n])
    for n in range(3):
        tb[14 + n, 0:128] = jnp.transpose(mt[6 + n])
    raw_t = [0, 1, 2, 3, 4, 9, 10, 11, 12, 13, 14, 15, 16]
    low_z = [jnp.broadcast_to(tb[n, 0:1], (8, 128)) for n in raw_t]
    high_z = [jnp.broadcast_to(tb[n, 127:128], (8, 128)) for n in raw_t]
    pack(2, [jnp.where(low_row, x, y) for x, y in zip(low_z, high_z)], flag_z_top, flip_lane)

    @pl.when(greets[4])
    def _():
        pl.semaphore_wait(ready_sem.at[4], 1)

    copies[4].start()

    @pl.loop(0, 16)
    def _(block):
        rows = pl.ds(pl.multiple_of(block * 8, 8), 8)
        rho, beta = tb[0, rows], tb[4, rows]
        for n, value in enumerate(node_extras(rho, beta, 0.5 * rcp(rho), 0.5 * rcp(beta))):
            tb[5 + n, rows] = value

    def add(ref, rows, parts):
        for n in range(5):
            ref[n, rows] = ref[n, rows] + parts[n]

    def flipped(values, flag, flip):
        return [jnp.where(flag, flip(value), value) for value in values]

    for half in range(2):
        lower, upper = pl.ds(48 + 8 * half, 8), pl.ds(64 + 8 * half, 8)
        left = flipped(load_x(lower), flag_x_mid[half], flip_sub)
        to_l, to_u = pair(left, load_x(upper), 1.5, face=True)
        add(acc, lower, flipped(to_l, flag_x_mid[half], flip_sub))
        add(acc, upper, to_u)

    @pl.loop(0, 4)
    def _(chunk):
        def store(a, total):
            add(acc, pl.ds(chunk * 4 + a, 8, stride=16), total)

        line(lambda a: load_y(chunk * 4 + a), store)

    for ey in range(3):
        left = flipped(load_y(4 * ey + 3), flag_y_mid[ey], flip_sub)
        to_l, to_u = pair(left, load_y(4 * ey + 4), 1.5, face=True)
        add(acc, pl.ds(4 * ey + 3, 8, stride=16), flipped(to_l, flag_y_mid[ey], flip_sub))
        add(acc, pl.ds(4 * ey + 4, 8, stride=16), to_u)

    def rows_z(chunk, a):
        return pl.ds(chunk * 32 + a, 8, stride=4)

    def load_z(rows):
        return [tb[n, rows] for n in range(17)]

    @pl.loop(0, 4)
    def _(chunk):
        def store(a, total):
            for n in range(5):
                acct[n, rows_z(chunk, a)] = total[n]

        line(lambda a: load_z(rows_z(chunk, a)), store)

    for chunk in range(4):
        flag = flag_z[8 * chunk : 8 * chunk + 8] > 0.5
        lower = rows_z(chunk, 3)
        left = flipped(load_z(lower), flag, flip_lane)
        upper = rows_z(chunk, 4)
        right = load_z(upper)
        to_l, to_u = pair(left, right, 1.5, face=True)
        to_l = flipped(to_l, flag, flip_lane)
        if chunk == 3:
            inside = sub < 7
            to_l = [jnp.where(inside, x, 0.0) for x in to_l]
            to_u = [jnp.where(inside, x, 0.0) for x in to_u]
        add(acct, lower, to_l)
        add(acct, upper, to_u)

    for side in (4, 2, 3):
        on_side(side, copies[landing[side]].wait_recv)
    for n in range(13):
        recv[2, n] = pltpu.roll(recv[2, n], 1, 0)

    inflow = np.array(INFLOW_STATE)
    inflow_v = inflow[1:4] / inflow[0]
    inflow_p = 0.4 * (inflow[4] - 0.5 * np.sum(inflow[1:4] * inflow_v))
    far_values = [float(inflow[0]), *[float(x) for x in inflow_v], float(inflow[0] / (2.0 * inflow_p))]

    def mirror(v, g, turn):
        along = turn * dot3(v, g)
        return [x - along * y for x, y in zip(v, g)]

    def outer_node(slot, own, prim, normal):
        is_far, is_wall = mb[slot, 1] > 0.5, mb[slot, 2] > 0.5
        outside = is_far | is_wall
        g = own[14:17]
        image = [own[0], *mirror(own[1:4], g, 2.0 * rcp(dot3(g, g))), own[4]]
        prim = [jnp.where(is_far, f, jnp.where(is_wall, i, o)) for f, i, o in zip(far_values, image, prim)]
        normal = [jnp.where(outside, i, o) for i, o in zip(g, normal)]
        extras = node_extras(prim[0], prim[4], 0.5 * rcp(prim[0]), 0.5 * rcp(prim[4]))
        return [*prim, *extras], normal

    def side_faces(slot, own, other, w, normal):
        is_wall = mb[slot, 2] > 0.5
        outside = (mb[slot, 1] > 0.5) | is_wall
        w = [jnp.where(outside, 0.0, x) for x in w]
        mine, theirs = pair(own, [*other, *w, *normal], mb[slot, 0], face=True)
        g = own[14:17]
        back = [theirs[0], *mirror(theirs[1:4], g, 2.0 * rcp(dot3(g, g))), theirs[4]]
        return [x + jnp.where(is_wall, y, 0.0) for x, y in zip(mine, back)]

    @pl.loop(0, 3)
    def _(slot):
        own = [send[slot, n] for n in range(13)]
        other = [recv[slot, n] for n in range(13)]
        extras = node_extras(own[0], own[4], 0.5 * rcp(own[0]), 0.5 * rcp(own[4]))
        own = [*own[0:5], *extras, *own[5:13]]
        prim, normal = outer_node(slot + 4, own, other[0:5], other[10:13])
        for n, part in enumerate(side_faces(slot + 4, own, prim, other[5:10], normal)):
            gout[slot, n] = part

    add(acc, pl.ds(0, 8, stride=16), [gout[0, n] for n in range(5)])
    add(acc, pl.ds(15, 8, stride=16), flipped([gout[1, n] for n in range(5)], flag_y_top, flip_sub))
    for n in range(5):
        part = gout[2, n]
        part = jnp.where(flag_z_top, flip_lane(part), part)
        acct[n, 0:1] = acct[n, 0:1] + part[0:1]
        acct[n, 127:128] = acct[n, 127:128] + part[1:2]

    for n in range(5):
        acc[n] = acc[n] + jnp.transpose(acct[n, 0:128])

    def finish(rows, parts):
        v, beta, r = [nb[n, rows] for n in (1, 2, 3)], nb[4, rows], 2.0 * nb[7, rows]
        d_rho, d_v, d_beta = parts[0], parts[1:4], parts[4]
        db = d_beta * (beta * r)
        d_p = (-0.8 * beta) * db
        out_ref[4, rows] = d_p
        for n in range(3):
            out_ref[1 + n, rows] = d_v[n] * r - d_p * v[n]
        out_ref[0, rows] = d_rho + db - r * dot3(d_v, v) + 0.5 * d_p * dot3(v, v)

    @pl.loop(2, 14)
    def _(block):
        rows = pl.ds(pl.multiple_of(block * 8, 8), 8)
        finish(rows, [acc[n, rows] for n in range(5)])

    def x_rows_of(side, half):
        return pl.ds(side * 112 + half * 8, 8)

    def x_flags(side, half):
        return mb[2 * side + half, 3] > 0.5

    on_side(0, flag_copy.wait_recv)
    el[0:8, :] = recv_f[...].astype(f32)
    below = jnp.dot(el[0:8, :], spread, preferred_element_type=f32)
    for half in range(2):
        mb[half, 3] = jnp.where(
            sub < 4,
            jnp.broadcast_to(below[4 + 2 * half : 5 + 2 * half], (8, 128)),
            jnp.broadcast_to(below[5 + 2 * half : 6 + 2 * half], (8, 128)),
        )

    for side in (1, 0):
        for copy in raw_copies[landing[side]][-2:]:
            on_side(side, copy.wait_recv)
        for half in range(2):
            rows, flag = pl.ds(8 * half, 8), x_flags(side, half)
            u = flipped([recv_u[side, n, rows] for n in range(5)], flag, flip_sub)
            normal = flipped([recv_g[side, n, rows] for n in range(3)], flag, flip_sub)
            prim = primitives(u)
            other, normal = outer_node(2 * side + half, load_x(x_rows_of(side, half)), prim, normal)
            for n, value in enumerate([*other, *normal]):
                xo[2 * side + half, n] = value

    for side in (1, 0):
        on_side(side, weight_copies[landing[side]].wait_recv)
        for half in range(2):
            slot, rows = 2 * side + half, x_rows_of(side, half)
            w = flipped([recv_w[side, n, pl.ds(8 * half, 8)] for n in range(5)], x_flags(side, half), flip_sub)
            other, normal = [xo[slot, n] for n in range(9)], [xo[slot, 9 + n] for n in range(3)]
            parts = side_faces(slot, load_x(rows), other, w, normal)
            finish(rows, [acc[n, rows] + part for n, part in enumerate(parts)])

    for side in (4, 2, 3):
        on_side(side, copies[side].wait_send)
    for side in (1, 0):
        for copy in (*raw_copies[side], weight_copies[side]):
            on_side(side, copy.wait_send)


def solution(mesh):
    nx, ny, nz = mesh.shape["gx"], mesh.shape["gy"], mesh.shape["gz"]
    assert nz == 2

    def body(state, adjoint, metric, jacobian, boundary_kind_code, orient):
        assert state.shape == (5, 8, 16, 128)
        f32 = jnp.float32
        hbm = pl.BlockSpec(memory_space=pltpu.HBM)
        vmem = pltpu.VMEM
        out = pl.pallas_call(
            lambda *refs: kernel(nx, ny, *refs),
            out_shape=jax.ShapeDtypeStruct((5, 128, 128), f32),
            in_specs=[hbm] * 6,
            out_specs=pl.BlockSpec(memory_space=vmem),
            scratch_shapes=[
                vmem((5, 128, 128), f32),
                vmem((5, 128, 128), f32),
                vmem((9, 128, 128), f32),
                vmem((128, 128), f32),
                vmem((8, 32), jnp.int32),
                vmem((24, 32), jnp.int32),
                vmem((14, 128, 128), f32),
                vmem((17, 136, 128), f32),
                vmem((5, 128, 128), f32),
                vmem((5, 136, 128), f32),
                vmem((3, 13, 8, 128), f32),
                vmem((3, 13, 8, 128), f32),
                vmem((3, 5, 8, 128), f32),
                vmem((SLOTS, 4, 8, 128), f32),
                vmem((32, 32), f32),
                vmem((2, 5, 16, 128), f32),
                vmem((2, 5, 16, 128), f32),
                vmem((2, 3, 16, 128), f32),
                vmem((2, 5, 16, 128), f32),
                vmem((8, 32), jnp.int32),
                vmem((4, 12, 8, 128), f32),
                pltpu.SemaphoreType.DMA((16,)),
                pltpu.SemaphoreType.DMA((3,)),
                pltpu.SemaphoreType.DMA((3,)),
                pltpu.SemaphoreType.DMA((8,)),
                pltpu.SemaphoreType.DMA((8,)),
                pltpu.SemaphoreType.REGULAR((5,)),
            ],
            compiler_params=pltpu.CompilerParams(
                collective_id=0, has_side_effects=True, vmem_limit_bytes=32 * 1024 * 1024
            ),
            name="adjoint_residual",
        )(
            *(
                pltpu.with_memory_space_constraint(value, pltpu.HBM)
                for value in (
                    state.reshape(5, 128, 128),
                    adjoint.reshape(5, 128, 128),
                    metric.reshape(9, 128, 128),
                    jacobian.reshape(128, 128),
                    boundary_kind_code.reshape(8, 32),
                    orient.reshape(24, 32),
                )
            )
        )
        return out.reshape(5, 8, 16, 128)

    return jax.shard_map(
        body,
        mesh=mesh,
        in_specs=(
            P(None, "gx", "gy", "gz"),
            P(None, "gx", "gy", "gz"),
            P(None, "gx", "gy", "gz"),
            P("gx", "gy", "gz"),
            P("gx", "gy", "gz"),
            P(None, "gx", "gy", "gz"),
        ),
        out_specs=P(None, "gx", "gy", "gz"),
        check_vma=False,
    )
```

```python
import jax
import jax.numpy as jnp
import numpy as np
from jax import lax
from jax.experimental import pallas as pl
from jax.experimental.pallas import tpu as pltpu
from jax.sharding import PartitionSpec as P

INFLOW_STATE = (1.0, 0.4, 0.0, 0.1, 2.085)
MESH = pl.DeviceIdType.MESH
SLOTS = 7


def lobatto_matrix():
    points = np.array([-1.0, -1.0 / np.sqrt(5.0), 1.0 / np.sqrt(5.0), 1.0])
    weights = np.array(
        [
            1.0 / np.prod([points[place] - points[other] for other in range(4) if other != place])
            for place in range(4)
        ]
    )
    table = np.zeros((4, 4))
    for place in range(4):
        for other in range(4):
            if other != place:
                table[place, other] = (
                    weights[other] / weights[place] / (points[place] - points[other])
                )
        table[place, place] = -np.sum(table[place])
    return table


QUAD = (1.0, 5.0, 5.0, 1.0)
TABLE = lobatto_matrix()


def rcp(value):
    guess = pl.reciprocal(value, approx=True)
    return guess * (2.0 - value * guess)


def dot3(first, second):
    return first[0] * second[0] + first[1] * second[1] + first[2] * second[2]


def log_terms(a, b, log_a, log_b, inv_a, inv_b):
    s = a + b
    rs = rcp(s)
    f = (a - b) * rs
    q = f * f
    small = q < 0.01
    series = 1.0 + q * (1.0 / 3.0 + q * (1.0 / 5.0 + q * (1.0 / 7.0)))
    slope = f * (2.0 / 3.0 + q * (4.0 / 5.0 + q * (6.0 / 7.0)))
    rf = rcp(f)
    logged = (log_a - log_b) * rf
    log_slope = ((s * inv_a) * (s * inv_b) - logged) * rf
    return s, rs, f, jnp.where(small, series, logged), jnp.where(small, slope, log_slope)


def pair(left, right, scale, left_weight=1.0, right_weight=1.0, face=False):
    rho_l, vl, beta_l = left[0], left[1:4], left[4]
    rho_r, vr, beta_r = right[0], right[1:4], right[4]
    wl, wr = left[9:14], right[9:14]
    if left_weight != 1.0:
        wl = [left_weight * w for w in wl]
    if right_weight != 1.0:
        wr = [right_weight * w for w in wr]
    om = [x - y for x, y in zip(wl, wr)]
    o0, ov, oh = om[0], om[1:4], om[4]
    g = [(x + y) * scale for x, y in zip(left[14:17], right[14:17])]
    vs = [x + y for x, y in zip(vl, vr)]
    rho_s, _, rho_f, rho_factor, rho_slope = log_terms(
        rho_l, rho_r, left[5], right[5], left[7], right[7]
    )
    _, beta_i, beta_f, beta_factor, beta_slope = log_terms(
        beta_l, beta_r, left[6], right[6], left[8], right[8]
    )
    p = rcp(rho_factor)
    half_p = 0.5 * p
    mean = rho_s * half_p
    through = dot3(vs, g)
    a = o0 + 0.5 * dot3(ov, vs) + oh * (dot3(vl, vr) + 5.0 * (beta_factor * beta_i))
    b = dot3(ov, g) + oh * through
    ph = rho_s * beta_i
    bi = beta_i * b
    ua = through * a
    k = half_p * (p * rho_slope)
    x = ua * (half_p + k * rho_f) + bi
    y = ua * k
    d_rho_l, d_rho_r = x - y, x + y
    t = mean * through
    e = t * oh
    c = mean * a + ph * oh
    half_t = 0.5 * t
    z = [c * gg + half_t * oo for gg, oo in zip(g, ov)]
    d_v_l = [zz + e * v for zz, v in zip(z, vr)]
    d_v_r = [zz + e * v for zz, v in zip(z, vl)]
    e5 = (-5.0 * e) * (beta_i * beta_i)
    x = e5 * (beta_factor + beta_slope * beta_f) - ph * bi
    y = e5 * beta_slope
    d_beta_l, d_beta_r = x - y, x + y
    if face:
        xl = o0 + dot3(ov, vl) + oh * (10.0 * left[8] * 0.5 + dot3(vl, vl))
        xr = o0 + dot3(ov, vr) + oh * (10.0 * right[8] * 0.5 + dot3(vr, vr))
        kappa = rho_l * xl - rho_r * xr
        n2 = dot3(g, g)
        half_len = 0.5 * jnp.sqrt(n2)
        cl = jnp.sqrt(1.4 * left[8])
        cr = jnp.sqrt(1.4 * right[8])
        sl = dot3(vl, g)
        sr = dot3(vr, g)
        mean_square = 0.5 * (sl * sl + sr * sr)
        rt = lax.rsqrt(mean_square)
        sigma = mean_square * rt + half_len * (cl + cr)
        kr = (0.5 * kappa) * rt
        krl, krr = kr * sl, kr * sr
        ml, mr = sigma * rho_l, sigma * rho_r
        oh2 = 2.0 * oh
        el, er = ml * oh2, mr * oh2
        d_v_l = [d + krl * gg + ml * oo + el * v for d, gg, oo, v in zip(d_v_l, g, ov, vl)]
        d_v_r = [d + krr * gg - mr * oo - er * v for d, gg, oo, v in zip(d_v_r, g, ov, vr)]
        d_rho_l = d_rho_l + sigma * xl
        d_rho_r = d_rho_r - sigma * xr
        kl = kappa * half_len
        d_beta_l = d_beta_l - left[8] * (kl * cl + 5.0 * (el * left[8]))
        d_beta_r = d_beta_r - right[8] * (kl * cr - 5.0 * (er * right[8]))
    return [d_rho_l, *d_v_l, d_beta_l], [d_rho_r, *d_v_r, d_beta_r]


def node_extras(rho, beta, inv_rho, inv_beta):
    return [0.5 * jnp.log(rho), 0.5 * jnp.log(beta), inv_rho, inv_beta]


def primitives(u):
    v = [x * rcp(u[0]) for x in u[1:4]]
    pressure = 0.4 * (u[4] - 0.5 * dot3(u[1:4], v))
    return [u[0], *v, (0.5 * u[0]) * rcp(pressure)]


def line(load, store):
    total = [None] * 4
    for a in range(4):
        for b in range(a + 1, 4):
            factor = 2.0 * QUAD[a] * TABLE[a, b] / 4.0
            wa, wb = 1.0 / QUAD[a], 1.0 / QUAD[b]
            if wa == wb:
                factor, wa, wb = factor * wa, 1.0, 1.0
            first, second = pair(load(a), load(b), float(factor), wa, wb)
            for node, part in ((a, first), (b, second)):
                total[node] = part if total[node] is None else [x + y for x, y in zip(total[node], part)]
    for a in range(4):
        store(a, total[a])


def kernel(
    nx, ny,
    state_ref, adj_ref, met_ref, jac_ref, code_ref, orient_ref, out_ref,
    st, ad, mt, jc, cd, ori, nb, tb, acc, acct, send, recv, gout, mb, el,
    send_w, recv_u, recv_g, recv_w, recv_f, xo,
    load_sem, send_sem, recv_sem, x_send_sem, x_recv_sem, ready_sem,
):
    f32 = jnp.float32
    ix, iy, iz = lax.axis_index("gx"), lax.axis_index("gy"), lax.axis_index("gz")
    low_x, high_x, low_y, high_y = ix == 0, ix == nx - 1, iy == 0, iy == ny - 1
    ids = [
        {"gx": lax.max(ix - 1, 0)}, {"gx": lax.min(ix + 1, nx - 1)},
        {"gy": lax.max(iy - 1, 0)}, {"gy": lax.min(iy + 1, ny - 1)},
        {"gz": 1 - iz},
    ]
    inner_side = [jnp.logical_not(e) for e in (low_x, high_x, low_y, high_y)] + [None]
    opens = [(ix + 3) % 4 < 2, ix % 4 >= 2, (iy + 3) % 4 != 3, iy % 4 == 3, iz == 0]

    def both(first, second):
        return second if first is None else first & second

    greets = [both(there, jnp.logical_not(theirs)) for there, theirs in zip(inner_side, opens)]
    greeted = [both(there, theirs) for there, theirs in zip(inner_side, opens)]
    place = [None, None, 0, 1, 2]

    outer = [pl.ds(0, 16), pl.ds(112, 16)]
    inner = pl.ds(16, 96)
    moves = [(code_ref, cd), (orient_ref, ori)]
    for rows in outer:
        moves += [(src.at[:, rows], dst.at[:, rows]) for src, dst in ((state_ref, st), (adj_ref, ad))]
        moves += [(jac_ref.at[rows], jc.at[rows]), (met_ref.at[0:3, rows], mt.at[0:3, rows])]
    moves += [(src.at[:, inner], dst.at[:, inner]) for src, dst in ((state_ref, st), (adj_ref, ad))]
    moves += [(jac_ref.at[inner], jc.at[inner]), (met_ref.at[3:6], mt.at[3:6])]
    moves += [(met_ref.at[0:3, inner], mt.at[0:3, inner]), (met_ref.at[6:9], mt.at[6:9])]
    loads = [pltpu.make_async_copy(src, dst, load_sem.at[n]) for n, (src, dst) in enumerate(moves)]
    barrier = pltpu.get_barrier_semaphore()
    for side in range(5):
        @pl.when(greets[side])
        def _(side=side):
            pl.semaphore_signal(barrier, inc=1, device_id=ids[side], device_id_type=MESH)

    for copy in loads:
        copy.start()
    for side in range(4):
        @pl.when(jnp.logical_not(inner_side[side]))
        def _(side=side):
            blank = jnp.zeros((8, 128), f32)
            if side < 2:
                for ref, count in ((recv_u, 5), (recv_g, 3), (recv_w, 5)):
                    for n in range(count):
                        for half in range(2):
                            ref[side, n, pl.ds(8 * half, 8)] = blank
                if side == 0:
                    recv_f[...] = jnp.zeros((8, 32), jnp.int32)
            else:
                for n in range(13):
                    recv[place[side], n] = blank

    landing = [1, 0, 3, 2, 4]
    ends = [pl.ds(0, 16), pl.ds(112, 16)]

    def remote(source, target, sent, received, side):
        return pltpu.make_async_remote_copy(
            src_ref=source, dst_ref=target, send_sem=sent, recv_sem=received,
            device_id=ids[side], device_id_type=MESH,
        )

    def x_copy(side, n, source, target):
        return remote(source, target, x_send_sem.at[4 * side + n], x_recv_sem.at[4 * landing[side] + n], side)

    raw_copies, weight_copies = [], []
    for side in range(2):
        to = landing[side]
        raw_copies.append(
            [
                x_copy(side, 0, state_ref.at[:, ends[side]], recv_u.at[to]),
                x_copy(side, 1, met_ref.at[0:3, ends[side]], recv_g.at[to]),
            ]
        )
        weight_copies.append(x_copy(side, 2, send_w.at[side], recv_w.at[to]))
    flag_copy = x_copy(1, 3, orient_ref.at[0:8], recv_f)
    raw_copies[1].insert(0, flag_copy)
    copies = {
        side: remote(
            send.at[place[side]], recv.at[place[landing[side]]],
            send_sem.at[place[side]], recv_sem.at[place[landing[side]]], side,
        )
        for side in (2, 3, 4)
    }

    def on_side(side, act):
        if inner_side[side] is None:
            act()
        else:
            pl.when(inner_side[side])(act)

    def start_raw(side):
        for copy in raw_copies[side]:
            copy.start()

    arrivals = sum(jnp.where(here, 1, 0) for here in greeted)

    @pl.when(arrivals > 0)
    def _():
        pl.semaphore_wait(barrier, arrivals)

    for side in (1, 0):
        pl.when(greeted[side])(lambda side=side: start_raw(side))
    for side in range(5):
        @pl.when(greeted[side])
        def _(side=side):
            pl.semaphore_signal(ready_sem.at[landing[side]], inc=1, device_id=ids[side], device_id_type=MESH)

    sub = lax.broadcasted_iota(jnp.int32, (8, 128), 0)
    lane = lax.broadcasted_iota(jnp.int32, (8, 128), 1)
    sub_flip = sub ^ 3
    lane_flip = lane ^ 48

    def flip_sub(value):
        return jnp.take_along_axis(value, sub_flip, axis=0, mode="promise_in_bounds")

    def flip_lane(value):
        return jnp.take_along_axis(value, lane_flip, axis=1, mode="promise_in_bounds")

    loads[0].wait()
    loads[1].wait()
    el[0:8, :] = cd[...].astype(f32)
    el[8:32, :] = ori[...].astype(f32)
    spread = (
        lax.broadcasted_iota(jnp.int32, (32, 128), 1) // 4 == lax.broadcasted_iota(jnp.int32, (32, 128), 0)
    ).astype(f32)
    wide = jnp.dot(el[...], spread, preferred_element_type=f32)
    xy = lax.broadcasted_iota(jnp.int32, (8, 128), 1)
    spread_xy = ((xy // 64) * 4 + (xy % 16) // 4 == sub).astype(f32)
    contract = (((0,), (0,)), ((), ()))
    code_z = lax.dot_general(el[0:8, :], spread_xy, contract, preferred_element_type=f32)
    flag_z = lax.dot_general(el[24:32, :], spread_xy, contract, preferred_element_type=f32)

    def two_rows(first, second):
        return jnp.where(
            sub < 4,
            jnp.broadcast_to(wide[first : first + 1], (8, 128)),
            jnp.broadcast_to(wide[second : second + 1], (8, 128)),
        )

    def x_rows(base, ex, half):
        return two_rows(base + ex * 4 + 2 * half, base + ex * 4 + 2 * half + 1)

    def y_rows(base, ey):
        return two_rows(base + ey, base + 4 + ey)

    codes = [x_rows(0, 0, 0), x_rows(0, 0, 1), x_rows(0, 1, 0), x_rows(0, 1, 1), y_rows(0, 0), y_rows(0, 3)]
    low_row = sub % 2 == 0
    codes.append(
        jnp.where(
            low_row,
            jnp.broadcast_to(code_z[0:1], (8, 128)),
            jnp.broadcast_to(code_z[31:32], (8, 128)),
        )
    )
    one, zero = jnp.ones((8, 128), f32), jnp.zeros((8, 128), f32)
    at_edge = [jnp.where(e, one, zero) for e in (low_x, low_x, high_x, high_x, low_y, high_y)]
    at_edge.append(jnp.where(low_row, jnp.where(iz == 0, one, zero), jnp.where(iz == 1, one, zero)))
    signs = [-1.5 * one, -1.5 * one, 1.5 * one, 1.5 * one, -1.5 * one, 1.5 * one, jnp.where(low_row, -1.5 * one, 1.5 * one)]
    for slot in range(SLOTS):
        mb[slot, 0] = signs[slot]
        far = at_edge[slot] * codes[slot]
        mb[slot, 1] = far
        mb[slot, 2] = at_edge[slot] - far
    flag_x_mid = [x_rows(8, 0, half) > 0.5 for half in range(2)]
    for half in range(2):
        mb[2 + half, 3] = x_rows(8, 1, half)
    flag_y_mid = [y_rows(16, ey) > 0.5 for ey in range(3)]
    flag_y_top = (y_rows(16, 3) > 0.5) & jnp.logical_not(high_y)
    flag_z_top = (jnp.broadcast_to(flag_z[31:32], (8, 128)) > 0.5) & jnp.logical_not(low_row) & (iz == 0)

    def convert(rows, keep=True):
        rho, m, energy = st[0, rows], [st[n, rows] for n in (1, 2, 3)], st[4, rows]
        r = rcp(rho)
        v = [x * r for x in m]
        pressure = 0.4 * (energy - 0.5 * dot3(m, v))
        beta = (0.5 * rho) * rcp(pressure)
        rj = -rcp(jc[rows])
        w = [ad[n, rows] * rj for n in range(5)]
        w[4] = 0.5 * w[4]
        values = [rho, *v, beta, *node_extras(rho, beta, 0.5 * r, pressure * r), *w]
        if keep:
            for n, value in enumerate(values):
                nb[n, rows] = value
        return values

    for load in loads[2:10]:
        load.wait()

    def pack(slot, values, flag=None, flip=None):
        for n, value in enumerate(values):
            if flag is not None:
                value = jnp.where(flag, flip(value), value)
            send[slot, n] = value

    for slot, block in ((2, 14), (3, 15), (0, 0), (1, 1)):
        values = convert(pl.ds(block * 8, 8))
        for n in range(5):
            send_w[slot // 2, n, pl.ds(8 * (slot % 2), 8)] = values[9 + n]
    for side in (1, 0):
        pl.when(greeted[side])(weight_copies[side].start)

    for load in loads[10:14]:
        load.wait()
    for slot, y, flag in ((0, 0, None), (1, 15, flag_y_top)):
        rows = pl.ds(y, 8, stride=16)
        values = convert(rows, keep=False)
        pack(slot, values[0:5] + values[9:14] + [mt[3 + n, rows] for n in range(3)], flag, flip_sub)
    for side in (2, 3):
        pl.when(greeted[side])(copies[side].start)

    @pl.loop(2, 14)
    def _(block):
        convert(pl.ds(pl.multiple_of(block * 8, 8), 8))

    def load_y(y):
        rows = pl.ds(y, 8, stride=16)
        return [nb[n, rows] for n in range(14)] + [mt[3 + n, rows] for n in range(3)]

    loads[14].wait()

    def load_x(rows):
        return [nb[n, rows] for n in range(14)] + [mt[n, rows] for n in range(3)]

    @pl.loop(0, 4)
    def _(chunk):
        base = (chunk // 2) * 64 + (chunk % 2) * 8

        def at(a):
            return pl.ds(pl.multiple_of(base + a * 16, 8), 8)

        def store(a, total):
            for n in range(5):
                acc[n, at(a)] = total[n]

        line(lambda a: load_x(at(a)), store)

    def answered(side, here):
        @pl.when(greets[side] & here)
        def _():
            pl.semaphore_wait(ready_sem.at[side], 1)
            if side < 2:
                start_raw(side)
                weight_copies[side].start()
            else:
                copies[side].start()

    answered(2, iy >= 0)
    answered(3, iy >= 0)
    answered(0, ix % 4 == 3)

    loads[15].wait()
    for n in range(5):
        tb[n, 0:128] = jnp.transpose(nb[n])
        tb[9 + n, 0:128] = jnp.transpose(nb[9 + n])
    for n in range(3):
        tb[14 + n, 0:128] = jnp.transpose(mt[6 + n])
    raw_t = [0, 1, 2, 3, 4, 9, 10, 11, 12, 13, 14, 15, 16]
    low_z = [jnp.broadcast_to(tb[n, 0:1], (8, 128)) for n in raw_t]
    high_z = [jnp.broadcast_to(tb[n, 127:128], (8, 128)) for n in raw_t]
    pack(2, [jnp.where(low_row, x, y) for x, y in zip(low_z, high_z)], flag_z_top, flip_lane)

    @pl.when(greets[4])
    def _():
        pl.semaphore_wait(ready_sem.at[4], 1)

    copies[4].start()

    @pl.loop(0, 16)
    def _(block):
        rows = pl.ds(pl.multiple_of(block * 8, 8), 8)
        rho, beta = tb[0, rows], tb[4, rows]
        for n, value in enumerate(node_extras(rho, beta, 0.5 * rcp(rho), 0.5 * rcp(beta))):
            tb[5 + n, rows] = value

    def add(ref, rows, parts):
        for n in range(5):
            ref[n, rows] = ref[n, rows] + parts[n]

    def flipped(values, flag, flip):
        return [jnp.where(flag, flip(value), value) for value in values]

    for half in range(2):
        lower, upper = pl.ds(48 + 8 * half, 8), pl.ds(64 + 8 * half, 8)
        left = flipped(load_x(lower), flag_x_mid[half], flip_sub)
        to_l, to_u = pair(left, load_x(upper), 1.5, face=True)
        add(acc, lower, flipped(to_l, flag_x_mid[half], flip_sub))
        add(acc, upper, to_u)

    @pl.loop(0, 4)
    def _(chunk):
        def store(a, total):
            add(acc, pl.ds(chunk * 4 + a, 8, stride=16), total)

        line(lambda a: load_y(chunk * 4 + a), store)

    for ey in range(3):
        left = flipped(load_y(4 * ey + 3), flag_y_mid[ey], flip_sub)
        to_l, to_u = pair(left, load_y(4 * ey + 4), 1.5, face=True)
        add(acc, pl.ds(4 * ey + 3, 8, stride=16), flipped(to_l, flag_y_mid[ey], flip_sub))
        add(acc, pl.ds(4 * ey + 4, 8, stride=16), to_u)

    answered(1, ix % 4 == 0)

    def rows_z(chunk, a):
        return pl.ds(chunk * 32 + a, 8, stride=4)

    def load_z(rows):
        return [tb[n, rows] for n in range(17)]

    @pl.loop(0, 4)
    def _(chunk):
        def store(a, total):
            for n in range(5):
                acct[n, rows_z(chunk, a)] = total[n]

        line(lambda a: load_z(rows_z(chunk, a)), store)

    answered(1, ix % 4 == 1)
    for chunk in range(4):
        flag = flag_z[8 * chunk : 8 * chunk + 8] > 0.5
        lower = rows_z(chunk, 3)
        left = flipped(load_z(lower), flag, flip_lane)
        upper = rows_z(chunk, 4)
        right = load_z(upper)
        to_l, to_u = pair(left, right, 1.5, face=True)
        to_l = flipped(to_l, flag, flip_lane)
        if chunk == 3:
            inside = sub < 7
            to_l = [jnp.where(inside, x, 0.0) for x in to_l]
            to_u = [jnp.where(inside, x, 0.0) for x in to_u]
        add(acct, lower, to_l)
        add(acct, upper, to_u)

    answered(0, ix % 4 == 0)

    for side in (4, 2, 3):
        on_side(side, copies[landing[side]].wait_recv)
    for n in range(13):
        recv[2, n] = pltpu.roll(recv[2, n], 1, 0)

    inflow = np.array(INFLOW_STATE)
    inflow_v = inflow[1:4] / inflow[0]
    inflow_p = 0.4 * (inflow[4] - 0.5 * np.sum(inflow[1:4] * inflow_v))
    far_values = [float(inflow[0]), *[float(x) for x in inflow_v], float(inflow[0] / (2.0 * inflow_p))]

    def mirror(v, g, turn):
        along = turn * dot3(v, g)
        return [x - along * y for x, y in zip(v, g)]

    def outer_node(slot, own, prim, normal):
        is_far, is_wall = mb[slot, 1] > 0.5, mb[slot, 2] > 0.5
        outside = is_far | is_wall
        g = own[14:17]
        image = [own[0], *mirror(own[1:4], g, 2.0 * rcp(dot3(g, g))), own[4]]
        prim = [jnp.where(is_far, f, jnp.where(is_wall, i, o)) for f, i, o in zip(far_values, image, prim)]
        normal = [jnp.where(outside, i, o) for i, o in zip(g, normal)]
        extras = node_extras(prim[0], prim[4], 0.5 * rcp(prim[0]), 0.5 * rcp(prim[4]))
        return [*prim, *extras], normal

    def side_faces(slot, own, other, w, normal):
        is_wall = mb[slot, 2] > 0.5
        outside = (mb[slot, 1] > 0.5) | is_wall
        w = [jnp.where(outside, 0.0, x) for x in w]
        mine, theirs = pair(own, [*other, *w, *normal], mb[slot, 0], face=True)
        g = own[14:17]
        back = [theirs[0], *mirror(theirs[1:4], g, 2.0 * rcp(dot3(g, g))), theirs[4]]
        return [x + jnp.where(is_wall, y, 0.0) for x, y in zip(mine, back)]

    @pl.loop(0, 3)
    def _(slot):
        own = [send[slot, n] for n in range(13)]
        other = [recv[slot, n] for n in range(13)]
        extras = node_extras(own[0], own[4], 0.5 * rcp(own[0]), 0.5 * rcp(own[4]))
        own = [*own[0:5], *extras, *own[5:13]]
        prim, normal = outer_node(slot + 4, own, other[0:5], other[10:13])
        for n, part in enumerate(side_faces(slot + 4, own, prim, other[5:10], normal)):
            gout[slot, n] = part

    add(acc, pl.ds(0, 8, stride=16), [gout[0, n] for n in range(5)])
    add(acc, pl.ds(15, 8, stride=16), flipped([gout[1, n] for n in range(5)], flag_y_top, flip_sub))
    for n in range(5):
        part = gout[2, n]
        part = jnp.where(flag_z_top, flip_lane(part), part)
        acct[n, 0:1] = acct[n, 0:1] + part[0:1]
        acct[n, 127:128] = acct[n, 127:128] + part[1:2]

    for n in range(5):
        acc[n] = acc[n] + jnp.transpose(acct[n, 0:128])

    def finish(rows, parts):
        v, beta, r = [nb[n, rows] for n in (1, 2, 3)], nb[4, rows], 2.0 * nb[7, rows]
        d_rho, d_v, d_beta = parts[0], parts[1:4], parts[4]
        db = d_beta * (beta * r)
        d_p = (-0.8 * beta) * db
        out_ref[4, rows] = d_p
        for n in range(3):
            out_ref[1 + n, rows] = d_v[n] * r - d_p * v[n]
        out_ref[0, rows] = d_rho + db - r * dot3(d_v, v) + 0.5 * d_p * dot3(v, v)

    @pl.loop(2, 14)
    def _(block):
        rows = pl.ds(pl.multiple_of(block * 8, 8), 8)
        finish(rows, [acc[n, rows] for n in range(5)])

    def x_rows_of(side, half):
        return pl.ds(side * 112 + half * 8, 8)

    def x_flags(side, half):
        return mb[2 * side + half, 3] > 0.5

    on_side(0, flag_copy.wait_recv)
    el[0:8, :] = recv_f[...].astype(f32)
    below = jnp.dot(el[0:8, :], spread, preferred_element_type=f32)
    for half in range(2):
        mb[half, 3] = jnp.where(
            sub < 4,
            jnp.broadcast_to(below[4 + 2 * half : 5 + 2 * half], (8, 128)),
            jnp.broadcast_to(below[5 + 2 * half : 6 + 2 * half], (8, 128)),
        )

    for side in (1, 0):
        for copy in raw_copies[landing[side]][-2:]:
            on_side(side, copy.wait_recv)
        for half in range(2):
            rows, flag = pl.ds(8 * half, 8), x_flags(side, half)
            u = flipped([recv_u[side, n, rows] for n in range(5)], flag, flip_sub)
            normal = flipped([recv_g[side, n, rows] for n in range(3)], flag, flip_sub)
            prim = primitives(u)
            other, normal = outer_node(2 * side + half, load_x(x_rows_of(side, half)), prim, normal)
            for n, value in enumerate([*other, *normal]):
                xo[2 * side + half, n] = value

    for side in (1, 0):
        on_side(side, weight_copies[landing[side]].wait_recv)
        for half in range(2):
            slot, rows = 2 * side + half, x_rows_of(side, half)
            w = flipped([recv_w[side, n, pl.ds(8 * half, 8)] for n in range(5)], x_flags(side, half), flip_sub)
            other, normal = [xo[slot, n] for n in range(9)], [xo[slot, 9 + n] for n in range(3)]
            parts = side_faces(slot, load_x(rows), other, w, normal)
            finish(rows, [acc[n, rows] + part for n, part in enumerate(parts)])

    for side in (4, 2, 3):
        on_side(side, copies[side].wait_send)
    for side in (1, 0):
        for copy in (*raw_copies[side], weight_copies[side]):
            on_side(side, copy.wait_send)


def solution(mesh):
    nx, ny, nz = mesh.shape["gx"], mesh.shape["gy"], mesh.shape["gz"]
    assert nz == 2

    def body(state, adjoint, metric, jacobian, boundary_kind_code, orient):
        assert state.shape == (5, 8, 16, 128)
        f32 = jnp.float32
        hbm = pl.BlockSpec(memory_space=pltpu.HBM)
        vmem = pltpu.VMEM
        out = pl.pallas_call(
            lambda *refs: kernel(nx, ny, *refs),
            out_shape=jax.ShapeDtypeStruct((5, 128, 128), f32),
            in_specs=[hbm] * 6,
            out_specs=pl.BlockSpec(memory_space=vmem),
            scratch_shapes=[
                vmem((5, 128, 128), f32),
                vmem((5, 128, 128), f32),
                vmem((9, 128, 128), f32),
                vmem((128, 128), f32),
                vmem((8, 32), jnp.int32),
                vmem((24, 32), jnp.int32),
                vmem((14, 128, 128), f32),
                vmem((17, 136, 128), f32),
                vmem((5, 128, 128), f32),
                vmem((5, 136, 128), f32),
                vmem((3, 13, 8, 128), f32),
                vmem((3, 13, 8, 128), f32),
                vmem((3, 5, 8, 128), f32),
                vmem((SLOTS, 4, 8, 128), f32),
                vmem((32, 32), f32),
                vmem((2, 5, 16, 128), f32),
                vmem((2, 5, 16, 128), f32),
                vmem((2, 3, 16, 128), f32),
                vmem((2, 5, 16, 128), f32),
                vmem((8, 32), jnp.int32),
                vmem((4, 12, 8, 128), f32),
                pltpu.SemaphoreType.DMA((16,)),
                pltpu.SemaphoreType.DMA((3,)),
                pltpu.SemaphoreType.DMA((3,)),
                pltpu.SemaphoreType.DMA((8,)),
                pltpu.SemaphoreType.DMA((8,)),
                pltpu.SemaphoreType.REGULAR((5,)),
            ],
            compiler_params=pltpu.CompilerParams(
                collective_id=0, has_side_effects=True, vmem_limit_bytes=32 * 1024 * 1024
            ),
            name="adjoint_residual",
        )(
            *(
                pltpu.with_memory_space_constraint(value, pltpu.HBM)
                for value in (
                    state.reshape(5, 128, 128),
                    adjoint.reshape(5, 128, 128),
                    metric.reshape(9, 128, 128),
                    jacobian.reshape(128, 128),
                    boundary_kind_code.reshape(8, 32),
                    orient.reshape(24, 32),
                )
            )
        )
        return out.reshape(5, 8, 16, 128)

    return jax.shard_map(
        body,
        mesh=mesh,
        in_specs=(
            P(None, "gx", "gy", "gz"),
            P(None, "gx", "gy", "gz"),
            P(None, "gx", "gy", "gz"),
            P("gx", "gy", "gz"),
            P("gx", "gy", "gz"),
            P(None, "gx", "gy", "gz"),
        ),
        out_specs=P(None, "gx", "gy", "gz"),
        check_vma=False,
    )
```

```python
import jax
import jax.numpy as jnp
import numpy as np
from jax import lax
from jax.experimental import pallas as pl
from jax.experimental.pallas import tpu as pltpu
from jax.sharding import PartitionSpec as P

INFLOW_STATE = (1.0, 0.4, 0.0, 0.1, 2.085)
MESH = pl.DeviceIdType.MESH
SLOTS = 7


def lobatto_matrix():
    points = np.array([-1.0, -1.0 / np.sqrt(5.0), 1.0 / np.sqrt(5.0), 1.0])
    weights = np.array(
        [
            1.0 / np.prod([points[place] - points[other] for other in range(4) if other != place])
            for place in range(4)
        ]
    )
    table = np.zeros((4, 4))
    for place in range(4):
        for other in range(4):
            if other != place:
                table[place, other] = (
                    weights[other] / weights[place] / (points[place] - points[other])
                )
        table[place, place] = -np.sum(table[place])
    return table


QUAD = (1.0, 5.0, 5.0, 1.0)
TABLE = lobatto_matrix()


def rcp(value):
    guess = pl.reciprocal(value, approx=True)
    return guess * (2.0 - value * guess)


def dot3(first, second):
    return first[0] * second[0] + first[1] * second[1] + first[2] * second[2]


def log_terms(a, b, log_a, log_b, inv_a, inv_b):
    s = a + b
    rs = rcp(s)
    f = (a - b) * rs
    q = f * f
    small = q < 0.01
    series = 1.0 + q * (1.0 / 3.0 + q * (1.0 / 5.0 + q * (1.0 / 7.0)))
    slope = f * (2.0 / 3.0 + q * (4.0 / 5.0 + q * (6.0 / 7.0)))
    rf = rcp(f)
    logged = (log_a - log_b) * rf
    log_slope = ((s * inv_a) * (s * inv_b) - logged) * rf
    return s, rs, f, jnp.where(small, series, logged), jnp.where(small, slope, log_slope)


def pair(left, right, scale, left_weight=1.0, right_weight=1.0, face=False):
    rho_l, vl, beta_l = left[0], left[1:4], left[4]
    rho_r, vr, beta_r = right[0], right[1:4], right[4]
    wl, wr = left[9:14], right[9:14]
    if left_weight != 1.0:
        wl = [left_weight * w for w in wl]
    if right_weight != 1.0:
        wr = [right_weight * w for w in wr]
    om = [x - y for x, y in zip(wl, wr)]
    o0, ov, oh = om[0], om[1:4], om[4]
    g = [(x + y) * scale for x, y in zip(left[14:17], right[14:17])]
    vs = [x + y for x, y in zip(vl, vr)]
    rho_s, _, rho_f, rho_factor, rho_slope = log_terms(
        rho_l, rho_r, left[5], right[5], left[7], right[7]
    )
    _, beta_i, beta_f, beta_factor, beta_slope = log_terms(
        beta_l, beta_r, left[6], right[6], left[8], right[8]
    )
    p = rcp(rho_factor)
    half_p = 0.5 * p
    mean = rho_s * half_p
    through = dot3(vs, g)
    a = o0 + 0.5 * dot3(ov, vs) + oh * (dot3(vl, vr) + 5.0 * (beta_factor * beta_i))
    b = dot3(ov, g) + oh * through
    ph = rho_s * beta_i
    bi = beta_i * b
    ua = through * a
    k = half_p * (p * rho_slope)
    x = ua * (half_p + k * rho_f) + bi
    y = ua * k
    d_rho_l, d_rho_r = x - y, x + y
    t = mean * through
    e = t * oh
    c = mean * a + ph * oh
    half_t = 0.5 * t
    z = [c * gg + half_t * oo for gg, oo in zip(g, ov)]
    d_v_l = [zz + e * v for zz, v in zip(z, vr)]
    d_v_r = [zz + e * v for zz, v in zip(z, vl)]
    e5 = (-5.0 * e) * (beta_i * beta_i)
    x = e5 * (beta_factor + beta_slope * beta_f) - ph * bi
    y = e5 * beta_slope
    d_beta_l, d_beta_r = x - y, x + y
    if face:
        xl = o0 + dot3(ov, vl) + oh * (10.0 * left[8] * 0.5 + dot3(vl, vl))
        xr = o0 + dot3(ov, vr) + oh * (10.0 * right[8] * 0.5 + dot3(vr, vr))
        kappa = rho_l * xl - rho_r * xr
        n2 = dot3(g, g)
        half_len = 0.5 * jnp.sqrt(n2)
        cl = jnp.sqrt(1.4 * left[8])
        cr = jnp.sqrt(1.4 * right[8])
        sl = dot3(vl, g)
        sr = dot3(vr, g)
        mean_square = 0.5 * (sl * sl + sr * sr)
        rt = lax.rsqrt(mean_square)
        sigma = mean_square * rt + half_len * (cl + cr)
        kr = (0.5 * kappa) * rt
        krl, krr = kr * sl, kr * sr
        ml, mr = sigma * rho_l, sigma * rho_r
        oh2 = 2.0 * oh
        el, er = ml * oh2, mr * oh2
        d_v_l = [d + krl * gg + ml * oo + el * v for d, gg, oo, v in zip(d_v_l, g, ov, vl)]
        d_v_r = [d + krr * gg - mr * oo - er * v for d, gg, oo, v in zip(d_v_r, g, ov, vr)]
        d_rho_l = d_rho_l + sigma * xl
        d_rho_r = d_rho_r - sigma * xr
        kl = kappa * half_len
        d_beta_l = d_beta_l - left[8] * (kl * cl + 5.0 * (el * left[8]))
        d_beta_r = d_beta_r - right[8] * (kl * cr - 5.0 * (er * right[8]))
    return [d_rho_l, *d_v_l, d_beta_l], [d_rho_r, *d_v_r, d_beta_r]


def node_extras(rho, beta, inv_rho, inv_beta):
    return [0.5 * jnp.log(rho), 0.5 * jnp.log(beta), inv_rho, inv_beta]


def primitives(u):
    v = [x * rcp(u[0]) for x in u[1:4]]
    pressure = 0.4 * (u[4] - 0.5 * dot3(u[1:4], v))
    return [u[0], *v, (0.5 * u[0]) * rcp(pressure)]


def line(load, store):
    total = [None] * 4
    for a in range(4):
        for b in range(a + 1, 4):
            factor = 2.0 * QUAD[a] * TABLE[a, b] / 4.0
            wa, wb = 1.0 / QUAD[a], 1.0 / QUAD[b]
            if wa == wb:
                factor, wa, wb = factor * wa, 1.0, 1.0
            first, second = pair(load(a), load(b), float(factor), wa, wb)
            for node, part in ((a, first), (b, second)):
                total[node] = part if total[node] is None else [x + y for x, y in zip(total[node], part)]
    for a in range(4):
        store(a, total[a])


def kernel(
    nx, ny,
    state_ref, adj_ref, met_ref, jac_ref, code_ref, orient_ref, out_ref,
    st, ad, mt, jc, cd, ori, nb, tb, acc, acct, send, recv, gout, mb, el,
    send_w, recv_u, recv_g, recv_w, recv_f, xo,
    load_sem, send_sem, recv_sem, x_send_sem, x_recv_sem, ready_sem,
):
    f32 = jnp.float32
    ix, iy, iz = lax.axis_index("gx"), lax.axis_index("gy"), lax.axis_index("gz")
    low_x, high_x, low_y, high_y = ix == 0, ix == nx - 1, iy == 0, iy == ny - 1
    ids = [
        {"gx": lax.max(ix - 1, 0)}, {"gx": lax.min(ix + 1, nx - 1)},
        {"gy": lax.max(iy - 1, 0)}, {"gy": lax.min(iy + 1, ny - 1)},
        {"gz": 1 - iz},
    ]
    inner_side = [jnp.logical_not(e) for e in (low_x, high_x, low_y, high_y)] + [None]
    opens = [(ix + 3) % 4 < 2, ix % 4 >= 2, (iy + 3) % 4 != 3, iy % 4 == 3, iz == 0]

    def both(first, second):
        return second if first is None else first & second

    greets = [both(there, jnp.logical_not(theirs)) for there, theirs in zip(inner_side, opens)]
    greeted = [both(there, theirs) for there, theirs in zip(inner_side, opens)]
    place = [None, None, 0, 1, 2]

    outer = [pl.ds(0, 16), pl.ds(112, 16)]
    inner = pl.ds(16, 96)
    moves = [(code_ref, cd), (orient_ref, ori)]
    for rows in outer:
        moves += [(src.at[:, rows], dst.at[:, rows]) for src, dst in ((state_ref, st), (adj_ref, ad))]
        moves += [(jac_ref.at[rows], jc.at[rows]), (met_ref.at[0:3, rows], mt.at[0:3, rows])]
    moves += [(src.at[:, inner], dst.at[:, inner]) for src, dst in ((state_ref, st), (adj_ref, ad))]
    moves += [(jac_ref.at[inner], jc.at[inner]), (met_ref.at[3:6], mt.at[3:6])]
    moves += [(met_ref.at[0:3, inner], mt.at[0:3, inner]), (met_ref.at[6:9], mt.at[6:9])]
    loads = [pltpu.make_async_copy(src, dst, load_sem.at[n]) for n, (src, dst) in enumerate(moves)]
    barrier = pltpu.get_barrier_semaphore()
    for side in range(5):
        @pl.when(greets[side])
        def _(side=side):
            pl.semaphore_signal(barrier, inc=1, device_id=ids[side], device_id_type=MESH)

    for copy in loads:
        copy.start()
    for side in range(4):
        @pl.when(jnp.logical_not(inner_side[side]))
        def _(side=side):
            blank = jnp.zeros((8, 128), f32)
            if side < 2:
                for ref, count in ((recv_u, 5), (recv_g, 3), (recv_w, 5)):
                    for n in range(count):
                        for half in range(2):
                            ref[side, n, pl.ds(8 * half, 8)] = blank
                if side == 0:
                    recv_f[...] = jnp.zeros((8, 32), jnp.int32)
            else:
                for n in range(13):
                    recv[place[side], n] = blank

    landing = [1, 0, 3, 2, 4]
    ends = [pl.ds(0, 16), pl.ds(112, 16)]

    def remote(source, target, sent, received, side):
        return pltpu.make_async_remote_copy(
            src_ref=source, dst_ref=target, send_sem=sent, recv_sem=received,
            device_id=ids[side], device_id_type=MESH,
        )

    def x_copy(side, n, source, target):
        return remote(source, target, x_send_sem.at[4 * side + n], x_recv_sem.at[4 * landing[side] + n], side)

    raw_copies, weight_copies = [], []
    for side in range(2):
        to = landing[side]
        raw_copies.append(
            [
                x_copy(side, 0, state_ref.at[:, ends[side]], recv_u.at[to]),
                x_copy(side, 1, met_ref.at[0:3, ends[side]], recv_g.at[to]),
            ]
        )
        weight_copies.append(x_copy(side, 2, send_w.at[side], recv_w.at[to]))
    flag_copy = x_copy(1, 3, orient_ref.at[0:8], recv_f)
    raw_copies[1].insert(0, flag_copy)
    copies = {
        side: remote(
            send.at[place[side]], recv.at[place[landing[side]]],
            send_sem.at[place[side]], recv_sem.at[place[landing[side]]], side,
        )
        for side in (2, 3, 4)
    }

    def on_side(side, act):
        if inner_side[side] is None:
            act()
        else:
            pl.when(inner_side[side])(act)

    def start_raw(side):
        for copy in raw_copies[side]:
            copy.start()

    arrivals = sum(jnp.where(here, 1, 0) for here in greeted)

    @pl.when(arrivals > 0)
    def _():
        pl.semaphore_wait(barrier, arrivals)

    for side in range(5):
        @pl.when(greeted[side])
        def _(side=side):
            pl.semaphore_signal(ready_sem.at[landing[side]], inc=1, device_id=ids[side], device_id_type=MESH)

    for side in (1, 0):
        pl.when(greeted[side])(lambda side=side: start_raw(side))

    sub = lax.broadcasted_iota(jnp.int32, (8, 128), 0)
    lane = lax.broadcasted_iota(jnp.int32, (8, 128), 1)
    sub_flip = sub ^ 3
    lane_flip = lane ^ 48

    def flip_sub(value):
        return jnp.take_along_axis(value, sub_flip, axis=0, mode="promise_in_bounds")

    def flip_lane(value):
        return jnp.take_along_axis(value, lane_flip, axis=1, mode="promise_in_bounds")

    loads[0].wait()
    loads[1].wait()
    el[0:8, :] = cd[...].astype(f32)
    el[8:32, :] = ori[...].astype(f32)
    spread = (
        lax.broadcasted_iota(jnp.int32, (32, 128), 1) // 4 == lax.broadcasted_iota(jnp.int32, (32, 128), 0)
    ).astype(f32)
    wide = jnp.dot(el[...], spread, preferred_element_type=f32)
    xy = lax.broadcasted_iota(jnp.int32, (8, 128), 1)
    spread_xy = ((xy // 64) * 4 + (xy % 16) // 4 == sub).astype(f32)
    contract = (((0,), (0,)), ((), ()))
    code_z = lax.dot_general(el[0:8, :], spread_xy, contract, preferred_element_type=f32)
    flag_z = lax.dot_general(el[24:32, :], spread_xy, contract, preferred_element_type=f32)

    def two_rows(first, second):
        return jnp.where(
            sub < 4,
            jnp.broadcast_to(wide[first : first + 1], (8, 128)),
            jnp.broadcast_to(wide[second : second + 1], (8, 128)),
        )

    def x_rows(base, ex, half):
        return two_rows(base + ex * 4 + 2 * half, base + ex * 4 + 2 * half + 1)

    def y_rows(base, ey):
        return two_rows(base + ey, base + 4 + ey)

    codes = [x_rows(0, 0, 0), x_rows(0, 0, 1), x_rows(0, 1, 0), x_rows(0, 1, 1), y_rows(0, 0), y_rows(0, 3)]
    low_row = sub % 2 == 0
    codes.append(
        jnp.where(
            low_row,
            jnp.broadcast_to(code_z[0:1], (8, 128)),
            jnp.broadcast_to(code_z[31:32], (8, 128)),
        )
    )
    one, zero = jnp.ones((8, 128), f32), jnp.zeros((8, 128), f32)
    at_edge = [jnp.where(e, one, zero) for e in (low_x, low_x, high_x, high_x, low_y, high_y)]
    at_edge.append(jnp.where(low_row, jnp.where(iz == 0, one, zero), jnp.where(iz == 1, one, zero)))
    signs = [-1.5 * one, -1.5 * one, 1.5 * one, 1.5 * one, -1.5 * one, 1.5 * one, jnp.where(low_row, -1.5 * one, 1.5 * one)]
    for slot in range(SLOTS):
        mb[slot, 0] = signs[slot]
        far = at_edge[slot] * codes[slot]
        mb[slot, 1] = far
        mb[slot, 2] = at_edge[slot] - far
    flag_x_mid = [x_rows(8, 0, half) > 0.5 for half in range(2)]
    for half in range(2):
        mb[2 + half, 3] = x_rows(8, 1, half)
    flag_y_mid = [y_rows(16, ey) > 0.5 for ey in range(3)]
    flag_y_top = (y_rows(16, 3) > 0.5) & jnp.logical_not(high_y)
    flag_z_top = (jnp.broadcast_to(flag_z[31:32], (8, 128)) > 0.5) & jnp.logical_not(low_row) & (iz == 0)

    def convert(rows, keep=True):
        rho, m, energy = st[0, rows], [st[n, rows] for n in (1, 2, 3)], st[4, rows]
        r = rcp(rho)
        v = [x * r for x in m]
        pressure = 0.4 * (energy - 0.5 * dot3(m, v))
        beta = (0.5 * rho) * rcp(pressure)
        rj = -rcp(jc[rows])
        w = [ad[n, rows] * rj for n in range(5)]
        w[4] = 0.5 * w[4]
        values = [rho, *v, beta, *node_extras(rho, beta, 0.5 * r, pressure * r), *w]
        if keep:
            for n, value in enumerate(values):
                nb[n, rows] = value
        return values

    for load in loads[2:10]:
        load.wait()

    def pack(slot, values, flag=None, flip=None):
        for n, value in enumerate(values):
            if flag is not None:
                value = jnp.where(flag, flip(value), value)
            send[slot, n] = value

    for slot, block in ((2, 14), (3, 15), (0, 0), (1, 1)):
        values = convert(pl.ds(block * 8, 8))
        for n in range(5):
            send_w[slot // 2, n, pl.ds(8 * (slot % 2), 8)] = values[9 + n]
    for side in (1, 0):
        pl.when(greeted[side])(weight_copies[side].start)

    for load in loads[10:14]:
        load.wait()
    for slot, y, flag in ((0, 0, None), (1, 15, flag_y_top)):
        rows = pl.ds(y, 8, stride=16)
        values = convert(rows, keep=False)
        pack(slot, values[0:5] + values[9:14] + [mt[3 + n, rows] for n in range(3)], flag, flip_sub)
    for side in (2, 3):
        pl.when(greeted[side])(copies[side].start)

    @pl.loop(2, 14)
    def _(block):
        convert(pl.ds(pl.multiple_of(block * 8, 8), 8))

    def load_y(y):
        rows = pl.ds(y, 8, stride=16)
        return [nb[n, rows] for n in range(14)] + [mt[3 + n, rows] for n in range(3)]

    loads[14].wait()

    def load_x(rows):
        return [nb[n, rows] for n in range(14)] + [mt[n, rows] for n in range(3)]

    @pl.loop(0, 4)
    def _(chunk):
        base = (chunk // 2) * 64 + (chunk % 2) * 8

        def at(a):
            return pl.ds(pl.multiple_of(base + a * 16, 8), 8)

        def store(a, total):
            for n in range(5):
                acc[n, at(a)] = total[n]

        line(lambda a: load_x(at(a)), store)

    def answered(side, here):
        @pl.when(greets[side] & here)
        def _():
            pl.semaphore_wait(ready_sem.at[side], 1)
            if side < 2:
                start_raw(side)
                weight_copies[side].start()
            else:
                copies[side].start()

    answered(2, iy >= 0)
    answered(3, iy >= 0)
    answered(0, ix % 4 == 3)

    loads[15].wait()
    for n in range(5):
        tb[n, 0:128] = jnp.transpose(nb[n])
        tb[9 + n, 0:128] = jnp.transpose(nb[9 + n])
    for n in range(3):
        tb[14 + n, 0:128] = jnp.transpose(mt[6 + n])
    raw_t = [0, 1, 2, 3, 4, 9, 10, 11, 12, 13, 14, 15, 16]
    low_z = [jnp.broadcast_to(tb[n, 0:1], (8, 128)) for n in raw_t]
    high_z = [jnp.broadcast_to(tb[n, 127:128], (8, 128)) for n in raw_t]
    pack(2, [jnp.where(low_row, x, y) for x, y in zip(low_z, high_z)], flag_z_top, flip_lane)

    @pl.when(greets[4])
    def _():
        pl.semaphore_wait(ready_sem.at[4], 1)

    copies[4].start()

    @pl.loop(0, 16)
    def _(block):
        rows = pl.ds(pl.multiple_of(block * 8, 8), 8)
        rho, beta = tb[0, rows], tb[4, rows]
        for n, value in enumerate(node_extras(rho, beta, 0.5 * rcp(rho), 0.5 * rcp(beta))):
            tb[5 + n, rows] = value

    def add(ref, rows, parts):
        for n in range(5):
            ref[n, rows] = ref[n, rows] + parts[n]

    def flipped(values, flag, flip):
        return [jnp.where(flag, flip(value), value) for value in values]

    for half in range(2):
        lower, upper = pl.ds(48 + 8 * half, 8), pl.ds(64 + 8 * half, 8)
        left = flipped(load_x(lower), flag_x_mid[half], flip_sub)
        to_l, to_u = pair(left, load_x(upper), 1.5, face=True)
        add(acc, lower, flipped(to_l, flag_x_mid[half], flip_sub))
        add(acc, upper, to_u)

    @pl.loop(0, 4)
    def _(chunk):
        def store(a, total):
            add(acc, pl.ds(chunk * 4 + a, 8, stride=16), total)

        line(lambda a: load_y(chunk * 4 + a), store)

    for ey in range(3):
        left = flipped(load_y(4 * ey + 3), flag_y_mid[ey], flip_sub)
        to_l, to_u = pair(left, load_y(4 * ey + 4), 1.5, face=True)
        add(acc, pl.ds(4 * ey + 3, 8, stride=16), flipped(to_l, flag_y_mid[ey], flip_sub))
        add(acc, pl.ds(4 * ey + 4, 8, stride=16), to_u)

    answered(1, ix % 4 == 0)

    def rows_z(chunk, a):
        return pl.ds(chunk * 32 + a, 8, stride=4)

    def load_z(rows):
        return [tb[n, rows] for n in range(17)]

    @pl.loop(0, 4)
    def _(chunk):
        def store(a, total):
            for n in range(5):
                acct[n, rows_z(chunk, a)] = total[n]

        line(lambda a: load_z(rows_z(chunk, a)), store)

    answered(1, ix % 4 == 1)
    for chunk in range(4):
        flag = flag_z[8 * chunk : 8 * chunk + 8] > 0.5
        lower = rows_z(chunk, 3)
        left = flipped(load_z(lower), flag, flip_lane)
        upper = rows_z(chunk, 4)
        right = load_z(upper)
        to_l, to_u = pair(left, right, 1.5, face=True)
        to_l = flipped(to_l, flag, flip_lane)
        if chunk == 3:
            inside = sub < 7
            to_l = [jnp.where(inside, x, 0.0) for x in to_l]
            to_u = [jnp.where(inside, x, 0.0) for x in to_u]
        add(acct, lower, to_l)
        add(acct, upper, to_u)

    answered(0, ix % 4 == 0)

    for side in (4, 2, 3):
        on_side(side, copies[landing[side]].wait_recv)
    for n in range(13):
        recv[2, n] = pltpu.roll(recv[2, n], 1, 0)

    inflow = np.array(INFLOW_STATE)
    inflow_v = inflow[1:4] / inflow[0]
    inflow_p = 0.4 * (inflow[4] - 0.5 * np.sum(inflow[1:4] * inflow_v))
    far_values = [float(inflow[0]), *[float(x) for x in inflow_v], float(inflow[0] / (2.0 * inflow_p))]

    def mirror(v, g, turn):
        along = turn * dot3(v, g)
        return [x - along * y for x, y in zip(v, g)]

    def outer_node(slot, own, prim, normal):
        is_far, is_wall = mb[slot, 1] > 0.5, mb[slot, 2] > 0.5
        outside = is_far | is_wall
        g = own[14:17]
        image = [own[0], *mirror(own[1:4], g, 2.0 * rcp(dot3(g, g))), own[4]]
        prim = [jnp.where(is_far, f, jnp.where(is_wall, i, o)) for f, i, o in zip(far_values, image, prim)]
        normal = [jnp.where(outside, i, o) for i, o in zip(g, normal)]
        extras = node_extras(prim[0], prim[4], 0.5 * rcp(prim[0]), 0.5 * rcp(prim[4]))
        return [*prim, *extras], normal

    def side_faces(slot, own, other, w, normal):
        is_wall = mb[slot, 2] > 0.5
        outside = (mb[slot, 1] > 0.5) | is_wall
        w = [jnp.where(outside, 0.0, x) for x in w]
        mine, theirs = pair(own, [*other, *w, *normal], mb[slot, 0], face=True)
        g = own[14:17]
        back = [theirs[0], *mirror(theirs[1:4], g, 2.0 * rcp(dot3(g, g))), theirs[4]]
        return [x + jnp.where(is_wall, y, 0.0) for x, y in zip(mine, back)]

    @pl.loop(0, 3)
    def _(slot):
        own = [send[slot, n] for n in range(13)]
        other = [recv[slot, n] for n in range(13)]
        extras = node_extras(own[0], own[4], 0.5 * rcp(own[0]), 0.5 * rcp(own[4]))
        own = [*own[0:5], *extras, *own[5:13]]
        prim, normal = outer_node(slot + 4, own, other[0:5], other[10:13])
        for n, part in enumerate(side_faces(slot + 4, own, prim, other[5:10], normal)):
            gout[slot, n] = part

    add(acc, pl.ds(0, 8, stride=16), [gout[0, n] for n in range(5)])
    add(acc, pl.ds(15, 8, stride=16), flipped([gout[1, n] for n in range(5)], flag_y_top, flip_sub))
    for n in range(5):
        part = gout[2, n]
        part = jnp.where(flag_z_top, flip_lane(part), part)
        acct[n, 0:1] = acct[n, 0:1] + part[0:1]
        acct[n, 127:128] = acct[n, 127:128] + part[1:2]

    for n in range(5):
        acc[n] = acc[n] + jnp.transpose(acct[n, 0:128])

    def finish(rows, parts):
        v, beta, r = [nb[n, rows] for n in (1, 2, 3)], nb[4, rows], 2.0 * nb[7, rows]
        d_rho, d_v, d_beta = parts[0], parts[1:4], parts[4]
        db = d_beta * (beta * r)
        d_p = (-0.8 * beta) * db
        out_ref[4, rows] = d_p
        for n in range(3):
            out_ref[1 + n, rows] = d_v[n] * r - d_p * v[n]
        out_ref[0, rows] = d_rho + db - r * dot3(d_v, v) + 0.5 * d_p * dot3(v, v)

    @pl.loop(2, 14)
    def _(block):
        rows = pl.ds(pl.multiple_of(block * 8, 8), 8)
        finish(rows, [acc[n, rows] for n in range(5)])

    def x_rows_of(side, half):
        return pl.ds(side * 112 + half * 8, 8)

    def x_flags(side, half):
        return mb[2 * side + half, 3] > 0.5

    on_side(0, flag_copy.wait_recv)
    el[0:8, :] = recv_f[...].astype(f32)
    below = jnp.dot(el[0:8, :], spread, preferred_element_type=f32)
    for half in range(2):
        mb[half, 3] = jnp.where(
            sub < 4,
            jnp.broadcast_to(below[4 + 2 * half : 5 + 2 * half], (8, 128)),
            jnp.broadcast_to(below[5 + 2 * half : 6 + 2 * half], (8, 128)),
        )

    for side in (1, 0):
        for copy in raw_copies[landing[side]][-2:]:
            on_side(side, copy.wait_recv)
        for half in range(2):
            rows, flag = pl.ds(8 * half, 8), x_flags(side, half)
            u = flipped([recv_u[side, n, rows] for n in range(5)], flag, flip_sub)
            normal = flipped([recv_g[side, n, rows] for n in range(3)], flag, flip_sub)
            prim = primitives(u)
            other, normal = outer_node(2 * side + half, load_x(x_rows_of(side, half)), prim, normal)
            for n, value in enumerate([*other, *normal]):
                xo[2 * side + half, n] = value

    for side in (1, 0):
        on_side(side, weight_copies[landing[side]].wait_recv)
        for half in range(2):
            slot, rows = 2 * side + half, x_rows_of(side, half)
            w = flipped([recv_w[side, n, pl.ds(8 * half, 8)] for n in range(5)], x_flags(side, half), flip_sub)
            other, normal = [xo[slot, n] for n in range(9)], [xo[slot, 9 + n] for n in range(3)]
            parts = side_faces(slot, load_x(rows), other, w, normal)
            finish(rows, [acc[n, rows] + part for n, part in enumerate(parts)])

    for side in (4, 2, 3):
        on_side(side, copies[side].wait_send)
    for side in (1, 0):
        for copy in (*raw_copies[side], weight_copies[side]):
            on_side(side, copy.wait_send)


def solution(mesh):
    nx, ny, nz = mesh.shape["gx"], mesh.shape["gy"], mesh.shape["gz"]
    assert nz == 2

    def body(state, adjoint, metric, jacobian, boundary_kind_code, orient):
        assert state.shape == (5, 8, 16, 128)
        f32 = jnp.float32
        hbm = pl.BlockSpec(memory_space=pltpu.HBM)
        vmem = pltpu.VMEM
        out = pl.pallas_call(
            lambda *refs: kernel(nx, ny, *refs),
            out_shape=jax.ShapeDtypeStruct((5, 128, 128), f32),
            in_specs=[hbm] * 6,
            out_specs=pl.BlockSpec(memory_space=vmem),
            scratch_shapes=[
                vmem((5, 128, 128), f32),
                vmem((5, 128, 128), f32),
                vmem((9, 128, 128), f32),
                vmem((128, 128), f32),
                vmem((8, 32), jnp.int32),
                vmem((24, 32), jnp.int32),
                vmem((14, 128, 128), f32),
                vmem((17, 136, 128), f32),
                vmem((5, 128, 128), f32),
                vmem((5, 136, 128), f32),
                vmem((3, 13, 8, 128), f32),
                vmem((3, 13, 8, 128), f32),
                vmem((3, 5, 8, 128), f32),
                vmem((SLOTS, 4, 8, 128), f32),
                vmem((32, 32), f32),
                vmem((2, 5, 16, 128), f32),
                vmem((2, 5, 16, 128), f32),
                vmem((2, 3, 16, 128), f32),
                vmem((2, 5, 16, 128), f32),
                vmem((8, 32), jnp.int32),
                vmem((4, 12, 8, 128), f32),
                pltpu.SemaphoreType.DMA((16,)),
                pltpu.SemaphoreType.DMA((3,)),
                pltpu.SemaphoreType.DMA((3,)),
                pltpu.SemaphoreType.DMA((8,)),
                pltpu.SemaphoreType.DMA((8,)),
                pltpu.SemaphoreType.REGULAR((5,)),
            ],
            compiler_params=pltpu.CompilerParams(
                collective_id=0, has_side_effects=True, vmem_limit_bytes=32 * 1024 * 1024
            ),
            name="adjoint_residual",
        )(
            *(
                pltpu.with_memory_space_constraint(value, pltpu.HBM)
                for value in (
                    state.reshape(5, 128, 128),
                    adjoint.reshape(5, 128, 128),
                    metric.reshape(9, 128, 128),
                    jacobian.reshape(128, 128),
                    boundary_kind_code.reshape(8, 32),
                    orient.reshape(24, 32),
                )
            )
        )
        return out.reshape(5, 8, 16, 128)

    return jax.shard_map(
        body,
        mesh=mesh,
        in_specs=(
            P(None, "gx", "gy", "gz"),
            P(None, "gx", "gy", "gz"),
            P(None, "gx", "gy", "gz"),
            P("gx", "gy", "gz"),
            P("gx", "gy", "gz"),
            P(None, "gx", "gy", "gz"),
        ),
        out_specs=P(None, "gx", "gy", "gz"),
        check_vma=False,
    )
```

```python
import jax
import jax.numpy as jnp
import numpy as np
from jax import lax
from jax.experimental import pallas as pl
from jax.experimental.pallas import tpu as pltpu
from jax.sharding import PartitionSpec as P

INFLOW_STATE = (1.0, 0.4, 0.0, 0.1, 2.085)
MESH = pl.DeviceIdType.MESH
SLOTS = 7


def lobatto_matrix():
    points = np.array([-1.0, -1.0 / np.sqrt(5.0), 1.0 / np.sqrt(5.0), 1.0])
    weights = np.array(
        [
            1.0 / np.prod([points[place] - points[other] for other in range(4) if other != place])
            for place in range(4)
        ]
    )
    table = np.zeros((4, 4))
    for place in range(4):
        for other in range(4):
            if other != place:
                table[place, other] = (
                    weights[other] / weights[place] / (points[place] - points[other])
                )
        table[place, place] = -np.sum(table[place])
    return table


QUAD = (1.0, 5.0, 5.0, 1.0)
TABLE = lobatto_matrix()


def rcp(value):
    guess = pl.reciprocal(value, approx=True)
    return guess * (2.0 - value * guess)


def dot3(first, second):
    return first[0] * second[0] + first[1] * second[1] + first[2] * second[2]


def log_terms(a, b, log_a, log_b, inv_a, inv_b):
    s = a + b
    rs = rcp(s)
    f = (a - b) * rs
    q = f * f
    small = q < 0.01
    series = 1.0 + q * (1.0 / 3.0 + q * (1.0 / 5.0 + q * (1.0 / 7.0)))
    slope = f * (2.0 / 3.0 + q * (4.0 / 5.0 + q * (6.0 / 7.0)))
    rf = rcp(f)
    logged = (log_a - log_b) * rf
    log_slope = ((s * inv_a) * (s * inv_b) - logged) * rf
    return s, rs, f, jnp.where(small, series, logged), jnp.where(small, slope, log_slope)


def pair(left, right, scale, left_weight=1.0, right_weight=1.0, face=False):
    rho_l, vl, beta_l = left[0], left[1:4], left[4]
    rho_r, vr, beta_r = right[0], right[1:4], right[4]
    wl, wr = left[9:14], right[9:14]
    if left_weight != 1.0:
        wl = [left_weight * w for w in wl]
    if right_weight != 1.0:
        wr = [right_weight * w for w in wr]
    om = [x - y for x, y in zip(wl, wr)]
    o0, ov, oh = om[0], om[1:4], om[4]
    g = [(x + y) * scale for x, y in zip(left[14:17], right[14:17])]
    vs = [x + y for x, y in zip(vl, vr)]
    rho_s, _, rho_f, rho_factor, rho_slope = log_terms(
        rho_l, rho_r, left[5], right[5], left[7], right[7]
    )
    _, beta_i, beta_f, beta_factor, beta_slope = log_terms(
        beta_l, beta_r, left[6], right[6], left[8], right[8]
    )
    p = rcp(rho_factor)
    half_p = 0.5 * p
    mean = rho_s * half_p
    through = dot3(vs, g)
    a = o0 + 0.5 * dot3(ov, vs) + oh * (dot3(vl, vr) + 5.0 * (beta_factor * beta_i))
    b = dot3(ov, g) + oh * through
    ph = rho_s * beta_i
    bi = beta_i * b
    ua = through * a
    k = half_p * (p * rho_slope)
    x = ua * (half_p + k * rho_f) + bi
    y = ua * k
    d_rho_l, d_rho_r = x - y, x + y
    t = mean * through
    e = t * oh
    c = mean * a + ph * oh
    half_t = 0.5 * t
    z = [c * gg + half_t * oo for gg, oo in zip(g, ov)]
    d_v_l = [zz + e * v for zz, v in zip(z, vr)]
    d_v_r = [zz + e * v for zz, v in zip(z, vl)]
    e5 = (-5.0 * e) * (beta_i * beta_i)
    x = e5 * (beta_factor + beta_slope * beta_f) - ph * bi
    y = e5 * beta_slope
    d_beta_l, d_beta_r = x - y, x + y
    if face:
        xl = o0 + dot3(ov, vl) + oh * (10.0 * left[8] * 0.5 + dot3(vl, vl))
        xr = o0 + dot3(ov, vr) + oh * (10.0 * right[8] * 0.5 + dot3(vr, vr))
        kappa = rho_l * xl - rho_r * xr
        n2 = dot3(g, g)
        half_len = 0.5 * jnp.sqrt(n2)
        cl = jnp.sqrt(1.4 * left[8])
        cr = jnp.sqrt(1.4 * right[8])
        sl = dot3(vl, g)
        sr = dot3(vr, g)
        mean_square = 0.5 * (sl * sl + sr * sr)
        rt = lax.rsqrt(mean_square)
        sigma = mean_square * rt + half_len * (cl + cr)
        kr = (0.5 * kappa) * rt
        krl, krr = kr * sl, kr * sr
        ml, mr = sigma * rho_l, sigma * rho_r
        oh2 = 2.0 * oh
        el, er = ml * oh2, mr * oh2
        d_v_l = [d + krl * gg + ml * oo + el * v for d, gg, oo, v in zip(d_v_l, g, ov, vl)]
        d_v_r = [d + krr * gg - mr * oo - er * v for d, gg, oo, v in zip(d_v_r, g, ov, vr)]
        d_rho_l = d_rho_l + sigma * xl
        d_rho_r = d_rho_r - sigma * xr
        kl = kappa * half_len
        d_beta_l = d_beta_l - left[8] * (kl * cl + 5.0 * (el * left[8]))
        d_beta_r = d_beta_r - right[8] * (kl * cr - 5.0 * (er * right[8]))
    return [d_rho_l, *d_v_l, d_beta_l], [d_rho_r, *d_v_r, d_beta_r]


def node_extras(rho, beta, inv_rho, inv_beta):
    return [0.5 * jnp.log(rho), 0.5 * jnp.log(beta), inv_rho, inv_beta]


def primitives(u):
    v = [x * rcp(u[0]) for x in u[1:4]]
    pressure = 0.4 * (u[4] - 0.5 * dot3(u[1:4], v))
    return [u[0], *v, (0.5 * u[0]) * rcp(pressure)]


def line(load, store):
    total = [None] * 4
    for a in range(4):
        for b in range(a + 1, 4):
            factor = 2.0 * QUAD[a] * TABLE[a, b] / 4.0
            wa, wb = 1.0 / QUAD[a], 1.0 / QUAD[b]
            if wa == wb:
                factor, wa, wb = factor * wa, 1.0, 1.0
            first, second = pair(load(a), load(b), float(factor), wa, wb)
            for node, part in ((a, first), (b, second)):
                total[node] = part if total[node] is None else [x + y for x, y in zip(total[node], part)]
    for a in range(4):
        store(a, total[a])


def kernel(
    nx, ny,
    state_ref, adj_ref, met_ref, jac_ref, code_ref, orient_ref, out_ref,
    st, ad, mt, jc, cd, ori, nb, tb, acc, acct, send, recv, gout, mb, el,
    send_w, recv_u, recv_g, recv_w, recv_f, xo,
    load_sem, send_sem, recv_sem, x_send_sem, x_recv_sem, ready_sem,
):
    f32 = jnp.float32
    ix, iy, iz = lax.axis_index("gx"), lax.axis_index("gy"), lax.axis_index("gz")
    low_x, high_x, low_y, high_y = ix == 0, ix == nx - 1, iy == 0, iy == ny - 1
    ids = [
        {"gx": lax.max(ix - 1, 0)}, {"gx": lax.min(ix + 1, nx - 1)},
        {"gy": lax.max(iy - 1, 0)}, {"gy": lax.min(iy + 1, ny - 1)},
        {"gz": 1 - iz},
    ]
    inner_side = [jnp.logical_not(e) for e in (low_x, high_x, low_y, high_y)] + [None]
    below, here = (ix + 3) % 4, ix % 4
    first = [below >= 2, here < 2, iy % 4 == 0, iy % 4 != 3]
    tied = [below == 2, here == 2]
    slow = tied[1] & inner_side[1]

    place = [None, None, 0, 1, 2]
    greets = [there & mine for there, mine in zip(inner_side, first)]
    greeted = [there & jnp.logical_not(mine) for there, mine in zip(inner_side, first)]
    early = [greeted[side] & jnp.logical_not(tied[side]) for side in range(2)]

    def count(*flags):
        return sum(jnp.where(flag, 1, 0) for flag in flags)

    outer = [pl.ds(0, 16), pl.ds(112, 16)]
    inner = pl.ds(16, 96)
    moves = [(code_ref, cd), (orient_ref, ori)]
    for rows in outer:
        moves += [(src.at[:, rows], dst.at[:, rows]) for src, dst in ((state_ref, st), (adj_ref, ad))]
        moves += [(jac_ref.at[rows], jc.at[rows]), (met_ref.at[0:3, rows], mt.at[0:3, rows])]
    moves += [(src.at[:, inner], dst.at[:, inner]) for src, dst in ((state_ref, st), (adj_ref, ad))]
    moves += [(jac_ref.at[inner], jc.at[inner]), (met_ref.at[3:6], mt.at[3:6])]
    moves += [(met_ref.at[0:3, inner], mt.at[0:3, inner]), (met_ref.at[6:9], mt.at[6:9])]
    loads = [pltpu.make_async_copy(src, dst, load_sem.at[n]) for n, (src, dst) in enumerate(moves)]
    barrier = pltpu.get_barrier_semaphore()
    def signal(semaphore, target):
        pl.semaphore_signal(semaphore, inc=1, device_id=target, device_id_type=MESH)

    for side in range(4):
        @pl.when(greets[side])
        def _(side=side):
            signal(barrier, {**ids[side], "gz": jnp.where(tied[side], 0, 1) if side < 2 else 0})

    for copy in loads:
        copy.start()
    for side in range(4):
        @pl.when(jnp.logical_not(inner_side[side]))
        def _(side=side):
            blank = jnp.zeros((8, 128), f32)
            if side < 2:
                for ref, count in ((recv_u, 5), (recv_g, 3), (recv_w, 5)):
                    for n in range(count):
                        for half in range(2):
                            ref[side, n, pl.ds(8 * half, 8)] = blank
                if side == 0:
                    recv_f[...] = jnp.zeros((8, 32), jnp.int32)
            else:
                for n in range(13):
                    recv[place[side], n] = blank

    landing = [1, 0, 3, 2, 4]
    ends = [pl.ds(0, 16), pl.ds(112, 16)]

    def remote(source, target, sent, received, side):
        return pltpu.make_async_remote_copy(
            src_ref=source, dst_ref=target, send_sem=sent, recv_sem=received,
            device_id=ids[side], device_id_type=MESH,
        )

    def x_copy(side, n, source, target):
        return remote(source, target, x_send_sem.at[4 * side + n], x_recv_sem.at[4 * landing[side] + n], side)

    raw_copies, weight_copies = [], []
    for side in range(2):
        to = landing[side]
        raw_copies.append(
            [
                x_copy(side, 0, state_ref.at[:, ends[side]], recv_u.at[to]),
                x_copy(side, 1, met_ref.at[0:3, ends[side]], recv_g.at[to]),
            ]
        )
        weight_copies.append(x_copy(side, 2, send_w.at[side], recv_w.at[to]))
    flag_copy = x_copy(1, 3, orient_ref.at[0:8], recv_f)
    raw_copies[1].insert(0, flag_copy)
    copies = {
        side: remote(
            send.at[place[side]], recv.at[place[landing[side]]],
            send_sem.at[place[side]], recv_sem.at[place[landing[side]]], side,
        )
        for side in (2, 3, 4)
    }

    def on_side(side, act):
        if inner_side[side] is None:
            act()
        else:
            pl.when(inner_side[side])(act)

    def start_raw(side):
        for copy in raw_copies[side]:
            copy.start()

    def answer(side, core):
        signal(ready_sem.at[landing[side]], {**ids[side], "gz": core})

    @pl.when(iz == 1)
    def _():
        @pl.when(early[0] | early[1])
        def _():
            pl.semaphore_wait(barrier, 2 * count(early[0], early[1]))

        signal(barrier, {"gz": 0})
        for side in (1, 0):
            @pl.when(early[side])
            def _(side=side):
                answer(side, 1)
                start_raw(side)

    def meet():
        pl.semaphore_wait(barrier, 2 * count(slow, greeted[2], greeted[3]) + 1)
        for side in (1, 0):
            @pl.when(early[side])
            def _(side=side):
                answer(side, 0)

        signal(ready_sem.at[4], {"gz": 1})
        for side in (1, 2, 3):
            @pl.when(slow if side == 1 else greeted[side])
            def _(side=side):
                answer(side, 0)
                answer(side, 1)

    @pl.when((iz == 0) & jnp.logical_not(slow))
    def _():
        meet()
        for side in (1, 0):
            pl.when(early[side])(lambda side=side: start_raw(side))

    sub = lax.broadcasted_iota(jnp.int32, (8, 128), 0)
    lane = lax.broadcasted_iota(jnp.int32, (8, 128), 1)
    sub_flip = sub ^ 3
    lane_flip = lane ^ 48

    def flip_sub(value):
        return jnp.take_along_axis(value, sub_flip, axis=0, mode="promise_in_bounds")

    def flip_lane(value):
        return jnp.take_along_axis(value, lane_flip, axis=1, mode="promise_in_bounds")

    loads[0].wait()
    loads[1].wait()
    el[0:8, :] = cd[...].astype(f32)
    el[8:32, :] = ori[...].astype(f32)
    spread = (
        lax.broadcasted_iota(jnp.int32, (32, 128), 1) // 4 == lax.broadcasted_iota(jnp.int32, (32, 128), 0)
    ).astype(f32)
    wide = jnp.dot(el[...], spread, preferred_element_type=f32)
    xy = lax.broadcasted_iota(jnp.int32, (8, 128), 1)
    spread_xy = ((xy // 64) * 4 + (xy % 16) // 4 == sub).astype(f32)
    contract = (((0,), (0,)), ((), ()))
    code_z = lax.dot_general(el[0:8, :], spread_xy, contract, preferred_element_type=f32)
    flag_z = lax.dot_general(el[24:32, :], spread_xy, contract, preferred_element_type=f32)

    def two_rows(first, second):
        return jnp.where(
            sub < 4,
            jnp.broadcast_to(wide[first : first + 1], (8, 128)),
            jnp.broadcast_to(wide[second : second + 1], (8, 128)),
        )

    def x_rows(base, ex, half):
        return two_rows(base + ex * 4 + 2 * half, base + ex * 4 + 2 * half + 1)

    def y_rows(base, ey):
        return two_rows(base + ey, base + 4 + ey)

    codes = [x_rows(0, 0, 0), x_rows(0, 0, 1), x_rows(0, 1, 0), x_rows(0, 1, 1), y_rows(0, 0), y_rows(0, 3)]
    low_row = sub % 2 == 0
    codes.append(
        jnp.where(
            low_row,
            jnp.broadcast_to(code_z[0:1], (8, 128)),
            jnp.broadcast_to(code_z[31:32], (8, 128)),
        )
    )
    one, zero = jnp.ones((8, 128), f32), jnp.zeros((8, 128), f32)
    at_edge = [jnp.where(e, one, zero) for e in (low_x, low_x, high_x, high_x, low_y, high_y)]
    at_edge.append(jnp.where(low_row, jnp.where(iz == 0, one, zero), jnp.where(iz == 1, one, zero)))
    signs = [-1.5 * one, -1.5 * one, 1.5 * one, 1.5 * one, -1.5 * one, 1.5 * one, jnp.where(low_row, -1.5 * one, 1.5 * one)]
    for slot in range(SLOTS):
        mb[slot, 0] = signs[slot]
        far = at_edge[slot] * codes[slot]
        mb[slot, 1] = far
        mb[slot, 2] = at_edge[slot] - far
    flag_x_mid = [x_rows(8, 0, half) > 0.5 for half in range(2)]
    for half in range(2):
        mb[2 + half, 3] = x_rows(8, 1, half)
    flag_y_mid = [y_rows(16, ey) > 0.5 for ey in range(3)]
    flag_y_top = (y_rows(16, 3) > 0.5) & jnp.logical_not(high_y)
    flag_z_top = (jnp.broadcast_to(flag_z[31:32], (8, 128)) > 0.5) & jnp.logical_not(low_row) & (iz == 0)

    def convert(rows, keep=True):
        rho, m, energy = st[0, rows], [st[n, rows] for n in (1, 2, 3)], st[4, rows]
        r = rcp(rho)
        v = [x * r for x in m]
        pressure = 0.4 * (energy - 0.5 * dot3(m, v))
        beta = (0.5 * rho) * rcp(pressure)
        rj = -rcp(jc[rows])
        w = [ad[n, rows] * rj for n in range(5)]
        w[4] = 0.5 * w[4]
        values = [rho, *v, beta, *node_extras(rho, beta, 0.5 * r, pressure * r), *w]
        if keep:
            for n, value in enumerate(values):
                nb[n, rows] = value
        return values

    for load in loads[2:10]:
        load.wait()

    def pack(slot, values, flag=None, flip=None):
        for n, value in enumerate(values):
            if flag is not None:
                value = jnp.where(flag, flip(value), value)
            send[slot, n] = value

    for slot, block in ((2, 14), (3, 15), (0, 0), (1, 1)):
        values = convert(pl.ds(block * 8, 8))
        for n in range(5):
            send_w[slot // 2, n, pl.ds(8 * (slot % 2), 8)] = values[9 + n]
    prompt = (iz == 1) | jnp.logical_not(slow)
    for side in (1, 0):
        pl.when(early[side] & prompt)(weight_copies[side].start)

    for load in loads[10:14]:
        load.wait()
    for slot, y, flag in ((0, 0, None), (1, 15, flag_y_top)):
        rows = pl.ds(y, 8, stride=16)
        values = convert(rows, keep=False)
        pack(slot, values[0:5] + values[9:14] + [mt[3 + n, rows] for n in range(3)], flag, flip_sub)

    for side in (2, 3):
        pl.when(greeted[side] & (iz == 0) & prompt)(copies[side].start)

    @pl.loop(2, 14)
    def _(block):
        convert(pl.ds(pl.multiple_of(block * 8, 8), 8))

    def load_y(y):
        rows = pl.ds(y, 8, stride=16)
        return [nb[n, rows] for n in range(14)] + [mt[3 + n, rows] for n in range(3)]

    loads[14].wait()

    def load_x(rows):
        return [nb[n, rows] for n in range(14)] + [mt[n, rows] for n in range(3)]

    @pl.loop(0, 4)
    def _(chunk):
        base = (chunk // 2) * 64 + (chunk % 2) * 8

        def at(a):
            return pl.ds(pl.multiple_of(base + a * 16, 8), 8)

        def store(a, total):
            for n in range(5):
                acc[n, at(a)] = total[n]

        line(lambda a: load_x(at(a)), store)

    def answered(side, here):
        @pl.when(greets[side] & here)
        def _():
            pl.semaphore_wait(ready_sem.at[side], 1)
            if side < 2:
                start_raw(side)
                weight_copies[side].start()
            else:
                copies[side].start()

    @pl.when(iz == 1)
    def _():
        pl.semaphore_wait(ready_sem.at[4], 1)

    pl.when(jnp.logical_not(prompt))(meet)
    for side in (2, 3):
        pl.when(greeted[side] & ((iz == 1) | jnp.logical_not(prompt)))(copies[side].start)
    for side in (1, 0):
        @pl.when(early[side] & jnp.logical_not(prompt))
        def _(side=side):
            start_raw(side)
            weight_copies[side].start()

    @pl.when(slow)
    def _():
        start_raw(1)
        weight_copies[1].start()

    answered(0, here == 3)

    loads[15].wait()
    for n in range(5):
        tb[n, 0:128] = jnp.transpose(nb[n])
        tb[9 + n, 0:128] = jnp.transpose(nb[9 + n])
    for n in range(3):
        tb[14 + n, 0:128] = jnp.transpose(mt[6 + n])
    raw_t = [0, 1, 2, 3, 4, 9, 10, 11, 12, 13, 14, 15, 16]
    low_z = [jnp.broadcast_to(tb[n, 0:1], (8, 128)) for n in raw_t]
    high_z = [jnp.broadcast_to(tb[n, 127:128], (8, 128)) for n in raw_t]
    pack(2, [jnp.where(low_row, x, y) for x, y in zip(low_z, high_z)], flag_z_top, flip_lane)
    copies[4].start()
    answered(3, here != 2)

    @pl.loop(0, 16)
    def _(block):
        rows = pl.ds(pl.multiple_of(block * 8, 8), 8)
        rho, beta = tb[0, rows], tb[4, rows]
        for n, value in enumerate(node_extras(rho, beta, 0.5 * rcp(rho), 0.5 * rcp(beta))):
            tb[5 + n, rows] = value

    def add(ref, rows, parts):
        for n in range(5):
            ref[n, rows] = ref[n, rows] + parts[n]

    def flipped(values, flag, flip):
        return [jnp.where(flag, flip(value), value) for value in values]

    for half in range(2):
        lower, upper = pl.ds(48 + 8 * half, 8), pl.ds(64 + 8 * half, 8)
        left = flipped(load_x(lower), flag_x_mid[half], flip_sub)
        to_l, to_u = pair(left, load_x(upper), 1.5, face=True)
        add(acc, lower, flipped(to_l, flag_x_mid[half], flip_sub))
        add(acc, upper, to_u)

    @pl.loop(0, 4)
    def _(chunk):
        def store(a, total):
            add(acc, pl.ds(chunk * 4 + a, 8, stride=16), total)

        line(lambda a: load_y(chunk * 4 + a), store)

    for ey in range(3):
        left = flipped(load_y(4 * ey + 3), flag_y_mid[ey], flip_sub)
        to_l, to_u = pair(left, load_y(4 * ey + 4), 1.5, face=True)
        add(acc, pl.ds(4 * ey + 3, 8, stride=16), flipped(to_l, flag_y_mid[ey], flip_sub))
        add(acc, pl.ds(4 * ey + 4, 8, stride=16), to_u)

    answered(3, here == 2)
    answered(2, iy >= 0)
    answered(1, here == 0)

    def rows_z(chunk, a):
        return pl.ds(chunk * 32 + a, 8, stride=4)

    def load_z(rows):
        return [tb[n, rows] for n in range(17)]

    @pl.loop(0, 4)
    def _(chunk):
        def store(a, total):
            for n in range(5):
                acct[n, rows_z(chunk, a)] = total[n]

        line(lambda a: load_z(rows_z(chunk, a)), store)

    answered(1, here == 1)
    for chunk in range(4):
        flag = flag_z[8 * chunk : 8 * chunk + 8] > 0.5
        lower = rows_z(chunk, 3)
        left = flipped(load_z(lower), flag, flip_lane)
        upper = rows_z(chunk, 4)
        right = load_z(upper)
        to_l, to_u = pair(left, right, 1.5, face=True)
        to_l = flipped(to_l, flag, flip_lane)
        if chunk == 3:
            inside = sub < 7
            to_l = [jnp.where(inside, x, 0.0) for x in to_l]
            to_u = [jnp.where(inside, x, 0.0) for x in to_u]
        add(acct, lower, to_l)
        add(acct, upper, to_u)

    answered(0, here == 0)

    for side in (4, 2, 3):
        on_side(side, copies[landing[side]].wait_recv)
    for n in range(13):
        recv[2, n] = pltpu.roll(recv[2, n], 1, 0)

    inflow = np.array(INFLOW_STATE)
    inflow_v = inflow[1:4] / inflow[0]
    inflow_p = 0.4 * (inflow[4] - 0.5 * np.sum(inflow[1:4] * inflow_v))
    far_values = [float(inflow[0]), *[float(x) for x in inflow_v], float(inflow[0] / (2.0 * inflow_p))]

    def mirror(v, g, turn):
        along = turn * dot3(v, g)
        return [x - along * y for x, y in zip(v, g)]

    def outer_node(slot, own, prim, normal):
        is_far, is_wall = mb[slot, 1] > 0.5, mb[slot, 2] > 0.5
        outside = is_far | is_wall
        g = own[14:17]
        image = [own[0], *mirror(own[1:4], g, 2.0 * rcp(dot3(g, g))), own[4]]
        prim = [jnp.where(is_far, f, jnp.where(is_wall, i, o)) for f, i, o in zip(far_values, image, prim)]
        normal = [jnp.where(outside, i, o) for i, o in zip(g, normal)]
        extras = node_extras(prim[0], prim[4], 0.5 * rcp(prim[0]), 0.5 * rcp(prim[4]))
        return [*prim, *extras], normal

    def side_faces(slot, own, other, w, normal):
        is_wall = mb[slot, 2] > 0.5
        outside = (mb[slot, 1] > 0.5) | is_wall
        w = [jnp.where(outside, 0.0, x) for x in w]
        mine, theirs = pair(own, [*other, *w, *normal], mb[slot, 0], face=True)
        g = own[14:17]
        back = [theirs[0], *mirror(theirs[1:4], g, 2.0 * rcp(dot3(g, g))), theirs[4]]
        return [x + jnp.where(is_wall, y, 0.0) for x, y in zip(mine, back)]

    @pl.loop(0, 3)
    def _(slot):
        own = [send[slot, n] for n in range(13)]
        other = [recv[slot, n] for n in range(13)]
        extras = node_extras(own[0], own[4], 0.5 * rcp(own[0]), 0.5 * rcp(own[4]))
        own = [*own[0:5], *extras, *own[5:13]]
        prim, normal = outer_node(slot + 4, own, other[0:5], other[10:13])
        for n, part in enumerate(side_faces(slot + 4, own, prim, other[5:10], normal)):
            gout[slot, n] = part

    add(acc, pl.ds(0, 8, stride=16), [gout[0, n] for n in range(5)])
    add(acc, pl.ds(15, 8, stride=16), flipped([gout[1, n] for n in range(5)], flag_y_top, flip_sub))
    for n in range(5):
        part = gout[2, n]
        part = jnp.where(flag_z_top, flip_lane(part), part)
        acct[n, 0:1] = acct[n, 0:1] + part[0:1]
        acct[n, 127:128] = acct[n, 127:128] + part[1:2]

    for n in range(5):
        acc[n] = acc[n] + jnp.transpose(acct[n, 0:128])

    def finish(rows, parts):
        v, beta, r = [nb[n, rows] for n in (1, 2, 3)], nb[4, rows], 2.0 * nb[7, rows]
        d_rho, d_v, d_beta = parts[0], parts[1:4], parts[4]
        db = d_beta * (beta * r)
        d_p = (-0.8 * beta) * db
        out_ref[4, rows] = d_p
        for n in range(3):
            out_ref[1 + n, rows] = d_v[n] * r - d_p * v[n]
        out_ref[0, rows] = d_rho + db - r * dot3(d_v, v) + 0.5 * d_p * dot3(v, v)

    @pl.loop(2, 14)
    def _(block):
        rows = pl.ds(pl.multiple_of(block * 8, 8), 8)
        finish(rows, [acc[n, rows] for n in range(5)])

    def x_rows_of(side, half):
        return pl.ds(side * 112 + half * 8, 8)

    def x_flags(side, half):
        return mb[2 * side + half, 3] > 0.5

    on_side(0, flag_copy.wait_recv)
    el[0:8, :] = recv_f[...].astype(f32)
    below_flags = jnp.dot(el[0:8, :], spread, preferred_element_type=f32)
    for half in range(2):
        mb[half, 3] = jnp.where(
            sub < 4,
            jnp.broadcast_to(below_flags[4 + 2 * half : 5 + 2 * half], (8, 128)),
            jnp.broadcast_to(below_flags[5 + 2 * half : 6 + 2 * half], (8, 128)),
        )

    for side in (1, 0):
        for copy in raw_copies[landing[side]][-2:]:
            on_side(side, copy.wait_recv)
        for half in range(2):
            rows, flag = pl.ds(8 * half, 8), x_flags(side, half)
            u = flipped([recv_u[side, n, rows] for n in range(5)], flag, flip_sub)
            normal = flipped([recv_g[side, n, rows] for n in range(3)], flag, flip_sub)
            prim = primitives(u)
            other, normal = outer_node(2 * side + half, load_x(x_rows_of(side, half)), prim, normal)
            for n, value in enumerate([*other, *normal]):
                xo[2 * side + half, n] = value

    for side in (1, 0):
        on_side(side, weight_copies[landing[side]].wait_recv)
        for half in range(2):
            slot, rows = 2 * side + half, x_rows_of(side, half)
            w = flipped([recv_w[side, n, pl.ds(8 * half, 8)] for n in range(5)], x_flags(side, half), flip_sub)
            other, normal = [xo[slot, n] for n in range(9)], [xo[slot, 9 + n] for n in range(3)]
            parts = side_faces(slot, load_x(rows), other, w, normal)
            finish(rows, [acc[n, rows] + part for n, part in enumerate(parts)])

    for side in (4, 2, 3):
        on_side(side, copies[side].wait_send)
    for side in (1, 0):
        for copy in (*raw_copies[side], weight_copies[side]):
            on_side(side, copy.wait_send)


def solution(mesh):
    nx, ny, nz = mesh.shape["gx"], mesh.shape["gy"], mesh.shape["gz"]
    assert nz == 2

    def body(state, adjoint, metric, jacobian, boundary_kind_code, orient):
        assert state.shape == (5, 8, 16, 128)
        f32 = jnp.float32
        hbm = pl.BlockSpec(memory_space=pltpu.HBM)
        vmem = pltpu.VMEM
        out = pl.pallas_call(
            lambda *refs: kernel(nx, ny, *refs),
            out_shape=jax.ShapeDtypeStruct((5, 128, 128), f32),
            in_specs=[hbm] * 6,
            out_specs=pl.BlockSpec(memory_space=vmem),
            scratch_shapes=[
                vmem((5, 128, 128), f32),
                vmem((5, 128, 128), f32),
                vmem((9, 128, 128), f32),
                vmem((128, 128), f32),
                vmem((8, 32), jnp.int32),
                vmem((24, 32), jnp.int32),
                vmem((14, 128, 128), f32),
                vmem((17, 136, 128), f32),
                vmem((5, 128, 128), f32),
                vmem((5, 136, 128), f32),
                vmem((3, 13, 8, 128), f32),
                vmem((3, 13, 8, 128), f32),
                vmem((3, 5, 8, 128), f32),
                vmem((SLOTS, 4, 8, 128), f32),
                vmem((32, 32), f32),
                vmem((2, 5, 16, 128), f32),
                vmem((2, 5, 16, 128), f32),
                vmem((2, 3, 16, 128), f32),
                vmem((2, 5, 16, 128), f32),
                vmem((8, 32), jnp.int32),
                vmem((4, 12, 8, 128), f32),
                pltpu.SemaphoreType.DMA((16,)),
                pltpu.SemaphoreType.DMA((3,)),
                pltpu.SemaphoreType.DMA((3,)),
                pltpu.SemaphoreType.DMA((8,)),
                pltpu.SemaphoreType.DMA((8,)),
                pltpu.SemaphoreType.REGULAR((5,)),
            ],
            compiler_params=pltpu.CompilerParams(
                collective_id=0, has_side_effects=True, vmem_limit_bytes=32 * 1024 * 1024
            ),
            name="adjoint_residual",
        )(
            *(
                pltpu.with_memory_space_constraint(value, pltpu.HBM)
                for value in (
                    state.reshape(5, 128, 128),
                    adjoint.reshape(5, 128, 128),
                    metric.reshape(9, 128, 128),
                    jacobian.reshape(128, 128),
                    boundary_kind_code.reshape(8, 32),
                    orient.reshape(24, 32),
                )
            )
        )
        return out.reshape(5, 8, 16, 128)

    return jax.shard_map(
        body,
        mesh=mesh,
        in_specs=(
            P(None, "gx", "gy", "gz"),
            P(None, "gx", "gy", "gz"),
            P(None, "gx", "gy", "gz"),
            P("gx", "gy", "gz"),
            P("gx", "gy", "gz"),
            P(None, "gx", "gy", "gz"),
        ),
        out_specs=P(None, "gx", "gy", "gz"),
        check_vma=False,
    )
```

```python
import jax
import jax.numpy as jnp
import numpy as np
from jax import lax
from jax.experimental import pallas as pl
from jax.experimental.pallas import tpu as pltpu
from jax.sharding import PartitionSpec as P

INFLOW_STATE = (1.0, 0.4, 0.0, 0.1, 2.085)
MESH = pl.DeviceIdType.MESH
SLOTS = 7


def lobatto_matrix():
    points = np.array([-1.0, -1.0 / np.sqrt(5.0), 1.0 / np.sqrt(5.0), 1.0])
    weights = np.array(
        [
            1.0 / np.prod([points[place] - points[other] for other in range(4) if other != place])
            for place in range(4)
        ]
    )
    table = np.zeros((4, 4))
    for place in range(4):
        for other in range(4):
            if other != place:
                table[place, other] = (
                    weights[other] / weights[place] / (points[place] - points[other])
                )
        table[place, place] = -np.sum(table[place])
    return table


QUAD = (1.0, 5.0, 5.0, 1.0)
TABLE = lobatto_matrix()


def rcp(value):
    guess = pl.reciprocal(value, approx=True)
    return guess * (2.0 - value * guess)


def dot3(first, second):
    return first[0] * second[0] + first[1] * second[1] + first[2] * second[2]


def log_terms(a, b, log_a, log_b, inv_a, inv_b):
    s = a + b
    rs = rcp(s)
    f = (a - b) * rs
    q = f * f
    small = q < 0.01
    series = 1.0 + q * (1.0 / 3.0 + q * (1.0 / 5.0 + q * (1.0 / 7.0)))
    slope = f * (2.0 / 3.0 + q * (4.0 / 5.0 + q * (6.0 / 7.0)))
    rf = rcp(f)
    logged = (log_a - log_b) * rf
    log_slope = ((s * inv_a) * (s * inv_b) - logged) * rf
    return s, rs, f, jnp.where(small, series, logged), jnp.where(small, slope, log_slope)


def pair(left, right, scale, left_weight=1.0, right_weight=1.0, face=False):
    rho_l, vl, beta_l = left[0], left[1:4], left[4]
    rho_r, vr, beta_r = right[0], right[1:4], right[4]
    wl, wr = left[9:14], right[9:14]
    if left_weight != 1.0:
        wl = [left_weight * w for w in wl]
    if right_weight != 1.0:
        wr = [right_weight * w for w in wr]
    om = [x - y for x, y in zip(wl, wr)]
    o0, ov, oh = om[0], om[1:4], om[4]
    g = [(x + y) * scale for x, y in zip(left[14:17], right[14:17])]
    vs = [x + y for x, y in zip(vl, vr)]
    rho_s, _, rho_f, rho_factor, rho_slope = log_terms(
        rho_l, rho_r, left[5], right[5], left[7], right[7]
    )
    _, beta_i, beta_f, beta_factor, beta_slope = log_terms(
        beta_l, beta_r, left[6], right[6], left[8], right[8]
    )
    p = rcp(rho_factor)
    half_p = 0.5 * p
    mean = rho_s * half_p
    through = dot3(vs, g)
    a = o0 + 0.5 * dot3(ov, vs) + oh * (dot3(vl, vr) + 5.0 * (beta_factor * beta_i))
    b = dot3(ov, g) + oh * through
    ph = rho_s * beta_i
    bi = beta_i * b
    ua = through * a
    k = half_p * (p * rho_slope)
    x = ua * (half_p + k * rho_f) + bi
    y = ua * k
    d_rho_l, d_rho_r = x - y, x + y
    t = mean * through
    e = t * oh
    c = mean * a + ph * oh
    half_t = 0.5 * t
    z = [c * gg + half_t * oo for gg, oo in zip(g, ov)]
    d_v_l = [zz + e * v for zz, v in zip(z, vr)]
    d_v_r = [zz + e * v for zz, v in zip(z, vl)]
    e5 = (-5.0 * e) * (beta_i * beta_i)
    x = e5 * (beta_factor + beta_slope * beta_f) - ph * bi
    y = e5 * beta_slope
    d_beta_l, d_beta_r = x - y, x + y
    if face:
        xl = o0 + dot3(ov, vl) + oh * (10.0 * left[8] * 0.5 + dot3(vl, vl))
        xr = o0 + dot3(ov, vr) + oh * (10.0 * right[8] * 0.5 + dot3(vr, vr))
        kappa = rho_l * xl - rho_r * xr
        n2 = dot3(g, g)
        half_len = 0.5 * jnp.sqrt(n2)
        cl = jnp.sqrt(1.4 * left[8])
        cr = jnp.sqrt(1.4 * right[8])
        sl = dot3(vl, g)
        sr = dot3(vr, g)
        mean_square = 0.5 * (sl * sl + sr * sr)
        rt = lax.rsqrt(mean_square)
        sigma = mean_square * rt + half_len * (cl + cr)
        kr = (0.5 * kappa) * rt
        krl, krr = kr * sl, kr * sr
        ml, mr = sigma * rho_l, sigma * rho_r
        oh2 = 2.0 * oh
        el, er = ml * oh2, mr * oh2
        d_v_l = [d + krl * gg + ml * oo + el * v for d, gg, oo, v in zip(d_v_l, g, ov, vl)]
        d_v_r = [d + krr * gg - mr * oo - er * v for d, gg, oo, v in zip(d_v_r, g, ov, vr)]
        d_rho_l = d_rho_l + sigma * xl
        d_rho_r = d_rho_r - sigma * xr
        kl = kappa * half_len
        d_beta_l = d_beta_l - left[8] * (kl * cl + 5.0 * (el * left[8]))
        d_beta_r = d_beta_r - right[8] * (kl * cr - 5.0 * (er * right[8]))
    return [d_rho_l, *d_v_l, d_beta_l], [d_rho_r, *d_v_r, d_beta_r]


def node_extras(rho, beta, inv_rho, inv_beta):
    return [0.5 * jnp.log(rho), 0.5 * jnp.log(beta), inv_rho, inv_beta]


def primitives(u):
    v = [x * rcp(u[0]) for x in u[1:4]]
    pressure = 0.4 * (u[4] - 0.5 * dot3(u[1:4], v))
    return [u[0], *v, (0.5 * u[0]) * rcp(pressure)]


def line(load, store):
    total = [None] * 4
    for a in range(4):
        for b in range(a + 1, 4):
            factor = 2.0 * QUAD[a] * TABLE[a, b] / 4.0
            wa, wb = 1.0 / QUAD[a], 1.0 / QUAD[b]
            if wa == wb:
                factor, wa, wb = factor * wa, 1.0, 1.0
            first, second = pair(load(a), load(b), float(factor), wa, wb)
            for node, part in ((a, first), (b, second)):
                total[node] = part if total[node] is None else [x + y for x, y in zip(total[node], part)]
    for a in range(4):
        store(a, total[a])


def kernel(
    nx, ny,
    state_ref, adj_ref, met_ref, jac_ref, code_ref, orient_ref, out_ref,
    st, ad, mt, jc, cd, ori, nb, tb, acc, acct, send, recv, gout, mb, el,
    send_w, recv_u, recv_g, recv_w, recv_f, xo,
    load_sem, send_sem, recv_sem, x_send_sem, x_recv_sem, ready_sem,
):
    f32 = jnp.float32
    ix, iy, iz = lax.axis_index("gx"), lax.axis_index("gy"), lax.axis_index("gz")
    low_x, high_x, low_y, high_y = ix == 0, ix == nx - 1, iy == 0, iy == ny - 1
    ids = [
        {"gx": lax.max(ix - 1, 0)}, {"gx": lax.min(ix + 1, nx - 1)},
        {"gy": lax.max(iy - 1, 0)}, {"gy": lax.min(iy + 1, ny - 1)},
        {"gz": 1 - iz},
    ]
    inner_side = [jnp.logical_not(e) for e in (low_x, high_x, low_y, high_y)] + [None]
    below, here = (ix + 3) % 4, ix % 4
    first = [below >= 2, here < 2, iy % 4 == 0, iy % 4 != 3]
    tied = [below == 2, here == 2]
    slow = tied[1] & inner_side[1]

    place = [None, None, 0, 1, 2]
    greets = [there & mine for there, mine in zip(inner_side, first)]
    greeted = [there & jnp.logical_not(mine) for there, mine in zip(inner_side, first)]
    early = [greeted[side] & jnp.logical_not(tied[side]) for side in range(2)]

    def count(*flags):
        return sum(jnp.where(flag, 1, 0) for flag in flags)

    moves = [(code_ref, cd), (orient_ref, ori), (adj_ref, ad), (jac_ref, jc), (state_ref, st)]
    moves += [(met_ref.at[rows], mt.at[rows]) for rows in (pl.ds(3, 3), pl.ds(0, 3), pl.ds(6, 3))]
    loads = [pltpu.make_async_copy(src, dst, load_sem.at[n]) for n, (src, dst) in enumerate(moves)]
    barrier = pltpu.get_barrier_semaphore()
    def signal(semaphore, target):
        pl.semaphore_signal(semaphore, inc=1, device_id=target, device_id_type=MESH)

    for side in range(4):
        @pl.when(greets[side])
        def _(side=side):
            signal(barrier, {**ids[side], "gz": jnp.where(tied[side], 0, 1) if side < 2 else 0})

    landing = [1, 0, 3, 2, 4]
    ends = [pl.ds(0, 16), pl.ds(112, 16)]

    def remote(source, target, sent, received, side):
        return pltpu.make_async_remote_copy(
            src_ref=source, dst_ref=target, send_sem=sent, recv_sem=received,
            device_id=ids[side], device_id_type=MESH,
        )

    def x_copy(side, n, source, target):
        return remote(source, target, x_send_sem.at[4 * side + n], x_recv_sem.at[4 * landing[side] + n], side)

    raw_copies, weight_copies = [], []
    for side in range(2):
        to = landing[side]
        raw_copies.append(
            [
                x_copy(side, 0, state_ref.at[:, ends[side]], recv_u.at[to]),
                x_copy(side, 1, met_ref.at[0:3, ends[side]], recv_g.at[to]),
            ]
        )
        weight_copies.append(x_copy(side, 2, send_w.at[side], recv_w.at[to]))
    flag_copy = x_copy(1, 3, orient_ref.at[0:8], recv_f)
    raw_copies[1].insert(0, flag_copy)
    copies = {
        side: remote(
            send.at[place[side]], recv.at[place[landing[side]]],
            send_sem.at[place[side]], recv_sem.at[place[landing[side]]], side,
        )
        for side in (2, 3, 4)
    }

    def on_side(side, act):
        if inner_side[side] is None:
            act()
        else:
            pl.when(inner_side[side])(act)

    def start_raw(side):
        for copy in raw_copies[side]:
            copy.start()

    def answer(side, core):
        signal(ready_sem.at[landing[side]], {**ids[side], "gz": core})

    @pl.when(iz == 1)
    def _():
        @pl.when(early[0] | early[1])
        def _():
            pl.semaphore_wait(barrier, 2 * count(early[0], early[1]))

        signal(barrier, {"gz": 0})
        for side in (1, 0):
            @pl.when(early[side])
            def _(side=side):
                answer(side, 1)
                start_raw(side)

    for copy in loads:
        copy.start()
    for side in range(4):
        @pl.when(jnp.logical_not(inner_side[side]))
        def _(side=side):
            blank = jnp.zeros((8, 128), f32)
            if side < 2:
                for ref, count in ((recv_u, 5), (recv_g, 3), (recv_w, 5)):
                    for n in range(count):
                        for half in range(2):
                            ref[side, n, pl.ds(8 * half, 8)] = blank
                if side == 0:
                    recv_f[...] = jnp.zeros((8, 32), jnp.int32)
            else:
                for n in range(13):
                    recv[place[side], n] = blank

    def meet():
        pl.semaphore_wait(barrier, 2 * count(slow, greeted[2], greeted[3]) + 1)
        for side in (1, 0):
            @pl.when(early[side])
            def _(side=side):
                answer(side, 0)

        signal(ready_sem.at[4], {"gz": 1})
        for side in (1, 2, 3):
            @pl.when(slow if side == 1 else greeted[side])
            def _(side=side):
                answer(side, 0)
                answer(side, 1)

    @pl.when((iz == 0) & jnp.logical_not(slow))
    def _():
        meet()
        for side in (1, 0):
            pl.when(early[side])(lambda side=side: start_raw(side))

    sub = lax.broadcasted_iota(jnp.int32, (8, 128), 0)
    lane = lax.broadcasted_iota(jnp.int32, (8, 128), 1)
    sub_flip = sub ^ 3
    lane_flip = lane ^ 48

    def flip_sub(value):
        return jnp.take_along_axis(value, sub_flip, axis=0, mode="promise_in_bounds")

    def flip_lane(value):
        return jnp.take_along_axis(value, lane_flip, axis=1, mode="promise_in_bounds")

    loads[0].wait()
    loads[1].wait()
    el[0:8, :] = cd[...].astype(f32)
    el[8:32, :] = ori[...].astype(f32)
    spread = (
        lax.broadcasted_iota(jnp.int32, (32, 128), 1) // 4 == lax.broadcasted_iota(jnp.int32, (32, 128), 0)
    ).astype(f32)
    wide = jnp.dot(el[...], spread, preferred_element_type=f32)
    xy = lax.broadcasted_iota(jnp.int32, (8, 128), 1)
    spread_xy = ((xy // 64) * 4 + (xy % 16) // 4 == sub).astype(f32)
    contract = (((0,), (0,)), ((), ()))
    code_z = lax.dot_general(el[0:8, :], spread_xy, contract, preferred_element_type=f32)
    flag_z = lax.dot_general(el[24:32, :], spread_xy, contract, preferred_element_type=f32)

    def two_rows(first, second):
        return jnp.where(
            sub < 4,
            jnp.broadcast_to(wide[first : first + 1], (8, 128)),
            jnp.broadcast_to(wide[second : second + 1], (8, 128)),
        )

    def x_rows(base, ex, half):
        return two_rows(base + ex * 4 + 2 * half, base + ex * 4 + 2 * half + 1)

    def y_rows(base, ey):
        return two_rows(base + ey, base + 4 + ey)

    codes = [x_rows(0, 0, 0), x_rows(0, 0, 1), x_rows(0, 1, 0), x_rows(0, 1, 1), y_rows(0, 0), y_rows(0, 3)]
    low_row = sub % 2 == 0
    codes.append(
        jnp.where(
            low_row,
            jnp.broadcast_to(code_z[0:1], (8, 128)),
            jnp.broadcast_to(code_z[31:32], (8, 128)),
        )
    )
    one, zero = jnp.ones((8, 128), f32), jnp.zeros((8, 128), f32)
    at_edge = [jnp.where(e, one, zero) for e in (low_x, low_x, high_x, high_x, low_y, high_y)]
    at_edge.append(jnp.where(low_row, jnp.where(iz == 0, one, zero), jnp.where(iz == 1, one, zero)))
    signs = [-1.5 * one, -1.5 * one, 1.5 * one, 1.5 * one, -1.5 * one, 1.5 * one, jnp.where(low_row, -1.5 * one, 1.5 * one)]
    for slot in range(SLOTS):
        mb[slot, 0] = signs[slot]
        far = at_edge[slot] * codes[slot]
        mb[slot, 1] = far
        mb[slot, 2] = at_edge[slot] - far
    flag_x_mid = [x_rows(8, 0, half) > 0.5 for half in range(2)]
    for half in range(2):
        mb[2 + half, 3] = x_rows(8, 1, half)
    flag_y_mid = [y_rows(16, ey) > 0.5 for ey in range(3)]
    flag_y_top = (y_rows(16, 3) > 0.5) & jnp.logical_not(high_y)
    flag_z_top = (jnp.broadcast_to(flag_z[31:32], (8, 128)) > 0.5) & jnp.logical_not(low_row) & (iz == 0)

    def convert(rows, keep=True):
        rho, m, energy = st[0, rows], [st[n, rows] for n in (1, 2, 3)], st[4, rows]
        r = rcp(rho)
        v = [x * r for x in m]
        pressure = 0.4 * (energy - 0.5 * dot3(m, v))
        beta = (0.5 * rho) * rcp(pressure)
        rj = -rcp(jc[rows])
        w = [ad[n, rows] * rj for n in range(5)]
        w[4] = 0.5 * w[4]
        values = [rho, *v, beta, *node_extras(rho, beta, 0.5 * r, pressure * r), *w]
        if keep:
            for n, value in enumerate(values):
                nb[n, rows] = value
        return values

    for load in loads[2:5]:
        load.wait()

    def pack(slot, values, flag=None, flip=None):
        for n, value in enumerate(values):
            if flag is not None:
                value = jnp.where(flag, flip(value), value)
            send[slot, n] = value

    for slot, block in ((2, 14), (3, 15), (0, 0), (1, 1)):
        values = convert(pl.ds(block * 8, 8))
        for n in range(5):
            send_w[slot // 2, n, pl.ds(8 * (slot % 2), 8)] = values[9 + n]
    prompt = (iz == 1) | jnp.logical_not(slow)
    for side in (1, 0):
        pl.when(early[side] & prompt)(weight_copies[side].start)

    loads[5].wait()
    for slot, y, flag in ((0, 0, None), (1, 15, flag_y_top)):
        rows = pl.ds(y, 8, stride=16)
        values = convert(rows, keep=False)
        pack(slot, values[0:5] + values[9:14] + [mt[3 + n, rows] for n in range(3)], flag, flip_sub)

    for side in (2, 3):
        pl.when(greeted[side] & (iz == 0) & prompt)(copies[side].start)

    @pl.loop(2, 14)
    def _(block):
        convert(pl.ds(pl.multiple_of(block * 8, 8), 8))

    def load_y(y):
        rows = pl.ds(y, 8, stride=16)
        return [nb[n, rows] for n in range(14)] + [mt[3 + n, rows] for n in range(3)]

    loads[6].wait()

    def load_x(rows):
        return [nb[n, rows] for n in range(14)] + [mt[n, rows] for n in range(3)]

    @pl.loop(0, 4)
    def _(chunk):
        base = (chunk // 2) * 64 + (chunk % 2) * 8

        def at(a):
            return pl.ds(pl.multiple_of(base + a * 16, 8), 8)

        def store(a, total):
            for n in range(5):
                acc[n, at(a)] = total[n]

        line(lambda a: load_x(at(a)), store)

    def answered(side, here):
        @pl.when(greets[side] & here)
        def _():
            pl.semaphore_wait(ready_sem.at[side], 1)
            if side < 2:
                start_raw(side)
                weight_copies[side].start()
            else:
                copies[side].start()

    @pl.when(iz == 1)
    def _():
        pl.semaphore_wait(ready_sem.at[4], 1)

    pl.when(jnp.logical_not(prompt))(meet)
    for side in (2, 3):
        pl.when(greeted[side] & ((iz == 1) | jnp.logical_not(prompt)))(copies[side].start)
    for side in (1, 0):
        @pl.when(early[side] & jnp.logical_not(prompt))
        def _(side=side):
            start_raw(side)
            weight_copies[side].start()

    @pl.when(slow)
    def _():
        start_raw(1)
        weight_copies[1].start()

    answered(2, here == 3)
    answered(0, here == 3)

    loads[7].wait()
    for n in range(5):
        tb[n, 0:128] = jnp.transpose(nb[n])
        tb[9 + n, 0:128] = jnp.transpose(nb[9 + n])
    for n in range(3):
        tb[14 + n, 0:128] = jnp.transpose(mt[6 + n])
    raw_t = [0, 1, 2, 3, 4, 9, 10, 11, 12, 13, 14, 15, 16]
    low_z = [jnp.broadcast_to(tb[n, 0:1], (8, 128)) for n in raw_t]
    high_z = [jnp.broadcast_to(tb[n, 127:128], (8, 128)) for n in raw_t]
    pack(2, [jnp.where(low_row, x, y) for x, y in zip(low_z, high_z)], flag_z_top, flip_lane)
    copies[4].start()
    answered(3, here != 2)

    @pl.loop(0, 16)
    def _(block):
        rows = pl.ds(pl.multiple_of(block * 8, 8), 8)
        rho, beta = tb[0, rows], tb[4, rows]
        for n, value in enumerate(node_extras(rho, beta, 0.5 * rcp(rho), 0.5 * rcp(beta))):
            tb[5 + n, rows] = value

    def add(ref, rows, parts):
        for n in range(5):
            ref[n, rows] = ref[n, rows] + parts[n]

    def flipped(values, flag, flip):
        return [jnp.where(flag, flip(value), value) for value in values]

    for half in range(2):
        lower, upper = pl.ds(48 + 8 * half, 8), pl.ds(64 + 8 * half, 8)
        left = flipped(load_x(lower), flag_x_mid[half], flip_sub)
        to_l, to_u = pair(left, load_x(upper), 1.5, face=True)
        add(acc, lower, flipped(to_l, flag_x_mid[half], flip_sub))
        add(acc, upper, to_u)

    @pl.loop(0, 4)
    def _(chunk):
        def store(a, total):
            add(acc, pl.ds(chunk * 4 + a, 8, stride=16), total)

        line(lambda a: load_y(chunk * 4 + a), store)

    for ey in range(3):
        left = flipped(load_y(4 * ey + 3), flag_y_mid[ey], flip_sub)
        to_l, to_u = pair(left, load_y(4 * ey + 4), 1.5, face=True)
        add(acc, pl.ds(4 * ey + 3, 8, stride=16), flipped(to_l, flag_y_mid[ey], flip_sub))
        add(acc, pl.ds(4 * ey + 4, 8, stride=16), to_u)

    answered(3, here == 2)
    answered(2, here != 3)
    answered(1, here == 0)

    def rows_z(chunk, a):
        return pl.ds(chunk * 32 + a, 8, stride=4)

    def load_z(rows):
        return [tb[n, rows] for n in range(17)]

    @pl.loop(0, 4)
    def _(chunk):
        def store(a, total):
            for n in range(5):
                acct[n, rows_z(chunk, a)] = total[n]

        line(lambda a: load_z(rows_z(chunk, a)), store)

    answered(1, here == 1)
    for chunk in range(4):
        flag = flag_z[8 * chunk : 8 * chunk + 8] > 0.5
        lower = rows_z(chunk, 3)
        left = flipped(load_z(lower), flag, flip_lane)
        upper = rows_z(chunk, 4)
        right = load_z(upper)
        to_l, to_u = pair(left, right, 1.5, face=True)
        to_l = flipped(to_l, flag, flip_lane)
        if chunk == 3:
            inside = sub < 7
            to_l = [jnp.where(inside, x, 0.0) for x in to_l]
            to_u = [jnp.where(inside, x, 0.0) for x in to_u]
        add(acct, lower, to_l)
        add(acct, upper, to_u)

    answered(0, here == 0)

    for side in (4, 2, 3):
        on_side(side, copies[landing[side]].wait_recv)
    for n in range(13):
        recv[2, n] = pltpu.roll(recv[2, n], 1, 0)

    inflow = np.array(INFLOW_STATE)
    inflow_v = inflow[1:4] / inflow[0]
    inflow_p = 0.4 * (inflow[4] - 0.5 * np.sum(inflow[1:4] * inflow_v))
    far_values = [float(inflow[0]), *[float(x) for x in inflow_v], float(inflow[0] / (2.0 * inflow_p))]

    def mirror(v, g, turn):
        along = turn * dot3(v, g)
        return [x - along * y for x, y in zip(v, g)]

    def outer_node(slot, own, prim, normal):
        is_far, is_wall = mb[slot, 1] > 0.5, mb[slot, 2] > 0.5
        outside = is_far | is_wall
        g = own[14:17]
        image = [own[0], *mirror(own[1:4], g, 2.0 * rcp(dot3(g, g))), own[4]]
        prim = [jnp.where(is_far, f, jnp.where(is_wall, i, o)) for f, i, o in zip(far_values, image, prim)]
        normal = [jnp.where(outside, i, o) for i, o in zip(g, normal)]
        extras = node_extras(prim[0], prim[4], 0.5 * rcp(prim[0]), 0.5 * rcp(prim[4]))
        return [*prim, *extras], normal

    def side_faces(slot, own, other, w, normal):
        is_wall = mb[slot, 2] > 0.5
        outside = (mb[slot, 1] > 0.5) | is_wall
        w = [jnp.where(outside, 0.0, x) for x in w]
        mine, theirs = pair(own, [*other, *w, *normal], mb[slot, 0], face=True)
        g = own[14:17]
        back = [theirs[0], *mirror(theirs[1:4], g, 2.0 * rcp(dot3(g, g))), theirs[4]]
        return [x + jnp.where(is_wall, y, 0.0) for x, y in zip(mine, back)]

    @pl.loop(0, 3)
    def _(slot):
        own = [send[slot, n] for n in range(13)]
        other = [recv[slot, n] for n in range(13)]
        extras = node_extras(own[0], own[4], 0.5 * rcp(own[0]), 0.5 * rcp(own[4]))
        own = [*own[0:5], *extras, *own[5:13]]
        prim, normal = outer_node(slot + 4, own, other[0:5], other[10:13])
        for n, part in enumerate(side_faces(slot + 4, own, prim, other[5:10], normal)):
            gout[slot, n] = part

    add(acc, pl.ds(0, 8, stride=16), [gout[0, n] for n in range(5)])
    add(acc, pl.ds(15, 8, stride=16), flipped([gout[1, n] for n in range(5)], flag_y_top, flip_sub))
    for n in range(5):
        part = gout[2, n]
        part = jnp.where(flag_z_top, flip_lane(part), part)
        acct[n, 0:1] = acct[n, 0:1] + part[0:1]
        acct[n, 127:128] = acct[n, 127:128] + part[1:2]

    for n in range(5):
        acc[n] = acc[n] + jnp.transpose(acct[n, 0:128])

    def finish(rows, parts):
        v, beta, r = [nb[n, rows] for n in (1, 2, 3)], nb[4, rows], 2.0 * nb[7, rows]
        d_rho, d_v, d_beta = parts[0], parts[1:4], parts[4]
        db = d_beta * (beta * r)
        d_p = (-0.8 * beta) * db
        out_ref[4, rows] = d_p
        for n in range(3):
            out_ref[1 + n, rows] = d_v[n] * r - d_p * v[n]
        out_ref[0, rows] = d_rho + db - r * dot3(d_v, v) + 0.5 * d_p * dot3(v, v)

    @pl.loop(2, 14)
    def _(block):
        rows = pl.ds(pl.multiple_of(block * 8, 8), 8)
        finish(rows, [acc[n, rows] for n in range(5)])

    def x_rows_of(side, half):
        return pl.ds(pl.multiple_of(side * 112 + half * 8, 8), 8)

    def x_flags(side, half):
        return mb[2 * side + half, 3] > 0.5

    on_side(0, flag_copy.wait_recv)
    el[0:8, :] = recv_f[...].astype(f32)
    below_flags = jnp.dot(el[0:8, :], spread, preferred_element_type=f32)
    for half in range(2):
        mb[half, 3] = jnp.where(
            sub < 4,
            jnp.broadcast_to(below_flags[4 + 2 * half : 5 + 2 * half], (8, 128)),
            jnp.broadcast_to(below_flags[5 + 2 * half : 6 + 2 * half], (8, 128)),
        )

    def arrive(side, *waits):
        for n in range(2):
            @pl.when((side == n) & inner_side[n])
            def _(n=n):
                for wait in waits:
                    wait(n)

    @pl.loop(0, 2)
    def _(turn):
        side = jnp.where(here == 0, 1 - turn, turn)
        arrive(
            side,
            lambda n: raw_copies[landing[n]][-2].wait_recv(),
            lambda n: raw_copies[landing[n]][-1].wait_recv(),
        )
        for half in range(2):
            slot, rows, flag = 2 * side + half, pl.ds(8 * half, 8), x_flags(side, half)
            u = flipped([recv_u[side, n, rows] for n in range(5)], flag, flip_sub)
            normal = flipped([recv_g[side, n, rows] for n in range(3)], flag, flip_sub)
            other, normal = outer_node(slot, load_x(x_rows_of(side, half)), primitives(u), normal)
            for n, value in enumerate([*other, *normal]):
                xo[slot, n] = value

    @pl.loop(0, 2)
    def _(turn):
        side = jnp.where(here == 0, 1 - turn, turn)
        arrive(side, lambda n: weight_copies[landing[n]].wait_recv())
        for half in range(2):
            slot, rows = 2 * side + half, x_rows_of(side, half)
            w = flipped([recv_w[side, n, pl.ds(8 * half, 8)] for n in range(5)], x_flags(side, half), flip_sub)
            other, normal = [xo[slot, n] for n in range(9)], [xo[slot, 9 + n] for n in range(3)]
            parts = side_faces(slot, load_x(rows), other, w, normal)
            finish(rows, [acc[n, rows] + part for n, part in enumerate(parts)])

    for side in (4, 2, 3):
        on_side(side, copies[side].wait_send)
    for side in (1, 0):
        for copy in (*raw_copies[side], weight_copies[side]):
            on_side(side, copy.wait_send)


def solution(mesh):
    nx, ny, nz = mesh.shape["gx"], mesh.shape["gy"], mesh.shape["gz"]
    assert nz == 2

    def body(state, adjoint, metric, jacobian, boundary_kind_code, orient):
        assert state.shape == (5, 8, 16, 128)
        f32 = jnp.float32
        hbm = pl.BlockSpec(memory_space=pltpu.HBM)
        vmem = pltpu.VMEM
        out = pl.pallas_call(
            lambda *refs: kernel(nx, ny, *refs),
            out_shape=jax.ShapeDtypeStruct((5, 128, 128), f32),
            in_specs=[hbm] * 6,
            out_specs=pl.BlockSpec(memory_space=vmem),
            scratch_shapes=[
                vmem((5, 128, 128), f32),
                vmem((5, 128, 128), f32),
                vmem((9, 128, 128), f32),
                vmem((128, 128), f32),
                vmem((8, 32), jnp.int32),
                vmem((24, 32), jnp.int32),
                vmem((14, 128, 128), f32),
                vmem((17, 136, 128), f32),
                vmem((5, 128, 128), f32),
                vmem((5, 136, 128), f32),
                vmem((3, 13, 8, 128), f32),
                vmem((3, 13, 8, 128), f32),
                vmem((3, 5, 8, 128), f32),
                vmem((SLOTS, 4, 8, 128), f32),
                vmem((32, 32), f32),
                vmem((2, 5, 16, 128), f32),
                vmem((2, 5, 16, 128), f32),
                vmem((2, 3, 16, 128), f32),
                vmem((2, 5, 16, 128), f32),
                vmem((8, 32), jnp.int32),
                vmem((4, 12, 8, 128), f32),
                pltpu.SemaphoreType.DMA((8,)),
                pltpu.SemaphoreType.DMA((3,)),
                pltpu.SemaphoreType.DMA((3,)),
                pltpu.SemaphoreType.DMA((8,)),
                pltpu.SemaphoreType.DMA((8,)),
                pltpu.SemaphoreType.REGULAR((5,)),
            ],
            compiler_params=pltpu.CompilerParams(
                collective_id=0, has_side_effects=True, vmem_limit_bytes=32 * 1024 * 1024
            ),
            name="adjoint_residual",
        )(
            *(
                pltpu.with_memory_space_constraint(value, pltpu.HBM)
                for value in (
                    state.reshape(5, 128, 128),
                    adjoint.reshape(5, 128, 128),
                    metric.reshape(9, 128, 128),
                    jacobian.reshape(128, 128),
                    boundary_kind_code.reshape(8, 32),
                    orient.reshape(24, 32),
                )
            )
        )
        return out.reshape(5, 8, 16, 128)

    return jax.shard_map(
        body,
        mesh=mesh,
        in_specs=(
            P(None, "gx", "gy", "gz"),
            P(None, "gx", "gy", "gz"),
            P(None, "gx", "gy", "gz"),
            P("gx", "gy", "gz"),
            P("gx", "gy", "gz"),
            P(None, "gx", "gy", "gz"),
        ),
        out_specs=P(None, "gx", "gy", "gz"),
        check_vma=False,
    )
```

```python
import jax
import jax.numpy as jnp
import numpy as np
from jax import lax
from jax.experimental import pallas as pl
from jax.experimental.pallas import tpu as pltpu
from jax.sharding import PartitionSpec as P

INFLOW_STATE = (1.0, 0.4, 0.0, 0.1, 2.085)
MESH = pl.DeviceIdType.MESH
SLOTS = 7


def lobatto_matrix():
    points = np.array([-1.0, -1.0 / np.sqrt(5.0), 1.0 / np.sqrt(5.0), 1.0])
    weights = np.array(
        [
            1.0 / np.prod([points[place] - points[other] for other in range(4) if other != place])
            for place in range(4)
        ]
    )
    table = np.zeros((4, 4))
    for place in range(4):
        for other in range(4):
            if other != place:
                table[place, other] = (
                    weights[other] / weights[place] / (points[place] - points[other])
                )
        table[place, place] = -np.sum(table[place])
    return table


QUAD = (1.0, 5.0, 5.0, 1.0)
TABLE = lobatto_matrix()


def rcp(value):
    guess = pl.reciprocal(value, approx=True)
    return guess * (2.0 - value * guess)


def dot3(first, second):
    return first[0] * second[0] + first[1] * second[1] + first[2] * second[2]


def log_terms(a, b, log_a, log_b, inv_a, inv_b):
    s = a + b
    rs = rcp(s)
    f = (a - b) * rs
    q = f * f
    small = q < 0.01
    series = 1.0 + q * (1.0 / 3.0 + q * (1.0 / 5.0 + q * (1.0 / 7.0)))
    slope = f * (2.0 / 3.0 + q * (4.0 / 5.0 + q * (6.0 / 7.0)))
    rf = rcp(f)
    logged = (log_a - log_b) * rf
    log_slope = ((s * inv_a) * (s * inv_b) - logged) * rf
    return s, rs, f, jnp.where(small, series, logged), jnp.where(small, slope, log_slope)


def pair(left, right, scale, left_weight=1.0, right_weight=1.0, face=False):
    rho_l, vl, beta_l = left[0], left[1:4], left[4]
    rho_r, vr, beta_r = right[0], right[1:4], right[4]
    wl, wr = left[9:14], right[9:14]
    if left_weight != 1.0:
        wl = [left_weight * w for w in wl]
    if right_weight != 1.0:
        wr = [right_weight * w for w in wr]
    om = [x - y for x, y in zip(wl, wr)]
    o0, ov, oh = om[0], om[1:4], om[4]
    g = [(x + y) * scale for x, y in zip(left[14:17], right[14:17])]
    vs = [x + y for x, y in zip(vl, vr)]
    rho_s, _, rho_f, rho_factor, rho_slope = log_terms(
        rho_l, rho_r, left[5], right[5], left[7], right[7]
    )
    _, beta_i, beta_f, beta_factor, beta_slope = log_terms(
        beta_l, beta_r, left[6], right[6], left[8], right[8]
    )
    p = rcp(rho_factor)
    half_p = 0.5 * p
    mean = rho_s * half_p
    through = dot3(vs, g)
    a = o0 + 0.5 * dot3(ov, vs) + oh * (dot3(vl, vr) + 5.0 * (beta_factor * beta_i))
    b = dot3(ov, g) + oh * through
    ph = rho_s * beta_i
    bi = beta_i * b
    ua = through * a
    k = half_p * (p * rho_slope)
    x = ua * (half_p + k * rho_f) + bi
    y = ua * k
    d_rho_l, d_rho_r = x - y, x + y
    t = mean * through
    e = t * oh
    c = mean * a + ph * oh
    half_t = 0.5 * t
    z = [c * gg + half_t * oo for gg, oo in zip(g, ov)]
    d_v_l = [zz + e * v for zz, v in zip(z, vr)]
    d_v_r = [zz + e * v for zz, v in zip(z, vl)]
    e5 = (-5.0 * e) * (beta_i * beta_i)
    x = e5 * (beta_factor + beta_slope * beta_f) - ph * bi
    y = e5 * beta_slope
    d_beta_l, d_beta_r = x - y, x + y
    if face:
        xl = o0 + dot3(ov, vl) + oh * (10.0 * left[8] * 0.5 + dot3(vl, vl))
        xr = o0 + dot3(ov, vr) + oh * (10.0 * right[8] * 0.5 + dot3(vr, vr))
        kappa = rho_l * xl - rho_r * xr
        n2 = dot3(g, g)
        half_len = 0.5 * jnp.sqrt(n2)
        cl = jnp.sqrt(1.4 * left[8])
        cr = jnp.sqrt(1.4 * right[8])
        sl = dot3(vl, g)
        sr = dot3(vr, g)
        mean_square = 0.5 * (sl * sl + sr * sr)
        rt = lax.rsqrt(mean_square)
        sigma = mean_square * rt + half_len * (cl + cr)
        kr = (0.5 * kappa) * rt
        krl, krr = kr * sl, kr * sr
        ml, mr = sigma * rho_l, sigma * rho_r
        oh2 = 2.0 * oh
        el, er = ml * oh2, mr * oh2
        d_v_l = [d + krl * gg + ml * oo + el * v for d, gg, oo, v in zip(d_v_l, g, ov, vl)]
        d_v_r = [d + krr * gg - mr * oo - er * v for d, gg, oo, v in zip(d_v_r, g, ov, vr)]
        d_rho_l = d_rho_l + sigma * xl
        d_rho_r = d_rho_r - sigma * xr
        kl = kappa * half_len
        d_beta_l = d_beta_l - left[8] * (kl * cl + 5.0 * (el * left[8]))
        d_beta_r = d_beta_r - right[8] * (kl * cr - 5.0 * (er * right[8]))
    return [d_rho_l, *d_v_l, d_beta_l], [d_rho_r, *d_v_r, d_beta_r]


def node_extras(rho, beta, inv_rho, inv_beta):
    return [0.5 * jnp.log(rho), 0.5 * jnp.log(beta), inv_rho, inv_beta]


def primitives(u):
    v = [x * rcp(u[0]) for x in u[1:4]]
    pressure = 0.4 * (u[4] - 0.5 * dot3(u[1:4], v))
    return [u[0], *v, (0.5 * u[0]) * rcp(pressure)]


def line(load, store):
    total = [None] * 4
    for a in range(4):
        for b in range(a + 1, 4):
            factor = 2.0 * QUAD[a] * TABLE[a, b] / 4.0
            wa, wb = 1.0 / QUAD[a], 1.0 / QUAD[b]
            if wa == wb:
                factor, wa, wb = factor * wa, 1.0, 1.0
            first, second = pair(load(a), load(b), float(factor), wa, wb)
            for node, part in ((a, first), (b, second)):
                total[node] = part if total[node] is None else [x + y for x, y in zip(total[node], part)]
    for a in range(4):
        store(a, total[a])


def kernel(
    nx, ny,
    state_ref, adj_ref, met_ref, jac_ref, code_ref, orient_ref, out_ref,
    st, ad, mt, jc, cd, ori, nb, tb, acc, acct, send, recv, gout, mb, el,
    send_w, recv_u, recv_g, recv_w, recv_f, xo,
    load_sem, send_sem, recv_sem, x_send_sem, x_recv_sem, ready_sem,
):
    f32 = jnp.float32
    ix, iy, iz = lax.axis_index("gx"), lax.axis_index("gy"), lax.axis_index("gz")
    low_x, high_x, low_y, high_y = ix == 0, ix == nx - 1, iy == 0, iy == ny - 1
    ids = [
        {"gx": lax.max(ix - 1, 0)}, {"gx": lax.min(ix + 1, nx - 1)},
        {"gy": lax.max(iy - 1, 0)}, {"gy": lax.min(iy + 1, ny - 1)},
        {"gz": 1 - iz},
    ]
    inner_side = [jnp.logical_not(e) for e in (low_x, high_x, low_y, high_y)] + [None]
    below, here = (ix + 3) % 4, ix % 4
    first = [below >= 2, here < 2, iy % 4 == 0, iy % 4 != 3]
    tied = [below == 2, here == 2]
    slow = tied[1] & inner_side[1]

    place = [None, None, 0, 1, 2]
    greets = [there & mine for there, mine in zip(inner_side, first)]
    greeted = [there & jnp.logical_not(mine) for there, mine in zip(inner_side, first)]
    early = [greeted[side] & jnp.logical_not(tied[side]) for side in range(2)]

    def count(*flags):
        return sum(jnp.where(flag, 1, 0) for flag in flags)

    moves = [(code_ref, cd), (orient_ref, ori), (adj_ref, ad), (jac_ref, jc), (state_ref, st)]
    moves += [(met_ref.at[rows], mt.at[rows]) for rows in (pl.ds(3, 3), pl.ds(0, 3), pl.ds(6, 3))]
    loads = [pltpu.make_async_copy(src, dst, load_sem.at[n]) for n, (src, dst) in enumerate(moves)]
    barrier = pltpu.get_barrier_semaphore()
    def signal(semaphore, target):
        pl.semaphore_signal(semaphore, inc=1, device_id=target, device_id_type=MESH)

    for side in range(4):
        @pl.when(greets[side])
        def _(side=side):
            signal(barrier, {**ids[side], "gz": jnp.where(tied[side], 0, 1) if side < 2 else 0})

    landing = [1, 0, 3, 2, 4]
    ends = [pl.ds(0, 16), pl.ds(112, 16)]

    def remote(source, target, sent, received, side):
        return pltpu.make_async_remote_copy(
            src_ref=source, dst_ref=target, send_sem=sent, recv_sem=received,
            device_id=ids[side], device_id_type=MESH,
        )

    def x_copy(side, n, source, target):
        return remote(source, target, x_send_sem.at[4 * side + n], x_recv_sem.at[4 * landing[side] + n], side)

    raw_copies, weight_copies = [], []
    for side in range(2):
        to = landing[side]
        raw_copies.append(
            [
                x_copy(side, 0, state_ref.at[:, ends[side]], recv_u.at[to]),
                x_copy(side, 1, met_ref.at[0:3, ends[side]], recv_g.at[to]),
            ]
        )
        weight_copies.append(x_copy(side, 2, send_w.at[side], recv_w.at[to]))
    flag_copy = x_copy(1, 3, orient_ref.at[0:8], recv_f)
    raw_copies[1].insert(0, flag_copy)
    copies = {
        side: remote(
            send.at[place[side]], recv.at[place[landing[side]]],
            send_sem.at[place[side]], recv_sem.at[place[landing[side]]], side,
        )
        for side in (2, 3, 4)
    }

    def on_side(side, act):
        if inner_side[side] is None:
            act()
        else:
            pl.when(inner_side[side])(act)

    def start_raw(side):
        for copy in raw_copies[side]:
            copy.start()

    def answer(side, core):
        signal(ready_sem.at[landing[side]], {**ids[side], "gz": core})

    @pl.when(iz == 1)
    def _():
        @pl.when(early[0] | early[1])
        def _():
            pl.semaphore_wait(barrier, 2 * count(early[0], early[1]))

        signal(barrier, {"gz": 0})
        for side in (1, 0):
            @pl.when(early[side])
            def _(side=side):
                answer(side, 1)
                start_raw(side)

    for copy in loads:
        copy.start()
    for side in range(4):
        @pl.when(jnp.logical_not(inner_side[side]))
        def _(side=side):
            blank = jnp.zeros((8, 128), f32)
            if side < 2:
                for ref, count in ((recv_u, 5), (recv_g, 3), (recv_w, 5)):
                    for n in range(count):
                        for half in range(2):
                            ref[side, n, pl.ds(8 * half, 8)] = blank
                if side == 0:
                    recv_f[...] = jnp.zeros((8, 32), jnp.int32)
            else:
                for n in range(13):
                    recv[place[side], n] = blank

    def meet():
        pl.semaphore_wait(barrier, 2 * count(slow, greeted[2], greeted[3]) + 1)
        for side in (1, 0):
            @pl.when(early[side])
            def _(side=side):
                answer(side, 0)
                pl.when(jnp.logical_not(slow))(lambda: start_raw(side))

        signal(ready_sem.at[4], {"gz": 1})
        for side in (1, 2, 3):
            @pl.when(slow if side == 1 else greeted[side])
            def _(side=side):
                answer(side, 0)
                answer(side, 1)

    @pl.when((iz == 0) & jnp.logical_not(slow))
    def _():
        meet()

    sub = lax.broadcasted_iota(jnp.int32, (8, 128), 0)
    lane = lax.broadcasted_iota(jnp.int32, (8, 128), 1)
    sub_flip = sub ^ 3
    lane_flip = lane ^ 48

    def flip_sub(value):
        return jnp.take_along_axis(value, sub_flip, axis=0, mode="promise_in_bounds")

    def flip_lane(value):
        return jnp.take_along_axis(value, lane_flip, axis=1, mode="promise_in_bounds")

    loads[0].wait()
    loads[1].wait()
    el[0:8, :] = cd[...].astype(f32)
    el[8:32, :] = ori[...].astype(f32)
    spread = (
        lax.broadcasted_iota(jnp.int32, (32, 128), 1) // 4 == lax.broadcasted_iota(jnp.int32, (32, 128), 0)
    ).astype(f32)
    wide = jnp.dot(el[...], spread, preferred_element_type=f32)
    xy = lax.broadcasted_iota(jnp.int32, (8, 128), 1)
    spread_xy = ((xy // 64) * 4 + (xy % 16) // 4 == sub).astype(f32)
    contract = (((0,), (0,)), ((), ()))
    code_z = lax.dot_general(el[0:8, :], spread_xy, contract, preferred_element_type=f32)
    flag_z = lax.dot_general(el[24:32, :], spread_xy, contract, preferred_element_type=f32)

    def two_rows(first, second):
        return jnp.where(
            sub < 4,
            jnp.broadcast_to(wide[first : first + 1], (8, 128)),
            jnp.broadcast_to(wide[second : second + 1], (8, 128)),
        )

    def x_rows(base, ex, half):
        return two_rows(base + ex * 4 + 2 * half, base + ex * 4 + 2 * half + 1)

    def y_rows(base, ey):
        return two_rows(base + ey, base + 4 + ey)

    codes = [x_rows(0, 0, 0), x_rows(0, 0, 1), x_rows(0, 1, 0), x_rows(0, 1, 1), y_rows(0, 0), y_rows(0, 3)]
    low_row = sub % 2 == 0
    codes.append(
        jnp.where(
            low_row,
            jnp.broadcast_to(code_z[0:1], (8, 128)),
            jnp.broadcast_to(code_z[31:32], (8, 128)),
        )
    )
    one, zero = jnp.ones((8, 128), f32), jnp.zeros((8, 128), f32)
    at_edge = [jnp.where(e, one, zero) for e in (low_x, low_x, high_x, high_x, low_y, high_y)]
    at_edge.append(jnp.where(low_row, jnp.where(iz == 0, one, zero), jnp.where(iz == 1, one, zero)))
    signs = [-1.5 * one, -1.5 * one, 1.5 * one, 1.5 * one, -1.5 * one, 1.5 * one, jnp.where(low_row, -1.5 * one, 1.5 * one)]
    for slot in range(SLOTS):
        mb[slot, 0] = signs[slot]
        far = at_edge[slot] * codes[slot]
        mb[slot, 1] = far
        mb[slot, 2] = at_edge[slot] - far
    flag_x_mid = [x_rows(8, 0, half) > 0.5 for half in range(2)]
    for half in range(2):
        mb[2 + half, 3] = x_rows(8, 1, half)
    flag_y_mid = [y_rows(16, ey) > 0.5 for ey in range(3)]
    flag_y_top = (y_rows(16, 3) > 0.5) & jnp.logical_not(high_y)
    flag_z_top = (jnp.broadcast_to(flag_z[31:32], (8, 128)) > 0.5) & jnp.logical_not(low_row) & (iz == 0)

    def convert(rows, keep=True):
        rho, m, energy = st[0, rows], [st[n, rows] for n in (1, 2, 3)], st[4, rows]
        r = rcp(rho)
        v = [x * r for x in m]
        pressure = 0.4 * (energy - 0.5 * dot3(m, v))
        beta = (0.5 * rho) * rcp(pressure)
        rj = -rcp(jc[rows])
        w = [ad[n, rows] * rj for n in range(5)]
        w[4] = 0.5 * w[4]
        values = [rho, *v, beta, *node_extras(rho, beta, 0.5 * r, pressure * r), *w]
        if keep:
            for n, value in enumerate(values):
                nb[n, rows] = value
        return values

    for load in loads[2:5]:
        load.wait()

    def pack(slot, values, flag=None, flip=None):
        for n, value in enumerate(values):
            if flag is not None:
                value = jnp.where(flag, flip(value), value)
            send[slot, n] = value

    for slot, block in ((2, 14), (3, 15), (0, 0), (1, 1)):
        values = convert(pl.ds(block * 8, 8))
        for n in range(5):
            send_w[slot // 2, n, pl.ds(8 * (slot % 2), 8)] = values[9 + n]
    prompt = (iz == 1) | jnp.logical_not(slow)
    for side in (1, 0):
        pl.when(early[side] & prompt)(weight_copies[side].start)

    loads[5].wait()
    for slot, y, flag in ((0, 0, None), (1, 15, flag_y_top)):
        rows = pl.ds(y, 8, stride=16)
        values = convert(rows, keep=False)
        pack(slot, values[0:5] + values[9:14] + [mt[3 + n, rows] for n in range(3)], flag, flip_sub)

    for side in (2, 3):
        pl.when(greeted[side] & (iz == 0) & prompt)(copies[side].start)

    @pl.loop(2, 14)
    def _(block):
        convert(pl.ds(pl.multiple_of(block * 8, 8), 8))

    def load_y(y):
        rows = pl.ds(y, 8, stride=16)
        return [nb[n, rows] for n in range(14)] + [mt[3 + n, rows] for n in range(3)]

    loads[6].wait()

    def load_x(rows):
        return [nb[n, rows] for n in range(14)] + [mt[n, rows] for n in range(3)]

    @pl.loop(0, 4)
    def _(chunk):
        base = (chunk // 2) * 64 + (chunk % 2) * 8

        def at(a):
            return pl.ds(pl.multiple_of(base + a * 16, 8), 8)

        def store(a, total):
            for n in range(5):
                acc[n, at(a)] = total[n]

        line(lambda a: load_x(at(a)), store)

    def answered(side, here):
        @pl.when(greets[side] & here)
        def _():
            pl.semaphore_wait(ready_sem.at[side], 1)
            if side < 2:
                start_raw(side)
                weight_copies[side].start()
            else:
                copies[side].start()

    @pl.when(iz == 1)
    def _():
        pl.semaphore_wait(ready_sem.at[4], 1)

    pl.when(jnp.logical_not(prompt))(meet)
    for side in (2, 3):
        pl.when(greeted[side] & ((iz == 1) | jnp.logical_not(prompt)))(copies[side].start)
    for side in (1, 0):
        @pl.when(early[side] & jnp.logical_not(prompt))
        def _(side=side):
            start_raw(side)
            weight_copies[side].start()

    @pl.when(slow)
    def _():
        start_raw(1)
        weight_copies[1].start()

    answered(2, here == 3)
    answered(0, here == 3)

    loads[7].wait()
    for n in range(5):
        tb[n, 0:128] = jnp.transpose(nb[n])
        tb[9 + n, 0:128] = jnp.transpose(nb[9 + n])
    for n in range(3):
        tb[14 + n, 0:128] = jnp.transpose(mt[6 + n])
    raw_t = [0, 1, 2, 3, 4, 9, 10, 11, 12, 13, 14, 15, 16]
    low_z = [jnp.broadcast_to(tb[n, 0:1], (8, 128)) for n in raw_t]
    high_z = [jnp.broadcast_to(tb[n, 127:128], (8, 128)) for n in raw_t]
    pack(2, [jnp.where(low_row, x, y) for x, y in zip(low_z, high_z)], flag_z_top, flip_lane)
    copies[4].start()
    answered(3, here != 2)

    @pl.loop(0, 16)
    def _(block):
        rows = pl.ds(pl.multiple_of(block * 8, 8), 8)
        rho, beta = tb[0, rows], tb[4, rows]
        for n, value in enumerate(node_extras(rho, beta, 0.5 * rcp(rho), 0.5 * rcp(beta))):
            tb[5 + n, rows] = value

    def add(ref, rows, parts):
        for n in range(5):
            ref[n, rows] = ref[n, rows] + parts[n]

    def flipped(values, flag, flip):
        return [jnp.where(flag, flip(value), value) for value in values]

    for half in range(2):
        lower, upper = pl.ds(48 + 8 * half, 8), pl.ds(64 + 8 * half, 8)
        left = flipped(load_x(lower), flag_x_mid[half], flip_sub)
        to_l, to_u = pair(left, load_x(upper), 1.5, face=True)
        add(acc, lower, flipped(to_l, flag_x_mid[half], flip_sub))
        add(acc, upper, to_u)

    @pl.loop(0, 4)
    def _(chunk):
        def store(a, total):
            add(acc, pl.ds(chunk * 4 + a, 8, stride=16), total)

        line(lambda a: load_y(chunk * 4 + a), store)

    for ey in range(3):
        left = flipped(load_y(4 * ey + 3), flag_y_mid[ey], flip_sub)
        to_l, to_u = pair(left, load_y(4 * ey + 4), 1.5, face=True)
        add(acc, pl.ds(4 * ey + 3, 8, stride=16), flipped(to_l, flag_y_mid[ey], flip_sub))
        add(acc, pl.ds(4 * ey + 4, 8, stride=16), to_u)

    answered(3, here == 2)
    answered(2, here != 3)
    answered(1, here == 0)

    def rows_z(chunk, a):
        return pl.ds(chunk * 32 + a, 8, stride=4)

    def load_z(rows):
        return [tb[n, rows] for n in range(17)]

    @pl.loop(0, 4)
    def _(chunk):
        def store(a, total):
            for n in range(5):
                acct[n, rows_z(chunk, a)] = total[n]

        line(lambda a: load_z(rows_z(chunk, a)), store)

    answered(1, here == 1)
    for chunk in range(4):
        flag = flag_z[8 * chunk : 8 * chunk + 8] > 0.5
        lower = rows_z(chunk, 3)
        left = flipped(load_z(lower), flag, flip_lane)
        upper = rows_z(chunk, 4)
        right = load_z(upper)
        to_l, to_u = pair(left, right, 1.5, face=True)
        to_l = flipped(to_l, flag, flip_lane)
        if chunk == 3:
            inside = sub < 7
            to_l = [jnp.where(inside, x, 0.0) for x in to_l]
            to_u = [jnp.where(inside, x, 0.0) for x in to_u]
        add(acct, lower, to_l)
        add(acct, upper, to_u)

    answered(0, here == 0)

    for side in (4, 2, 3):
        on_side(side, copies[landing[side]].wait_recv)
    for n in range(13):
        recv[2, n] = pltpu.roll(recv[2, n], 1, 0)

    inflow = np.array(INFLOW_STATE)
    inflow_v = inflow[1:4] / inflow[0]
    inflow_p = 0.4 * (inflow[4] - 0.5 * np.sum(inflow[1:4] * inflow_v))
    far_values = [float(inflow[0]), *[float(x) for x in inflow_v], float(inflow[0] / (2.0 * inflow_p))]

    def mirror(v, g, turn):
        along = turn * dot3(v, g)
        return [x - along * y for x, y in zip(v, g)]

    def outer_node(slot, own, prim, normal):
        is_far, is_wall = mb[slot, 1] > 0.5, mb[slot, 2] > 0.5
        outside = is_far | is_wall
        g = own[14:17]
        image = [own[0], *mirror(own[1:4], g, 2.0 * rcp(dot3(g, g))), own[4]]
        prim = [jnp.where(is_far, f, jnp.where(is_wall, i, o)) for f, i, o in zip(far_values, image, prim)]
        normal = [jnp.where(outside, i, o) for i, o in zip(g, normal)]
        extras = node_extras(prim[0], prim[4], 0.5 * rcp(prim[0]), 0.5 * rcp(prim[4]))
        return [*prim, *extras], normal

    def side_faces(slot, own, other, w, normal):
        is_wall = mb[slot, 2] > 0.5
        outside = (mb[slot, 1] > 0.5) | is_wall
        w = [jnp.where(outside, 0.0, x) for x in w]
        mine, theirs = pair(own, [*other, *w, *normal], mb[slot, 0], face=True)
        g = own[14:17]
        back = [theirs[0], *mirror(theirs[1:4], g, 2.0 * rcp(dot3(g, g))), theirs[4]]
        return [x + jnp.where(is_wall, y, 0.0) for x, y in zip(mine, back)]

    @pl.loop(0, 3)
    def _(slot):
        own = [send[slot, n] for n in range(13)]
        other = [recv[slot, n] for n in range(13)]
        extras = node_extras(own[0], own[4], 0.5 * rcp(own[0]), 0.5 * rcp(own[4]))
        own = [*own[0:5], *extras, *own[5:13]]
        prim, normal = outer_node(slot + 4, own, other[0:5], other[10:13])
        for n, part in enumerate(side_faces(slot + 4, own, prim, other[5:10], normal)):
            gout[slot, n] = part

    add(acc, pl.ds(0, 8, stride=16), [gout[0, n] for n in range(5)])
    add(acc, pl.ds(15, 8, stride=16), flipped([gout[1, n] for n in range(5)], flag_y_top, flip_sub))
    for n in range(5):
        part = gout[2, n]
        part = jnp.where(flag_z_top, flip_lane(part), part)
        acct[n, 0:1] = acct[n, 0:1] + part[0:1]
        acct[n, 127:128] = acct[n, 127:128] + part[1:2]

    for n in range(5):
        acc[n] = acc[n] + jnp.transpose(acct[n, 0:128])

    def finish(rows, parts):
        v, beta, r = [nb[n, rows] for n in (1, 2, 3)], nb[4, rows], 2.0 * nb[7, rows]
        d_rho, d_v, d_beta = parts[0], parts[1:4], parts[4]
        db = d_beta * (beta * r)
        d_p = (-0.8 * beta) * db
        out_ref[4, rows] = d_p
        for n in range(3):
            out_ref[1 + n, rows] = d_v[n] * r - d_p * v[n]
        out_ref[0, rows] = d_rho + db - r * dot3(d_v, v) + 0.5 * d_p * dot3(v, v)

    @pl.loop(2, 14)
    def _(block):
        rows = pl.ds(pl.multiple_of(block * 8, 8), 8)
        finish(rows, [acc[n, rows] for n in range(5)])

    def x_rows_of(side, half):
        return pl.ds(pl.multiple_of(side * 112 + half * 8, 8), 8)

    def x_flags(side, half):
        return mb[2 * side + half, 3] > 0.5

    on_side(0, flag_copy.wait_recv)
    el[0:8, :] = recv_f[...].astype(f32)
    below_flags = jnp.dot(el[0:8, :], spread, preferred_element_type=f32)
    for half in range(2):
        mb[half, 3] = jnp.where(
            sub < 4,
            jnp.broadcast_to(below_flags[4 + 2 * half : 5 + 2 * half], (8, 128)),
            jnp.broadcast_to(below_flags[5 + 2 * half : 6 + 2 * half], (8, 128)),
        )

    def arrive(side, *waits):
        for n in range(2):
            @pl.when((side == n) & inner_side[n])
            def _(n=n):
                for wait in waits:
                    wait(n)

    @pl.loop(0, 2)
    def _(turn):
        side = jnp.where(here == 0, 1 - turn, turn)
        arrive(
            side,
            lambda n: raw_copies[landing[n]][-2].wait_recv(),
            lambda n: raw_copies[landing[n]][-1].wait_recv(),
        )
        for half in range(2):
            slot, rows, flag = 2 * side + half, pl.ds(8 * half, 8), x_flags(side, half)
            u = flipped([recv_u[side, n, rows] for n in range(5)], flag, flip_sub)
            normal = flipped([recv_g[side, n, rows] for n in range(3)], flag, flip_sub)
            other, normal = outer_node(slot, load_x(x_rows_of(side, half)), primitives(u), normal)
            for n, value in enumerate([*other, *normal]):
                xo[slot, n] = value

    @pl.loop(0, 2)
    def _(turn):
        side = jnp.where(here == 0, 1 - turn, turn)
        arrive(side, lambda n: weight_copies[landing[n]].wait_recv())
        for half in range(2):
            slot, rows = 2 * side + half, x_rows_of(side, half)
            w = flipped([recv_w[side, n, pl.ds(8 * half, 8)] for n in range(5)], x_flags(side, half), flip_sub)
            other, normal = [xo[slot, n] for n in range(9)], [xo[slot, 9 + n] for n in range(3)]
            parts = side_faces(slot, load_x(rows), other, w, normal)
            finish(rows, [acc[n, rows] + part for n, part in enumerate(parts)])

    for side in (4, 2, 3):
        on_side(side, copies[side].wait_send)
    for side in (1, 0):
        for copy in (*raw_copies[side], weight_copies[side]):
            on_side(side, copy.wait_send)


def solution(mesh):
    nx, ny, nz = mesh.shape["gx"], mesh.shape["gy"], mesh.shape["gz"]
    assert nz == 2

    def body(state, adjoint, metric, jacobian, boundary_kind_code, orient):
        assert state.shape == (5, 8, 16, 128)
        f32 = jnp.float32
        hbm = pl.BlockSpec(memory_space=pltpu.HBM)
        vmem = pltpu.VMEM
        out = pl.pallas_call(
            lambda *refs: kernel(nx, ny, *refs),
            out_shape=jax.ShapeDtypeStruct((5, 128, 128), f32),
            in_specs=[hbm] * 6,
            out_specs=pl.BlockSpec(memory_space=vmem),
            scratch_shapes=[
                vmem((5, 128, 128), f32),
                vmem((5, 128, 128), f32),
                vmem((9, 128, 128), f32),
                vmem((128, 128), f32),
                vmem((8, 32), jnp.int32),
                vmem((24, 32), jnp.int32),
                vmem((14, 128, 128), f32),
                vmem((17, 136, 128), f32),
                vmem((5, 128, 128), f32),
                vmem((5, 136, 128), f32),
                vmem((3, 13, 8, 128), f32),
                vmem((3, 13, 8, 128), f32),
                vmem((3, 5, 8, 128), f32),
                vmem((SLOTS, 4, 8, 128), f32),
                vmem((32, 32), f32),
                vmem((2, 5, 16, 128), f32),
                vmem((2, 5, 16, 128), f32),
                vmem((2, 3, 16, 128), f32),
                vmem((2, 5, 16, 128), f32),
                vmem((8, 32), jnp.int32),
                vmem((4, 12, 8, 128), f32),
                pltpu.SemaphoreType.DMA((8,)),
                pltpu.SemaphoreType.DMA((3,)),
                pltpu.SemaphoreType.DMA((3,)),
                pltpu.SemaphoreType.DMA((8,)),
                pltpu.SemaphoreType.DMA((8,)),
                pltpu.SemaphoreType.REGULAR((5,)),
            ],
            compiler_params=pltpu.CompilerParams(
                collective_id=0, has_side_effects=True, vmem_limit_bytes=32 * 1024 * 1024
            ),
            name="adjoint_residual",
        )(
            *(
                pltpu.with_memory_space_constraint(value, pltpu.HBM)
                for value in (
                    state.reshape(5, 128, 128),
                    adjoint.reshape(5, 128, 128),
                    metric.reshape(9, 128, 128),
                    jacobian.reshape(128, 128),
                    boundary_kind_code.reshape(8, 32),
                    orient.reshape(24, 32),
                )
            )
        )
        return out.reshape(5, 8, 16, 128)

    return jax.shard_map(
        body,
        mesh=mesh,
        in_specs=(
            P(None, "gx", "gy", "gz"),
            P(None, "gx", "gy", "gz"),
            P(None, "gx", "gy", "gz"),
            P("gx", "gy", "gz"),
            P("gx", "gy", "gz"),
            P(None, "gx", "gy", "gz"),
        ),
        out_specs=P(None, "gx", "gy", "gz"),
        check_vma=False,
    )
```
